32 devices in a mesh: space: 8 (over z, y), orb: 4 (over x, core).
Axes of the slice: x: 2, y: 2, z: 4, core: 2. Of those that a mesh axis runs over, the one named last changes fastest.
Arguments:
- orbitals: float32 [8, 8192, 256], P('orb', 'space'), may hold values from -6 to 6
- near_source: int32 [8192, 27], P('space'), may hold values from 0 to 8191, as said below
- far_leaf: int32 [8192, 108], P('space'), may hold values from 0 to 8191, as said below
- far_mid: int32 [1024, 108], P('space'), may hold values from 0 to 1023, as said below
- far_top: int32 [128, 108], P('space'), may hold values from 0 to 127, as said below
- leaf_basis: bfloat16 [64, 256], replicated, may hold values from -0.375 to 0.375
- near_table: bfloat16 [27, 256, 256], replicated, may hold values from -0.078125 to 0.078125
- transfer: bfloat16 [8, 64, 64], replicated, may hold values from -0.75 to 0.75
- coupling: bfloat16 [108, 64, 64], replicated, may hold values from -0.078125 to 0.078125
- pair_transfer: bfloat16 [2, 64, 64], replicated, may hold values from -0.75 to 0.75
- coarse_coupling: bfloat16 [4, 64, 64], replicated, may hold values from -0.4375 to 0.4375
Outputs:
- relaxed: float32 [8, 8192, 256], P('orb', 'space')
The draws below stay inside these ranges and needn't reach their ends.
Inputs may be any that keep to these rules, and one draw needn't show every extreme that they name: `near_source`: with layer(t) = t // 64: every entry of leaf t lies in a layer at most 1 from layer(t); entry 13 is t itself; entry 0 is the leaf at t's transverse position one layer away. `far_leaf`: with layer(t) = t // 64: every entry of box t lies in a layer 2 or 3 away from layer(t); entry 0 is exactly 3 layers away. `far_mid`: with layer(t) = t // 16: every entry of box t lies in a layer 2 or 3 away from layer(t); entry 0 is exactly 3 layers away. `far_top`: with layer(t) = t // 4: every entry of box t lies in a layer 2 or 3 away from layer(t); entry 0 is exactly 3 layers away.
All inputs are finite; a program needn't handle non-finite values.
Results may differ from the reference program's by a relative error of at most 0.012.
Values may be sent and summed in bfloat16 or wider, within the bound.
No kernel may reach another device: no remote copies, remote signals or barrier semaphores. Data moves between devices by JAX's collectives and lax.ppermute only.
A program may use at most 192 MiB of HBM per device.

```python
import jax
import jax.numpy as jnp
from jax import lax

PTS = 256
RANK = 64
ORB = 8
KNEAR = 27
KFAR = 108
SIDE = 8
LEAVES = 8192
MIDS = 1024
TOPS = 128


def layered_list(key, box_count, layer_size, slot_count, nearby):
    first_key, second_key, third_key = jax.random.split(key, 3)
    target = jnp.arange(box_count, dtype=jnp.int32)
    layer_of = target // layer_size
    inside = target % layer_size
    layers = box_count // layer_size
    if nearby:
        layer_step = jax.random.randint(first_key, (box_count, slot_count), -1, 2, dtype=jnp.int32)
        chosen = jnp.clip(layer_of[:, None] + layer_step, 0, layers - 1)
        forced = jnp.where(layer_of + 1 < layers, layer_of + 1, layer_of - 1)
    else:
        sign_draw = jax.random.randint(first_key, (box_count, slot_count), 0, 2, dtype=jnp.int32) * 2 - 1
        distance = jax.random.randint(third_key, (box_count, slot_count), 2, 4, dtype=jnp.int32)
        chosen = layer_of[:, None] + sign_draw * distance
        outside = (chosen < 0) | (chosen >= layers)
        chosen = jnp.where(outside, layer_of[:, None] - sign_draw * distance, chosen)
        forced = jnp.where(layer_of + 3 < layers, layer_of + 3, layer_of - 3)
    positions = jax.random.randint(second_key, (box_count, slot_count), 0, layer_size, dtype=jnp.int32)
    sources = chosen * layer_size + positions
    sources = sources.at[:, 0].set(forced * layer_size + inside)
    if nearby:
        sources = sources.at[:, 13].set(target)
    return sources.astype(jnp.int32)


def draw_near_source(key, part):
    return layered_list(jax.random.fold_in(key, 11), LEAVES, SIDE * SIDE, KNEAR, True)


def draw_far_leaf(key, part):
    return layered_list(jax.random.fold_in(key, 23), LEAVES, SIDE * SIDE, KFAR, False)


def draw_far_mid(key, part):
    return layered_list(jax.random.fold_in(key, 37), MIDS, SIDE // 2 * (SIDE // 2), KFAR, False)


def draw_far_top(key, part):
    return layered_list(jax.random.fold_in(key, 41), TOPS, SIDE // 4 * (SIDE // 4), KFAR, False)


def block_scale(stream_key, extent, shards, low, largest):
    def one(axis_at, shards_of):
        steps = jax.random.uniform(jax.random.fold_in(jax.random.fold_in(stream_key, 6), axis_at), (shards_of,), jnp.float32, low / len(shards), largest / len(shards))
        return jnp.repeat(jnp.exp(steps), extent[axis_at] // shards_of).reshape((-1,) + (1,) * (len(extent) - axis_at - 1))

    loudness = one(*shards[0])
    for cut in shards[1:]:
        loudness = loudness * one(*cut)
    return loudness


def gaussian(stream_key, shape, width, most, cuts=(), kind=jnp.bfloat16):
    factor_of = block_scale(stream_key, shape, cuts, -0.22, 0.18) if cuts else 1.0
    array = jax.random.normal(stream_key, shape, jnp.float32) * width * factor_of
    return jnp.minimum(jnp.maximum(array, -most), most).astype(kind)


def setup_inputs(seed: int = 0) -> dict:
    streams_of = jax.random.split(jax.random.key(seed), 12)
    orbitals = gaussian(streams_of[0], (ORB, LEAVES, PTS), 1.0, 6.0, ((0, 4), (1, 8)), jnp.float32)
    near_source = draw_near_source(jax.random.fold_in(streams_of[11], 71), 0)
    far_leaf = draw_far_leaf(jax.random.fold_in(streams_of[11], 71), 0)
    far_mid = draw_far_mid(jax.random.fold_in(streams_of[11], 71), 0)
    far_top = draw_far_top(jax.random.fold_in(streams_of[11], 71), 0)
    leaf_basis = gaussian(streams_of[5], (RANK, PTS), PTS ** -0.5, 0.375)
    near_table = gaussian(streams_of[6], (KNEAR, PTS, PTS), (KNEAR * PTS) ** -0.5, 0.078125)
    transfer = gaussian(streams_of[7], (8, RANK, RANK), RANK ** -0.5, 0.75)
    coupling = gaussian(streams_of[8], (KFAR, RANK, RANK), (KFAR * RANK) ** -0.5, 0.078125)
    pair_transfer = gaussian(streams_of[9], (2, RANK, RANK), RANK ** -0.5, 0.75)
    coarse_coupling = gaussian(streams_of[10], (4, RANK, RANK), (3 * RANK) ** -0.5, 0.4375)
    return dict(orbitals=orbitals, near_source=near_source, far_leaf=far_leaf, far_mid=far_mid, far_top=far_top, leaf_basis=leaf_basis, near_table=near_table, transfer=transfer, coupling=coupling, pair_transfer=pair_transfer, coarse_coupling=coarse_coupling)


relax_step = 0.1


def octant_up(moments, side_boxes, transfer):
    orbits, node_count, rank_width = moments.shape
    layers = node_count // (side_boxes * side_boxes)
    half_side = side_boxes // 2
    shaped = moments.reshape(orbits, layers // 2, 2, half_side, 2, half_side, 2, rank_width).astype(jnp.float32)
    octant_grid = transfer.reshape(2, 2, 2, rank_width, rank_width).astype(jnp.float32)
    parents = jnp.einsum("oapbqcus,pqusr->oabcr", shaped, octant_grid)
    return parents.reshape(orbits, -1, rank_width).astype(jnp.bfloat16)


def octant_down(coeffs, side_boxes, transfer):
    orbits, node_count, rank_width = coeffs.shape
    layers = node_count // (side_boxes * side_boxes)
    shaped = coeffs.reshape(orbits, layers, side_boxes, side_boxes, rank_width).astype(jnp.float32)
    octant_grid = transfer.reshape(2, 2, 2, rank_width, rank_width).astype(jnp.float32)
    children = jnp.einsum("oabcr,pqusr->oapbqcus", shaped, octant_grid)
    return children.reshape(orbits, -1, rank_width)


def couple_lists(moments, sources, coupling, scale):
    orbits, node_count, rank_width = moments.shape

    def one_slot(running, inputs):
        column, matrix = inputs
        picked = jnp.take(moments, column, axis=1).astype(jnp.float32)
        return running + jnp.einsum("ons,rs->onr", picked, matrix.astype(jnp.float32)), None

    start = jnp.zeros((orbits, sources.shape[0], rank_width), jnp.float32)
    running, _ = lax.scan(one_slot, start, (sources.T, coupling))
    return scale * running


def near_sum(density, sources, near_table):
    orbits, node_count, points = density.shape

    def one_slot(running, inputs):
        column, matrix = inputs
        picked = jnp.take(density, column, axis=1).reshape(orbits * node_count, points)
        return running + jnp.dot(picked, matrix.T, preferred_element_type=jnp.float32), None

    start = jnp.zeros((orbits * node_count, points), jnp.float32)
    running, _ = lax.scan(one_slot, start, (sources.T, near_table))
    return running.reshape(orbits, node_count, points)


def shifted(values, offset):
    node_count = values.shape[1]
    if abs(offset) >= node_count:
        return jnp.zeros_like(values)
    empty = jnp.zeros((values.shape[0], abs(offset), values.shape[2]), values.dtype)
    if offset > 0:
        return jnp.concatenate([values[:, offset:], empty], axis=1)
    return jnp.concatenate([empty, values[:, :offset]], axis=1)


def coarse_couple(moments, coarse_coupling, scale):
    values = moments.astype(jnp.float32)
    node_count = values.shape[1]
    odd_rows = (jnp.arange(node_count) % 2).astype(jnp.float32)[None, :, None]
    even_rows = 1.0 - odd_rows

    def apply_matrix(which, offset):
        return jnp.einsum("ons,rs->onr", shifted(values, offset), coarse_coupling[which].astype(jnp.float32))

    running = apply_matrix(1, -2) + apply_matrix(2, 2) + even_rows * apply_matrix(3, 3) + odd_rows * apply_matrix(0, -3)
    return scale * running


def coarse_up(moments, pair_transfer):
    orbits, node_count, rank_width = moments.shape
    if node_count % 2 == 1:
        moments = jnp.concatenate([moments, jnp.zeros((orbits, 1, rank_width), moments.dtype)], axis=1)
    shaped = moments.reshape(orbits, -1, 2, rank_width).astype(jnp.float32)
    return jnp.einsum("oaps,psr->oar", shaped, pair_transfer.astype(jnp.float32)).astype(jnp.bfloat16)


def coarse_down(coeffs, pair_transfer, node_count):
    children = jnp.einsum("oar,psr->oaps", coeffs.astype(jnp.float32), pair_transfer.astype(jnp.float32))
    return children.reshape(coeffs.shape[0], -1, coeffs.shape[2])[:, :node_count]


def coarse_tree(cube_moments, coarse_coupling, pair_transfer):
    levels = [cube_moments]
    while levels[-1].shape[1] > 1:
        levels.append(coarse_up(levels[-1], pair_transfer))
    top_level = len(levels) - 1
    coeffs = coarse_couple(levels[top_level], coarse_coupling, 0.5 ** (3 + top_level)).astype(jnp.bfloat16)
    for depth_level in range(top_level - 1, -1, -1):
        pushed = coarse_down(coeffs, pair_transfer, levels[depth_level].shape[1])
        coupled = coarse_couple(levels[depth_level], coarse_coupling, 0.5 ** (3 + depth_level))
        coeffs = (coupled + pushed).astype(jnp.bfloat16)
    return coeffs


def reference(orbitals, near_source, far_leaf, far_mid, far_top, leaf_basis, near_table, transfer, coupling, pair_transfer, coarse_coupling):
    density = (orbitals * orbitals).astype(jnp.bfloat16)
    leaf_moments = jnp.einsum("olp,rp->olr", density.astype(jnp.float32), leaf_basis.astype(jnp.float32)).astype(jnp.bfloat16)
    mid_moments = octant_up(leaf_moments, SIDE, transfer)
    top_moments = octant_up(mid_moments, SIDE // 2, transfer)
    cube_moments = octant_up(top_moments, SIDE // 4, transfer)
    cube_coeffs = coarse_tree(cube_moments, coarse_coupling, pair_transfer)
    top_coeffs = (couple_lists(top_moments, far_top, coupling, 0.25) + octant_down(cube_coeffs, SIDE // 8, transfer)).astype(jnp.bfloat16)
    mid_coeffs = (couple_lists(mid_moments, far_mid, coupling, 0.5) + octant_down(top_coeffs, SIDE // 4, transfer)).astype(jnp.bfloat16)
    leaf_coeffs = (couple_lists(leaf_moments, far_leaf, coupling, 1.0) + octant_down(mid_coeffs, SIDE // 2, transfer)).astype(jnp.bfloat16)
    near_field = near_sum(density, near_source, near_table)
    far_field = jnp.einsum("olr,rp->olp", leaf_coeffs.astype(jnp.float32), leaf_basis.astype(jnp.float32))
    potential = near_field + far_field
    hartree = jnp.sum(potential, axis=0)
    return orbitals - relax_step * (hartree[None] - potential) * orbitals
```

```python
import functools

import jax
import jax.numpy as jnp
from jax import lax
from jax.experimental import pallas as pl
from jax.experimental.pallas import tpu as pltpu
from jax.sharding import PartitionSpec as P

SIDE = 8
LAYER = SIDE * SIDE
PAIR = 2 * LAYER
BF = jnp.bfloat16
F32 = jnp.float32
relax_step = 0.1
WIDE_MEMORY = pltpu.CompilerParams(vmem_limit_bytes=60 * 1024 * 1024)


def iota(shape, axis):
    return lax.broadcasted_iota(jnp.int32, shape, axis)


def dot(left, right):
    return jnp.dot(left, right, preferred_element_type=F32)


def dot_tn(left, right):
    return lax.dot_general(left, right, (((0,), (0,)), ((), ())), preferred_element_type=F32)


def dot_nt(left, right):
    return lax.dot_general(left, right, (((1,), (1,)), ((), ())), preferred_element_type=F32)


def pick_matrix(rows, source_of_lane):
    lanes = source_of_lane.shape[1]
    hit = iota((rows, lanes), 0) == jnp.broadcast_to(source_of_lane, (rows, lanes))
    return jnp.where(hit, 1.0, 0.0).astype(BF)


def index_columns(row, rows):
    lanes = row.shape[1]
    thin = jnp.broadcast_to(row, (16, lanes)).astype(BF)
    tall = jnp.concatenate([thin] * (rows // 16), axis=0)
    steps = iota((rows, lanes), 0).astype(F32).astype(BF)
    return jnp.where(steps == tall, jnp.ones((), BF), jnp.zeros((), BF))


def turned(values):
    return jnp.transpose(values)


def up_level(children, side, transfer_ref, rank):
    half_bits = (side // 2).bit_length() - 1
    lane = iota((1, 128), 1)
    depth = lax.shift_right_logical(lane, 2 * half_bits)
    across = lax.shift_right_logical(lane, half_bits) & (side // 2 - 1)
    along = lane & (side // 2 - 1)
    base = 2 * depth * side * side + 2 * across * side + 2 * along
    orbits = children.shape[0] // rank
    totals = [None] * orbits
    for octant in range(8):
        offset = (octant // 4) * side * side + (octant // 2 % 2) * side + octant % 2
        picked = dot(children, pick_matrix(children.shape[1], base + offset)).astype(BF)
        for o in range(orbits):
            part = dot_tn(transfer_ref[octant], picked[o * rank : (o + 1) * rank])
            totals[o] = part if totals[o] is None else totals[o] + part
    return jnp.concatenate(totals, axis=0).astype(BF)


def down_level(parents, child_lanes, side, transfer_ref, rank):
    bits = side.bit_length() - 1
    lane = iota((1, child_lanes), 1)
    depth = lax.shift_right_logical(lane, 2 * bits)
    across = lax.shift_right_logical(lane, bits) & (side - 1)
    along = lane & (side - 1)
    half = side // 2
    parent = (
        lax.shift_right_logical(depth, 1) * half * half
        + lax.shift_right_logical(across, 1) * half
        + lax.shift_right_logical(along, 1)
    )
    octant_of = 4 * (depth & 1) + 2 * (across & 1) + (along & 1)
    spread = dot(parents, pick_matrix(parents.shape[1], parent))
    orbits = parents.shape[0] // rank
    totals = [None] * orbits
    for octant in range(8):
        kept = jnp.where(octant_of == octant, spread, 0.0).astype(BF)
        for o in range(orbits):
            part = dot(transfer_ref[octant], kept[o * rank : (o + 1) * rank])
            totals[o] = part if totals[o] is None else totals[o] + part
    return jnp.concatenate(totals, axis=0)


def moments_kernel(
    place_ref,
    orbitals_ref,
    basis_ref,
    transfer_ref,
    dense_ref,
    whole_ref,
    odd_ref,
    left_ref,
    right_ref,
    cube_ref,
):
    orbits, leaves, points = orbitals_ref.shape
    rank = basis_ref.shape[0]
    wide = orbits * points
    basis = basis_ref[...]
    inner = leaves - 2 * LAYER
    gap = jnp.zeros((LAYER, points), F32)
    moments = []
    moments_odd = []
    for o in range(orbits):
        value = orbitals_ref[o]
        density = value * value
        rows = slice(o * points, (o + 1) * points)
        dense_ref[rows, :] = turned(density[LAYER : leaves - LAYER]).astype(BF)
        first = jnp.concatenate([gap, density[:LAYER]], axis=0)
        last = jnp.concatenate([density[leaves - LAYER :], gap], axis=0)
        left_ref[rows, :] = turned(first).astype(BF)
        right_ref[rows, :] = turned(last).astype(BF)
        moments.append(dot_nt(basis, density.astype(BF)))
        shifted = jnp.concatenate([gap, density, gap], axis=0).astype(BF)
        moments_odd.append(dot_nt(basis, shifted))
    moments = jnp.concatenate(moments, axis=0).astype(BF)
    moments_odd = jnp.concatenate(moments_odd, axis=0).astype(BF)
    blocks = leaves // PAIR
    for b in range(blocks):
        whole_ref[b] = moments[:, b * PAIR : (b + 1) * PAIR]
    for b in range(blocks + 1):
        odd_ref[b] = moments_odd[:, b * PAIR : (b + 1) * PAIR]
    mid = up_level(moments, SIDE, transfer_ref, rank)
    top = up_level(mid, SIDE // 2, transfer_ref, rank)
    cube = up_level(top, SIDE // 4, transfer_ref, rank)
    height = orbits * rank
    for ref, pieces in (
        (left_ref, (moments[:, :PAIR], moments_odd[:, :PAIR], moments_odd[:, PAIR : 2 * PAIR])),
        (
            right_ref,
            (
                moments[:, leaves - PAIR :],
                moments_odd[:, leaves - PAIR : leaves],
                moments_odd[:, leaves:],
            ),
        ),
    ):
        for n, piece in enumerate(pieces + (mid, top)):
            ref[wide + n * height : wide + (n + 1) * height, :] = piece
    own = leaves // (LAYER * SIDE)
    lane = iota((1, 128), 1)
    from_lane = lane - place_ref[0] * own
    from_lane = jnp.where((from_lane >= 0) & (from_lane < own), from_lane, -1)
    cube_ref[...] = dot(cube, pick_matrix(128, from_lane)).astype(BF)


def widen_kernel(coupling_ref, out_ref):
    slots, rank, _ = coupling_ref.shape
    count = slots // 2
    blank = jnp.zeros((rank, rank), F32)
    for half in range(2):
        for j in range(count):
            block = coupling_ref[half * count + j].astype(F32)
            cols = slice(j * 2 * rank, (j + 1) * 2 * rank)
            row = half * 2 * rank
            out_ref[row : row + rank, cols] = jnp.concatenate([block, blank], axis=1).astype(BF)
            out_ref[row + rank : row + 2 * rank, cols] = jnp.concatenate([blank, block], axis=1).astype(BF)


def near_body(start, source_ref, table_hbm, out_ref, sum_ref, side_ref, table_ref, wide_ref, turn_ref, picked_ref, sems):
    step = pl.program_id(0)
    slots, points, _ = table_hbm.shape

    def table_copy(k):
        return pltpu.make_async_copy(
            table_hbm.at[k], table_ref.at[:, pl.ds(k * points, points)], sems.at[k]
        )

    @pl.when(step == 0)
    def _():
        for k in range(slots):
            table_copy(k).start()

    wide_ref[:, :slots] = (source_ref[...] - start).astype(F32)
    turn_ref[...] = turned(wide_ref[...])
    orbits = side_ref.shape[0] // points
    group = 3

    def gather(chunk, carry):
        columns = []
        for n in range(group):
            columns.append(index_columns(turn_ref[pl.ds(chunk * group + n, 1), :], 2 * PAIR))
        picked = dot(side_ref[...], jnp.concatenate(columns, axis=1)).astype(BF)
        for n in range(group):
            row = pl.multiple_of((chunk * group + n) * points, points)
            for o in range(orbits):
                picked_ref[pl.ds(row, points), o * PAIR : (o + 1) * PAIR] = picked[
                    o * points : (o + 1) * points, n * PAIR : (n + 1) * PAIR
                ]
        return carry

    lax.fori_loop(0, slots // group, gather, 0)

    @pl.when(step == 0)
    def _():
        for k in range(slots):
            table_copy(k).wait()

    field = dot(table_ref[...], picked_ref[...])
    out_ref[0] = field
    total = field[:, :PAIR]
    for o in range(1, orbits):
        total = total + field[:, o * PAIR : (o + 1) * PAIR]
    sum_ref[0] = total.astype(BF)


def near_inner_kernel(first, pairs, place_ref, source_ref, early_ref, late_ref, table_hbm, *rest):
    out_ref, sum_ref, side_ref = rest[-8:-5]
    pair = first + pl.program_id(0)
    side_ref[:, :PAIR] = early_ref[...]
    side_ref[:, PAIR:] = late_ref[...]
    start = (place_ref[0] * pairs + pair) * PAIR - LAYER
    near_body(start, source_ref, table_hbm, out_ref, sum_ref, side_ref, *rest[-5:])


def near_outer_kernel(
    pairs, place_ref, source_ref, first_ref, last_ref, left_ref, right_ref, got_left_ref, got_right_ref, table_hbm, *rest
):
    out_ref, sum_ref, side_ref = rest[-8:-5]
    step = pl.program_id(0)

    @pl.when(step == 0)
    def _():
        side_ref[:, :PAIR] = left_ref[...] + got_left_ref[...]
        side_ref[:, PAIR:] = first_ref[...]

    @pl.when(step == 1)
    def _():
        side_ref[:, :PAIR] = last_ref[...]
        side_ref[:, PAIR:] = right_ref[...] + got_right_ref[...]

    start = (place_ref[0] * pairs + step * (pairs - 1)) * PAIR - LAYER
    near_body(start, source_ref, table_hbm, out_ref, sum_ref, side_ref, *rest[-5:])


def near_call(kernel, steps, pair_of, leaves, orbits, table, extra, extra_specs, place, source, before, rows):
    slots, points, _ = table.shape
    pairs = leaves // PAIR
    wide = orbits * points
    shapes = (
        jax.ShapeDtypeStruct((pairs, points, orbits * PAIR), F32),
        jax.ShapeDtypeStruct((pairs, points, PAIR), BF),
    )
    in_specs = [
        pl.BlockSpec(memory_space=pltpu.SMEM),
        pl.BlockSpec((PAIR, slots), lambda i: (pair_of(i), 0)),
        *extra_specs,
        pl.BlockSpec(memory_space=pl.ANY),
    ]
    operands = [place, source, *extra, table]
    aliases = {}
    if before is not None:
        aliases = {len(operands): 0, len(operands) + 1: 1}
        operands += list(before)
        in_specs += [pl.BlockSpec(memory_space=pl.ANY)] * 2
    return pl.pallas_call(
        kernel,
        grid=(steps,),
        in_specs=in_specs,
        out_specs=(
            pl.BlockSpec((1, points, orbits * PAIR), lambda i: (pair_of(i), 0, 0)),
            pl.BlockSpec((1, points, PAIR), lambda i: (pair_of(i), 0, 0)),
        ),
        out_shape=shapes,
        scratch_shapes=[
            pltpu.VMEM((wide, 2 * PAIR), BF),
            pltpu.VMEM((points, slots * points), BF),
            pltpu.VMEM((PAIR, 128), F32),
            pltpu.VMEM((128, PAIR), F32),
            pltpu.VMEM((slots * points, orbits * PAIR), BF),
            pltpu.SemaphoreType.DMA((slots,)),
        ],
        input_output_aliases=aliases,
        compiler_params=WIDE_MEMORY,
        cost_estimate=pl.CostEstimate(
            flops=steps * 4 * slots * points * points * orbits * PAIR,
            transcendentals=0,
            bytes_accessed=2 * slots * points * points + steps * 6 * points * orbits * PAIR,
        ),
    )(*operands)


def rolled(values, shift):
    return pltpu.roll(values, shift, 1)


def coarse_part(cubes, coupling_ref, pair_ref, count, rank):
    orbits = cubes.shape[0] // rank
    sizes = [count]
    while sizes[-1] > 1:
        sizes.append(sizes[-1] // 2)
    starts = [sum(sizes[:j]) for j in range(len(sizes))]
    last = len(sizes) - 1
    lane = iota((1, 128), 1)
    level = jnp.full((1, 128), -1, jnp.int32)
    node = jnp.zeros((1, 128), jnp.int32)
    size = jnp.zeros((1, 128), jnp.int32)
    start = jnp.zeros((1, 128), jnp.int32)
    child = jnp.full((1, 128), -1, jnp.int32)
    parent = jnp.full((1, 128), -1, jnp.int32)
    scale = jnp.zeros((1, 128), F32)
    for j, (begin, n) in enumerate(zip(starts, sizes)):
        here = (lane >= begin) & (lane < begin + n)
        level = jnp.where(here, j, level)
        node = jnp.where(here, lane - begin, node)
        size = jnp.where(here, n, size)
        start = jnp.where(here, begin, start)
        scale = jnp.where(here, 0.5 ** (3 + j), scale)
        if j:
            child = jnp.where(here, starts[j - 1] + 2 * (lane - begin), child)
        if j < last:
            parent = jnp.where(here, starts[j + 1] + lax.shift_right_logical(lane - begin, 1), parent)
    odd = node & 1
    picks = [pick_matrix(128, jnp.where(child >= 0, child + p, -1)) for p in range(2)]
    current = jnp.where(level == 0, cubes.astype(F32), 0.0).astype(BF)

    def split(values, o):
        return values[o * rank : (o + 1) * rank]

    for j in range(1, last + 1):
        sides = [dot(current, picks[p]).astype(BF) for p in range(2)]
        raised = jnp.concatenate(
            [
                dot_tn(pair_ref[0], split(sides[0], o)) + dot_tn(pair_ref[1], split(sides[1], o))
                for o in range(orbits)
            ],
            axis=0,
        )
        current = jnp.where(level == j, raised, current.astype(F32)).astype(BF)
    far = [None] * orbits
    for which, offset, parity in ((1, -2, None), (2, 2, None), (3, 3, 0), (0, -3, 1)):
        there = node + offset
        good = (there >= 0) & (there < size)
        if parity is not None:
            good = good & (odd == parity)
        side = dot(current, pick_matrix(128, jnp.where(good, start + there, -1))).astype(BF)
        for o in range(orbits):
            part = dot(coupling_ref[which], split(side, o))
            far[o] = part if far[o] is None else far[o] + part
    far = scale * jnp.concatenate(far, axis=0)
    coeffs = far.astype(BF)
    widen = pick_matrix(128, parent)
    for j in range(last - 1, -1, -1):
        spread = dot(coeffs, widen)
        parts = [jnp.where(odd == p, spread, 0.0).astype(BF) for p in range(2)]
        pushed = jnp.concatenate(
            [
                dot(pair_ref[0], split(parts[0], o)) + dot(pair_ref[1], split(parts[1], o))
                for o in range(orbits)
            ],
            axis=0,
        )
        coeffs = jnp.where(level == j, far + pushed, coeffs.astype(F32)).astype(BF)
    return coeffs


def tree_kernel(
    count,
    leaves,
    rank,
    place_ref,
    own_mid_ref,
    own_top_ref,
    left_mid_ref,
    left_top_ref,
    right_mid_ref,
    right_top_ref,
    cube_ref,
    weight_ref,
    transfer_ref,
    pair_ref,
    coarse_ref,
    far_mid_ref,
    far_top_ref,
    out_ref,
    wide_ref,
    turn_ref,
    picked_ref,
):
    place = place_ref[0]
    height = own_mid_ref.shape[0]
    slots = far_mid_ref.shape[1]
    half_slots = slots // 2
    mids = far_mid_ref.shape[0]
    tops = far_top_ref.shape[0]
    mid_rim = 3 * (SIDE // 2) ** 2
    top_rim = 3 * (SIDE // 4) ** 2
    lane = iota((height, 128), 1)

    cube_coeffs = coarse_part(cube_ref[...], coarse_ref, pair_ref, count, rank)
    own = leaves // (LAYER * SIDE)
    lane_row = iota((1, 128), 1)
    cube_own = dot(
        cube_coeffs, pick_matrix(128, jnp.where(lane_row < own, lane_row + place * own, -1))
    ).astype(BF)

    left = left_mid_ref[...].astype(F32)
    middle = rolled(own_mid_ref[...].astype(F32), mid_rim)
    right = rolled(right_mid_ref[...].astype(F32), mid_rim)
    left = rolled(left, mid_rim)
    mid_ext = jnp.concatenate(
        [jnp.where(lane < mid_rim, left, middle), jnp.where(lane < mid_rim, middle, right)], axis=1
    ).astype(BF)
    left = rolled(left_top_ref[...].astype(F32), 128 + top_rim - tops)
    middle = rolled(own_top_ref[...].astype(F32), top_rim)
    right = rolled(right_top_ref[...].astype(F32), top_rim + tops)
    top_ext = jnp.where(
        lane < top_rim, left, jnp.where(lane < top_rim + tops, middle, right)
    ).astype(BF)

    wide_ref[...] = jnp.full(wide_ref.shape, -1.0, F32)
    wide_ref[0, :, :slots] = (far_mid_ref[...] - (place * mids - mid_rim)).astype(F32)
    wide_ref[1, :tops, :slots] = (far_top_ref[...] - (place * tops - top_rim)).astype(F32)
    turn_ref[0] = turned(wide_ref[0])
    turn_ref[1] = turned(wide_ref[1])
    group = 6

    def gather(chunk, carry):
        mid_columns = []
        top_columns = []
        for n in range(group):
            mid_columns.append(index_columns(turn_ref[0, pl.ds(chunk * group + n, 1), :], 256))
            top_columns.append(index_columns(turn_ref[1, pl.ds(chunk * group + n, 1), :], 128))
        mid_picked = dot(mid_ext, jnp.concatenate(mid_columns, axis=1)).astype(BF)
        top_picked = dot(top_ext, jnp.concatenate(top_columns, axis=1)).astype(BF)
        for n in range(group):
            row = pl.multiple_of((chunk * group + n) * height, height)
            picked_ref[pl.ds(row, height), :128] = mid_picked[:, n * 128 : (n + 1) * 128]
            picked_ref[pl.ds(row, height), 128:] = top_picked[:, n * 128 : (n + 1) * 128]
        return carry

    lax.fori_loop(0, slots // group, gather, 0)
    depth = half_slots * height
    far = dot(weight_ref[:height], picked_ref[:depth]) + dot(weight_ref[height:], picked_ref[depth:])
    top = (0.25 * far[:, 128:] + down_level(cube_own, 128, SIDE // 4, transfer_ref, rank)).astype(BF)
    mid = (0.5 * far[:, :128] + down_level(top, 128, SIDE // 2, transfer_ref, rank)).astype(BF)
    out_ref[...] = down_level(mid, leaves, SIDE, transfer_ref, rank)


def leaf_kernel(
    pairs,
    place_ref,
    source_ref,
    whole_ref,
    odd_ref,
    left_ref,
    right_ref,
    weight_ref,
    down_ref,
    coeffs_ref,
    sum_ref,
    even_ref,
    shift_ref,
    wide_ref,
    turn_ref,
    rows_ref,
    picked_ref,
):
    step = pl.program_id(0)
    height = whole_ref.shape[1]
    slots = source_ref.shape[1]
    half_slots = slots // 2

    @pl.when(step == 0)
    def _():
        even_ref[0] = left_ref[:height]
        shift_ref[0] = left_ref[height : 2 * height]
        for b in range(pairs):
            even_ref[b + 1] = whole_ref[b]
        for b in range(1, pairs):
            shift_ref[b + 1] = odd_ref[b]
        shift_ref[1] = odd_ref[0] + left_ref[2 * height :]
        shift_ref[pairs + 1] = odd_ref[pairs] + right_ref[height : 2 * height]
        even_ref[pairs + 1] = right_ref[:height]
        shift_ref[pairs + 2] = right_ref[2 * height :]

    source = source_ref[...]
    layer_bits = LAYER.bit_length() - 1
    target_layer = (place_ref[0] * pairs + step) * 2 + lax.shift_right_logical(iota(source.shape, 0), layer_bits)
    away = lax.shift_right_logical(source, layer_bits) - target_layer
    away = jnp.where(away < 0, away + 3, away)
    wide_ref[:, :slots] = (away * LAYER + (source & (LAYER - 1))).astype(F32)
    turn_ref[...] = turned(wide_ref[...])
    early = turn_ref[:half_slots, :]
    late = turn_ref[half_slots:slots, :]
    low = iota((half_slots, PAIR), 1) < LAYER
    rows_ref[0, :half_slots, :] = jnp.where(low, early, rolled(late, LAYER))
    rows_ref[1, :half_slots, :] = jnp.where(low, rolled(early, LAYER), late)
    group = 6

    def gather(chunk, carry):
        for z in range(2):
            if z == 0:
                before, after = shift_ref[step], even_ref[step + 2]
            else:
                before, after = even_ref[step], shift_ref[step + 3]
            side = jnp.concatenate([before, after], axis=1)
            columns = []
            for n in range(group):
                columns.append(index_columns(rows_ref[z, pl.ds(chunk * group + n, 1), :], 256))
            picked = dot(side, jnp.concatenate(columns, axis=1)).astype(BF)
            for n in range(group):
                row = pl.multiple_of((chunk * group + n) * height, height)
                picked_ref[pl.ds(row, height), z * PAIR : (z + 1) * PAIR] = picked[
                    :, n * PAIR : (n + 1) * PAIR
                ]
        return carry

    lax.fori_loop(0, half_slots // group, gather, 0)
    both = dot(weight_ref[...], picked_ref[...])
    low = iota((height, PAIR), 1) < LAYER
    first = both[:height, :PAIR] + rolled(both[height:, :PAIR], LAYER)
    second = rolled(both[:height, PAIR:], LAYER) + both[height:, PAIR:]
    coeffs = (jnp.where(low, first, second) + down_ref[...]).astype(BF)
    coeffs_ref[...] = coeffs
    rank = sum_ref.shape[0]
    total = coeffs[:rank].astype(F32)
    for o in range(1, height // rank):
        total = total + coeffs[o * rank : (o + 1) * rank].astype(F32)
    sum_ref[...] = total.astype(BF)


def final_kernel(
    orbitals_ref, near_ref, sum_ref, other_sum_ref, coeffs_ref, total_ref, other_total_ref, basis_ref, out_ref
):
    orbits = orbitals_ref.shape[0]
    rank = basis_ref.shape[0]
    hartree = sum_ref[0].astype(F32) + other_sum_ref[0].astype(F32)
    total = total_ref[...].astype(F32) + other_total_ref[...].astype(F32)
    for o in range(orbits):
        rest = (total - coeffs_ref[o * rank : (o + 1) * rank].astype(F32)).astype(BF)
        gap = hartree - near_ref[0, :, o * PAIR : (o + 1) * PAIR] + dot_tn(basis_ref[...], rest)
        value = orbitals_ref[o]
        out_ref[o] = value - relax_step * turned(gap) * value


def swap(values, axis, bit):
    count = lax.axis_size(axis)
    return lax.ppermute(values, axis, [(i, i ^ bit) for i in range(count)])


def shards(
    orbitals,
    near_source,
    far_leaf,
    far_mid,
    far_top,
    leaf_basis,
    near_table,
    transfer,
    coupling,
    pair_transfer,
    coarse_coupling,
):
    orbits, leaves, points = orbitals.shape
    rank = leaf_basis.shape[0]
    devices = lax.axis_size("space")
    groups = lax.axis_size("orb")
    height = orbits * rank
    wide = orbits * points
    pairs = leaves // PAIR
    slots = far_leaf.shape[1]
    count = devices * (leaves // (LAYER * SIDE))
    assert height == 128 and leaves == 1024 and 2 * count - 1 <= 128
    assert devices & (devices - 1) == 0 and groups == 4
    place = lax.axis_index("space").astype(jnp.int32).reshape(1)
    message = wide + 5 * height
    smem = pl.BlockSpec(memory_space=pltpu.SMEM)

    dense, whole, odd, to_left, to_right, cubes = pl.pallas_call(
        moments_kernel,
        in_specs=[smem] + [pl.BlockSpec()] * 3,
        out_shape=(
            jax.ShapeDtypeStruct((wide, leaves - PAIR), BF),
            jax.ShapeDtypeStruct((pairs, height, PAIR), BF),
            jax.ShapeDtypeStruct((pairs + 1, height, PAIR), BF),
            jax.ShapeDtypeStruct((message, PAIR), BF),
            jax.ShapeDtypeStruct((message, PAIR), BF),
            jax.ShapeDtypeStruct((height, 128), BF),
        ),
        compiler_params=WIDE_MEMORY,
        name="moments",
    )(place, orbitals, leaf_basis, transfer)

    from_left = lax.ppermute(to_right, "space", [(i, i + 1) for i in range(devices - 1)])
    from_right = lax.ppermute(to_left, "space", [(i + 1, i) for i in range(devices - 1)])
    bit = 1
    while bit < devices:
        cubes = cubes + swap(cubes, "space", bit)
        bit *= 2

    weight = pl.pallas_call(
        widen_kernel,
        out_shape=jax.ShapeDtypeStruct((2 * height, slots // 2 * height), BF),
        compiler_params=WIDE_MEMORY,
        name="widen",
    )(coupling)

    block = lambda which: pl.BlockSpec((wide, PAIR), which)
    inner = pairs - 2
    near = near_call(
        functools.partial(near_inner_kernel, 1, pairs),
        inner,
        lambda i: i + 1,
        leaves,
        orbits,
        near_table,
        (dense, dense),
        (block(lambda i: (0, i)), block(lambda i: (0, i + 1))),
        place,
        near_source,
        None,
        None,
    )
    near, near_sum = near_call(
        functools.partial(near_outer_kernel, pairs),
        2,
        lambda i: i * (pairs - 1),
        leaves,
        orbits,
        near_table,
        (dense, dense, to_left, to_right, from_left, from_right),
        (
            block(lambda i: (0, 0)),
            block(lambda i: (0, inner)),
            block(lambda i: (0, 0)),
            block(lambda i: (0, 0)),
            block(lambda i: (0, 0)),
            block(lambda i: (0, 0)),
        ),
        place,
        near_source,
        near,
        None,
    )
    near_chip = near_sum + swap(near_sum, "orb", 1)

    box = lambda n: pl.BlockSpec((height, 128), lambda i: (n, 0))
    base = wide // height
    full = lambda shape: pl.BlockSpec(shape, lambda i: (0,) * len(shape))
    down = pl.pallas_call(
        functools.partial(tree_kernel, count, leaves, rank),
        grid=(1,),
        in_specs=[
            smem,
            box(base + 3),
            box(base + 4),
            box(base + 3),
            box(base + 4),
            box(base + 3),
            box(base + 4),
            full((height, 128)),
            full(weight.shape),
            full(transfer.shape),
            full(pair_transfer.shape),
            full(coarse_coupling.shape),
            full(far_mid.shape),
            full(far_top.shape),
        ],
        out_specs=full((height, leaves)),
        out_shape=jax.ShapeDtypeStruct((height, leaves), F32),
        scratch_shapes=[
            pltpu.VMEM((2, 128, 128), F32),
            pltpu.VMEM((2, 128, 128), F32),
            pltpu.VMEM((slots * height, 256), BF),
        ],
        compiler_params=WIDE_MEMORY,
        name="tree",
    )(
        place,
        to_left,
        to_left,
        from_left,
        from_left,
        from_right,
        from_right,
        cubes,
        weight,
        transfer,
        pair_transfer,
        coarse_coupling,
        far_mid,
        far_top,
    )
    near_other = swap(near_chip, "orb", 2)

    edge = lambda: pl.BlockSpec((3 * height, PAIR), lambda i: (0, 0))
    coeffs, coeff_sum = pl.pallas_call(
        functools.partial(leaf_kernel, pairs),
        grid=(pairs,),
        in_specs=[
            smem,
            pl.BlockSpec((PAIR, slots), lambda i: (i, 0)),
            full(whole.shape),
            full(odd.shape),
            edge(),
            edge(),
            full(weight.shape),
            pl.BlockSpec((height, PAIR), lambda i: (0, i)),
        ],
        out_specs=(
            pl.BlockSpec((height, PAIR), lambda i: (0, i)),
            pl.BlockSpec((rank, PAIR), lambda i: (0, i)),
        ),
        out_shape=(
            jax.ShapeDtypeStruct((height, leaves), BF),
            jax.ShapeDtypeStruct((rank, leaves), BF),
        ),
        scratch_shapes=[
            pltpu.VMEM((pairs + 2, height, PAIR), BF),
            pltpu.VMEM((pairs + 3, height, PAIR), BF),
            pltpu.VMEM((PAIR, 128), F32),
            pltpu.VMEM((128, PAIR), F32),
            pltpu.VMEM((2, slots // 2 + 2, PAIR), F32),
            pltpu.VMEM((slots // 2 * height, 2 * PAIR), BF),
        ],
        compiler_params=WIDE_MEMORY,
        name="leaf",
    )(
        place,
        far_leaf,
        whole,
        odd,
        from_left[wide : wide + 3 * height],
        from_right[wide : wide + 3 * height],
        weight,
        down,
    )
    coeff_chip = coeff_sum + swap(coeff_sum, "orb", 1)
    coeff_other = swap(coeff_chip, "orb", 2)

    per_pair = pl.BlockSpec((1, points, PAIR), lambda i: (i, 0, 0))
    per_rank = pl.BlockSpec((rank, PAIR), lambda i: (0, i))
    per_leaf = pl.BlockSpec((orbits, PAIR, points), lambda i: (0, i, 0))
    return pl.pallas_call(
        final_kernel,
        grid=(pairs,),
        in_specs=[
            per_leaf,
            pl.BlockSpec((1, points, orbits * PAIR), lambda i: (i, 0, 0)),
            per_pair,
            per_pair,
            pl.BlockSpec((height, PAIR), lambda i: (0, i)),
            per_rank,
            per_rank,
            full(leaf_basis.shape),
        ],
        out_specs=per_leaf,
        out_shape=jax.ShapeDtypeStruct(orbitals.shape, F32),
        compiler_params=WIDE_MEMORY,
        name="final",
    )(orbitals, near, near_chip, near_other, coeffs, coeff_chip, coeff_other, leaf_basis)


def solution(mesh):
    placed = (
        P("orb", "space", None),
        P("space", None),
        P("space", None),
        P("space", None),
        P("space", None),
        P(),
        P(),
        P(),
        P(),
        P(),
        P(),
    )
    return jax.shard_map(
        shards, mesh=mesh, in_specs=placed, out_specs=P("orb", "space", None), check_vma=False
    )
```

```python
import functools

import jax
import jax.numpy as jnp
from jax import lax
from jax.experimental import pallas as pl
from jax.experimental.pallas import tpu as pltpu
from jax.sharding import PartitionSpec as P


SIDE = 8
LAYER = SIDE * SIDE
PAIR = 2 * LAYER
BF = jnp.bfloat16
F32 = jnp.float32
relax_step = 0.1
WIDE_MEMORY = pltpu.CompilerParams(vmem_limit_bytes=60 * 1024 * 1024)


def iota(shape, axis):
    return lax.broadcasted_iota(jnp.int32, shape, axis)


def dot(left, right):
    return jnp.dot(left, right, preferred_element_type=F32)


def dot_tn(left, right):
    return lax.dot_general(left, right, (((0,), (0,)), ((), ())), preferred_element_type=F32)


def dot_nt(left, right):
    return lax.dot_general(left, right, (((1,), (1,)), ((), ())), preferred_element_type=F32)


def pick_matrix(rows, source_of_lane):
    lanes = source_of_lane.shape[1]
    hit = iota((rows, lanes), 0) == jnp.broadcast_to(source_of_lane, (rows, lanes))
    return jnp.where(hit, 1.0, 0.0).astype(BF)


def index_columns(row, rows):
    lanes = row.shape[1]
    thin = jnp.broadcast_to(row, (16, lanes)).astype(BF)
    tall = jnp.concatenate([thin] * (rows // 16), axis=0)
    steps = iota((rows, lanes), 0).astype(F32).astype(BF)
    return jnp.where(steps == tall, jnp.ones((), BF), jnp.zeros((), BF))


def turned(values):
    return jnp.transpose(values)


def up_level(children, side, transfer, rank):
    half_bits = (side // 2).bit_length() - 1
    lane = iota((1, 128), 1)
    depth = lax.shift_right_logical(lane, 2 * half_bits)
    across = lax.shift_right_logical(lane, half_bits) & (side // 2 - 1)
    along = lane & (side // 2 - 1)
    base = 2 * depth * side * side + 2 * across * side + 2 * along
    orbits = children.shape[0] // rank
    pieces = []
    for octant in range(8):
        offset = (octant // 4) * side * side + (octant // 2 % 2) * side + octant % 2
        pieces.append(dot(children, pick_matrix(children.shape[1], base + offset)).astype(BF))
    totals = []
    for o in range(orbits):
        stacked = jnp.concatenate([piece[o * rank : (o + 1) * rank] for piece in pieces], axis=0)
        totals.append(dot_tn(transfer, stacked))
    return jnp.concatenate(totals, axis=0).astype(BF)


def down_level(parents, child_lanes, side, transfer, rank):
    bits = side.bit_length() - 1
    lane = iota((1, child_lanes), 1)
    depth = lax.shift_right_logical(lane, 2 * bits)
    across = lax.shift_right_logical(lane, bits) & (side - 1)
    along = lane & (side - 1)
    half = side // 2
    parent = (
        lax.shift_right_logical(depth, 1) * half * half
        + lax.shift_right_logical(across, 1) * half
        + lax.shift_right_logical(along, 1)
    )
    octant_of = 4 * (depth & 1) + 2 * (across & 1) + (along & 1)
    spread = dot(parents, pick_matrix(parents.shape[1], parent)).astype(BF)
    thin = jnp.broadcast_to(octant_of.astype(F32), (16, child_lanes)).astype(BF)
    tall = jnp.concatenate([thin] * (rank // 16), axis=0)
    totals = []
    for o in range(parents.shape[0] // rank):
        own = spread[o * rank : (o + 1) * rank]
        kept = [jnp.where(tall == jnp.full((), octant, BF), own, jnp.zeros((), BF)) for octant in range(8)]
        totals.append(dot(transfer, jnp.concatenate(kept, axis=0)))
    return jnp.concatenate(totals, axis=0)


def moments_kernel(
    place_ref,
    orbitals_ref,
    basis_ref,
    transfer_ref,
    dense_ref,
    whole_ref,
    odd_ref,
    left_ref,
    right_ref,
):
    orbits, leaves, points = orbitals_ref.shape
    rank = basis_ref.shape[0]
    wide = orbits * points
    basis = basis_ref[...]
    gap = jnp.zeros((LAYER, points), F32)
    moments = []
    moments_odd = []
    for o in range(orbits):
        value = orbitals_ref[o]
        density = value * value
        rows = slice(o * points, (o + 1) * points)
        dense_ref[rows, :] = turned(density[LAYER : leaves - LAYER]).astype(BF)
        first = jnp.concatenate([gap, density[:LAYER]], axis=0)
        last = jnp.concatenate([density[leaves - LAYER :], gap], axis=0)
        left_ref[rows, :] = turned(first).astype(BF)
        right_ref[rows, :] = turned(last).astype(BF)
        moments.append(dot_nt(basis, density.astype(BF)))
        shifted = jnp.concatenate([gap, density, gap], axis=0).astype(BF)
        moments_odd.append(dot_nt(basis, shifted))
    moments = jnp.concatenate(moments, axis=0).astype(BF)
    moments_odd = jnp.concatenate(moments_odd, axis=0).astype(BF)
    blocks = leaves // PAIR
    for b in range(blocks):
        whole_ref[b] = moments[:, b * PAIR : (b + 1) * PAIR]
    for b in range(blocks + 1):
        odd_ref[b] = moments_odd[:, b * PAIR : (b + 1) * PAIR]
    transfer = transfer_ref[...]
    mid = up_level(moments, SIDE, transfer, rank)
    top = up_level(mid, SIDE // 2, transfer, rank)
    cube = up_level(top, SIDE // 4, transfer, rank)
    own = leaves // (LAYER * SIDE)
    lane = iota((1, 128), 1)
    from_lane = lane - place_ref[0] * own
    from_lane = jnp.where((from_lane >= 0) & (from_lane < own), from_lane, -1)
    cube = dot(cube, pick_matrix(128, from_lane)).astype(BF)
    height = orbits * rank
    for ref, pieces in (
        (left_ref, (moments[:, :PAIR], moments_odd[:, :PAIR], moments_odd[:, PAIR : 2 * PAIR])),
        (
            right_ref,
            (
                moments[:, leaves - PAIR :],
                moments_odd[:, leaves - PAIR : leaves],
                moments_odd[:, leaves:],
            ),
        ),
    ):
        for n, piece in enumerate(pieces + (mid, top, cube)):
            ref[wide + n * height : wide + (n + 1) * height, :] = piece


def widen_kernel(coupling_ref, out_ref):
    slots, rank, _ = coupling_ref.shape
    count = slots // 2
    blank = jnp.zeros((rank, rank), F32)
    for half in range(2):
        for j in range(count):
            block = coupling_ref[half * count + j].astype(F32)
            cols = slice(j * 2 * rank, (j + 1) * 2 * rank)
            row = half * 2 * rank
            out_ref[row : row + rank, cols] = jnp.concatenate([block, blank], axis=1).astype(BF)
            out_ref[row + rank : row + 2 * rank, cols] = jnp.concatenate([blank, block], axis=1).astype(BF)


def near_body(start, source_ref, table_hbm, out_ref, sum_ref, side_ref, table_ref, turn_ref, picked_ref, sems):
    step = pl.program_id(0)
    slots, points, _ = table_hbm.shape

    def table_copy(k):
        return pltpu.make_async_copy(
            table_hbm.at[k], table_ref.at[:, pl.ds(k * points, points)], sems.at[k]
        )

    @pl.when(step == 0)
    def _():
        for k in range(slots):
            table_copy(k).start()

    turn_ref[:slots, :] = (source_ref[...] - start).astype(F32)
    orbits = side_ref.shape[0] // points
    group = 2
    for begin in range(0, slots, group):
        chunk = range(begin, min(begin + group, slots))
        columns = [index_columns(turn_ref[k : k + 1, :], 2 * PAIR) for k in chunk]
        columns = jnp.concatenate(columns, axis=1)
        for o in range(orbits):
            picked = dot(side_ref[o * points : (o + 1) * points], columns).astype(BF)
            for n, k in enumerate(chunk):
                picked_ref[k * points : (k + 1) * points, o * PAIR : (o + 1) * PAIR] = picked[
                    :, n * PAIR : (n + 1) * PAIR
                ]

    @pl.when(step == 0)
    def _():
        for k in range(slots):
            table_copy(k).wait()

    for rows in (slice(0, points // 2), slice(points // 2, points)):
        field = dot(table_ref[rows, :], picked_ref[...])
        out_ref[0, rows, :] = field
        total = field[:, :PAIR]
        for o in range(1, orbits):
            total = total + field[:, o * PAIR : (o + 1) * PAIR]
        sum_ref[0, rows, :] = total.astype(BF)


def near_inner_kernel(first, pairs, place_ref, source_ref, early_ref, late_ref, table_hbm, *rest):
    out_ref, sum_ref, side_ref = rest[-7:-4]
    pair = first + pl.program_id(0)
    side_ref[:, :PAIR] = early_ref[...]
    side_ref[:, PAIR:] = late_ref[...]
    start = (place_ref[0] * pairs + pair) * PAIR - LAYER
    near_body(start, source_ref, table_hbm, out_ref, sum_ref, side_ref, *rest[-4:])


def near_outer_kernel(
    pairs, place_ref, source_ref, first_ref, last_ref, left_ref, right_ref, got_left_ref, got_right_ref, table_hbm, *rest
):
    out_ref, sum_ref, side_ref = rest[-7:-4]
    step = pl.program_id(0)

    @pl.when(step == 0)
    def _():
        side_ref[:, :PAIR] = left_ref[...] + got_left_ref[...]
        side_ref[:, PAIR:] = first_ref[...]

    @pl.when(step == 1)
    def _():
        side_ref[:, :PAIR] = last_ref[...]
        side_ref[:, PAIR:] = right_ref[...] + got_right_ref[...]

    start = (place_ref[0] * pairs + step * (pairs - 1)) * PAIR - LAYER
    near_body(start, source_ref, table_hbm, out_ref, sum_ref, side_ref, *rest[-4:])


def near_call(kernel, steps, pair_of, leaves, orbits, table, extra, extra_specs, place, source, before):
    slots, points, _ = table.shape
    pairs = leaves // PAIR
    wide = orbits * points
    shapes = (
        jax.ShapeDtypeStruct((pairs, points, orbits * PAIR), F32),
        jax.ShapeDtypeStruct((pairs, points, PAIR), BF),
    )
    in_specs = [
        pl.BlockSpec(memory_space=pltpu.SMEM),
        pl.BlockSpec((slots, PAIR), lambda i: (0, pair_of(i))),
        *extra_specs,
        pl.BlockSpec(memory_space=pl.ANY),
    ]
    operands = [place, source, *extra, table]
    aliases = {}
    if before is not None:
        aliases = {len(operands): 0, len(operands) + 1: 1}
        operands += list(before)
        in_specs += [pl.BlockSpec(memory_space=pl.ANY)] * 2
    return pl.pallas_call(
        kernel,
        grid=(steps,),
        in_specs=in_specs,
        out_specs=(
            pl.BlockSpec((1, points, orbits * PAIR), lambda i: (pair_of(i), 0, 0)),
            pl.BlockSpec((1, points, PAIR), lambda i: (pair_of(i), 0, 0)),
        ),
        out_shape=shapes,
        scratch_shapes=[
            pltpu.VMEM((wide, 2 * PAIR), BF),
            pltpu.VMEM((points, slots * points), BF),
            pltpu.VMEM((32, PAIR), F32),
            pltpu.VMEM((slots * points, orbits * PAIR), BF),
            pltpu.SemaphoreType.DMA((slots,)),
        ],
        input_output_aliases=aliases,
        compiler_params=WIDE_MEMORY,
        cost_estimate=pl.CostEstimate(
            flops=steps * 4 * slots * points * points * orbits * PAIR,
            transcendentals=0,
            bytes_accessed=2 * slots * points * points + steps * 6 * points * orbits * PAIR,
        ),
    )(*operands)


def rolled(values, shift):
    return pltpu.roll(values, shift, 1)


def coarse_part(cubes, coupling_ref, pair_ref, count, rank):
    orbits = cubes.shape[0] // rank
    sizes = [count]
    while sizes[-1] > 1:
        sizes.append(sizes[-1] // 2)
    starts = [sum(sizes[:j]) for j in range(len(sizes))]
    last = len(sizes) - 1
    lane = iota((1, 128), 1)
    level = jnp.full((1, 128), -1, jnp.int32)
    node = jnp.zeros((1, 128), jnp.int32)
    size = jnp.zeros((1, 128), jnp.int32)
    start = jnp.zeros((1, 128), jnp.int32)
    child = jnp.full((1, 128), -1, jnp.int32)
    parent = jnp.full((1, 128), -1, jnp.int32)
    scale = jnp.zeros((1, 128), F32)
    for j, (begin, n) in enumerate(zip(starts, sizes)):
        here = (lane >= begin) & (lane < begin + n)
        level = jnp.where(here, j, level)
        node = jnp.where(here, lane - begin, node)
        size = jnp.where(here, n, size)
        start = jnp.where(here, begin, start)
        scale = jnp.where(here, 0.5 ** (3 + j), scale)
        if j:
            child = jnp.where(here, starts[j - 1] + 2 * (lane - begin), child)
        if j < last:
            parent = jnp.where(here, starts[j + 1] + lax.shift_right_logical(lane - begin, 1), parent)
    odd = node & 1
    picks = [pick_matrix(128, jnp.where(child >= 0, child + p, -1)) for p in range(2)]
    current = jnp.where(level == 0, cubes.astype(F32), 0.0).astype(BF)

    def split(values, o):
        return values[o * rank : (o + 1) * rank]

    for j in range(1, last + 1):
        sides = [dot(current, picks[p]).astype(BF) for p in range(2)]
        raised = jnp.concatenate(
            [
                dot_tn(pair_ref[0], split(sides[0], o)) + dot_tn(pair_ref[1], split(sides[1], o))
                for o in range(orbits)
            ],
            axis=0,
        )
        current = jnp.where(level == j, raised, current.astype(F32)).astype(BF)
    far = [None] * orbits
    for which, offset, parity in ((1, -2, None), (2, 2, None), (3, 3, 0), (0, -3, 1)):
        there = node + offset
        good = (there >= 0) & (there < size)
        if parity is not None:
            good = good & (odd == parity)
        side = dot(current, pick_matrix(128, jnp.where(good, start + there, -1))).astype(BF)
        for o in range(orbits):
            part = dot(coupling_ref[which], split(side, o))
            far[o] = part if far[o] is None else far[o] + part
    far = scale * jnp.concatenate(far, axis=0)
    coeffs = far.astype(BF)
    widen = pick_matrix(128, parent)
    for j in range(last - 1, -1, -1):
        spread = dot(coeffs, widen)
        parts = [jnp.where(odd == p, spread, 0.0).astype(BF) for p in range(2)]
        pushed = jnp.concatenate(
            [
                dot(pair_ref[0], split(parts[0], o)) + dot(pair_ref[1], split(parts[1], o))
                for o in range(orbits)
            ],
            axis=0,
        )
        coeffs = jnp.where(level == j, far + pushed, coeffs.astype(F32)).astype(BF)
    return coeffs


def tree_kernel(
    count,
    leaves,
    rank,
    place_ref,
    own_mid_ref,
    own_top_ref,
    left_mid_ref,
    left_top_ref,
    right_mid_ref,
    right_top_ref,
    cube_ref,
    other_cube_ref,
    weight_ref,
    transfer_ref,
    pair_ref,
    coarse_ref,
    far_mid_ref,
    far_top_ref,
    out_ref,
    wide_ref,
    turn_ref,
    picked_ref,
):
    place = place_ref[0]
    height = own_mid_ref.shape[0]
    slots = far_mid_ref.shape[0]
    half_slots = slots // 2
    mids = far_mid_ref.shape[1]
    tops = far_top_ref.shape[0]
    mid_rim = 3 * (SIDE // 2) ** 2
    top_rim = 3 * (SIDE // 4) ** 2
    lane = iota((height, 128), 1)

    transfer = jnp.concatenate([transfer_ref[n].astype(F32) for n in range(8)], axis=1).astype(BF)
    cube_coeffs = coarse_part(cube_ref[...] + other_cube_ref[...], coarse_ref, pair_ref, count, rank)
    own = leaves // (LAYER * SIDE)
    lane_row = iota((1, 128), 1)
    cube_own = dot(
        cube_coeffs, pick_matrix(128, jnp.where(lane_row < own, lane_row + place * own, -1))
    ).astype(BF)

    left = left_mid_ref[...].astype(F32)
    middle = rolled(own_mid_ref[...].astype(F32), mid_rim)
    right = rolled(right_mid_ref[...].astype(F32), mid_rim)
    left = rolled(left, mid_rim)
    mid_ext = jnp.concatenate(
        [jnp.where(lane < mid_rim, left, middle), jnp.where(lane < mid_rim, middle, right)], axis=1
    ).astype(BF)
    left = rolled(left_top_ref[...].astype(F32), 128 + top_rim - tops)
    middle = rolled(own_top_ref[...].astype(F32), top_rim)
    right = rolled(right_top_ref[...].astype(F32), top_rim + tops)
    top_ext = jnp.where(
        lane < top_rim, left, jnp.where(lane < top_rim + tops, middle, right)
    ).astype(BF)

    wide_ref[...] = jnp.full(wide_ref.shape, -1.0, F32)
    wide_ref[:tops, :slots] = (far_top_ref[...] - (place * tops - top_rim)).astype(F32)
    turn_ref[0, :slots, :] = (far_mid_ref[...] - (place * mids - mid_rim)).astype(F32)
    packed = 128 // tops
    lanes = iota((1, 128), 1)
    tall = dot_tn(wide_ref[:tops, :].astype(BF), pick_matrix(tops, lanes & (tops - 1)))
    mine = iota((128, 128), 0) & (packed - 1)
    tall = jnp.where(mine == iota((128, 128), 1) // tops, tall, 0.0).astype(BF)
    rows = 128 // packed
    of_group = jnp.where(iota((rows, 128), 0) == iota((rows, 128), 1) // packed, 1.0, 0.0).astype(BF)
    turn_ref[1, :rows, :] = dot(of_group, tall)
    group = 2
    for begin in range(0, slots, packed * group):
        first = begin // packed
        here = range(min(group, pl.cdiv(slots - begin, packed)))
        top_columns = [index_columns(turn_ref[1, first + n : first + n + 1, :], 128) for n in here]
        top_picked = dot(top_ext, jnp.concatenate(top_columns, axis=1))
        for k in range(begin, min(slots, begin + packed * group)):
            block = top_picked[:, (k - begin) // packed * 128 :][:, :128]
            shift = (k % packed) * tops
            block = rolled(block, 128 - shift) if shift else block
            picked_ref[k * height : (k + 1) * height, 128:] = block.astype(BF)
    for begin in range(0, slots, group):
        mid_columns = [index_columns(turn_ref[0, begin + n : begin + n + 1, :], 256) for n in range(group)]
        mid_picked = dot(mid_ext, jnp.concatenate(mid_columns, axis=1)).astype(BF)
        for n in range(group):
            row = (begin + n) * height
            picked_ref[row : row + height, :128] = mid_picked[:, n * 128 : (n + 1) * 128]

    depth = half_slots * height
    far = dot(weight_ref[:height], picked_ref[:depth]) + dot(weight_ref[height:], picked_ref[depth:])
    top = (0.25 * far[:, 128:] + down_level(cube_own, 128, SIDE // 4, transfer, rank)).astype(BF)
    mid = (0.5 * far[:, :128] + down_level(top, 128, SIDE // 2, transfer, rank)).astype(BF)
    out_ref[...] = down_level(mid, leaves, SIDE, transfer, rank)


def leaf_kernel(
    pairs,
    place_ref,
    source_ref,
    whole_ref,
    odd_ref,
    left_ref,
    right_ref,
    weight_ref,
    down_ref,
    coeffs_ref,
    sum_ref,
    even_ref,
    shift_ref,
    turn_ref,
    rows_ref,
    picked_ref,
):
    step = pl.program_id(0)
    height = whole_ref.shape[1]
    slots = source_ref.shape[0]
    half_slots = slots // 2

    @pl.when(step == 0)
    def _():
        def piece(ref, n):
            first = ref.shape[0] - (6 - n) * height
            return ref[first : first + height]

        even_ref[0] = piece(left_ref, 0)
        shift_ref[0] = piece(left_ref, 1)
        for b in range(pairs):
            even_ref[b + 1] = whole_ref[b]
        for b in range(1, pairs):
            shift_ref[b + 1] = odd_ref[b]
        shift_ref[1] = odd_ref[0] + piece(left_ref, 2)
        shift_ref[pairs + 1] = odd_ref[pairs] + piece(right_ref, 1)
        even_ref[pairs + 1] = piece(right_ref, 0)
        shift_ref[pairs + 2] = piece(right_ref, 2)

    source = source_ref[...]
    layer_bits = LAYER.bit_length() - 1
    target_layer = (place_ref[0] * pairs + step) * 2 + lax.shift_right_logical(iota(source.shape, 1), layer_bits)
    away = lax.shift_right_logical(source, layer_bits) - target_layer
    away = jnp.where(away < 0, away + 3, away)
    turn_ref[:slots, :] = (away * LAYER + (source & (LAYER - 1))).astype(F32)
    early = turn_ref[:half_slots, :]
    late = turn_ref[half_slots:slots, :]
    low = iota((half_slots, PAIR), 1) < LAYER
    rows_ref[0, :half_slots, :] = jnp.where(low, early, rolled(late, LAYER))
    rows_ref[1, :half_slots, :] = jnp.where(low, rolled(early, LAYER), late)
    group = 2
    sides = (
        jnp.concatenate([shift_ref[step], even_ref[step + 2]], axis=1),
        jnp.concatenate([even_ref[step], shift_ref[step + 3]], axis=1),
    )
    for begin in range(0, half_slots, group):
        for z in range(2):
            columns = [index_columns(rows_ref[z, begin + n : begin + n + 1, :], 256) for n in range(group)]
            picked = dot(sides[z], jnp.concatenate(columns, axis=1)).astype(BF)
            for n in range(group):
                row = (begin + n) * height
                picked_ref[row : row + height, z * PAIR : (z + 1) * PAIR] = picked[
                    :, n * PAIR : (n + 1) * PAIR
                ]

    both = dot(weight_ref[...], picked_ref[...])
    low = iota((height, PAIR), 1) < LAYER
    first = both[:height, :PAIR] + rolled(both[height:, :PAIR], LAYER)
    second = rolled(both[:height, PAIR:], LAYER) + both[height:, PAIR:]
    coeffs = (jnp.where(low, first, second) + down_ref[...]).astype(BF)
    coeffs_ref[...] = coeffs
    rank = sum_ref.shape[0]
    total = coeffs[:rank].astype(F32)
    for o in range(1, height // rank):
        total = total + coeffs[o * rank : (o + 1) * rank].astype(F32)
    sum_ref[...] = total.astype(BF)


def final_kernel(
    orbitals_ref, near_ref, sum_ref, other_sum_ref, coeffs_ref, total_ref, other_total_ref, basis_ref, out_ref
):
    orbits = orbitals_ref.shape[0]
    rank = basis_ref.shape[0]
    for pair in range(near_ref.shape[0]):
        lanes = slice(pair * PAIR, (pair + 1) * PAIR)
        hartree = sum_ref[pair].astype(F32) + other_sum_ref[pair].astype(F32)
        total = total_ref[:, lanes].astype(F32) + other_total_ref[:, lanes].astype(F32)
        for o in range(orbits):
            rest = (total - coeffs_ref[o * rank : (o + 1) * rank, lanes].astype(F32)).astype(BF)
            gap = hartree - near_ref[pair, :, o * PAIR : (o + 1) * PAIR] + dot_tn(basis_ref[...], rest)
            value = orbitals_ref[o, lanes]
            out_ref[o, lanes] = value - relax_step * turned(gap) * value


def swap(values, axis, bit):
    count = lax.axis_size(axis)
    return lax.ppermute(values, axis, [(i, i ^ bit) for i in range(count)])


def step_along(values, distance, devices):
    pairs = [(i, i + distance) for i in range(devices) if 0 <= i + distance < devices]
    return lax.ppermute(values, "space", pairs)


def shards(
    orbitals,
    near_source,
    far_leaf,
    far_mid,
    far_top,
    leaf_basis,
    near_table,
    transfer,
    coupling,
    pair_transfer,
    coarse_coupling,
):
    orbits, leaves, points = orbitals.shape
    rank = leaf_basis.shape[0]
    devices = lax.axis_size("space")
    groups = lax.axis_size("orb")
    height = orbits * rank
    wide = orbits * points
    pairs = leaves // PAIR
    slots = far_leaf.shape[1]
    count = devices * (leaves // (LAYER * SIDE))
    assert height == 128 and leaves == 1024 and 2 * count - 1 <= 128
    assert devices & (devices - 1) == 0 and groups == 4
    place = lax.axis_index("space").astype(jnp.int32).reshape(1)
    message = wide + 6 * height
    smem = pl.BlockSpec(memory_space=pltpu.SMEM)

    dense, whole, odd, to_left, to_right = pl.pallas_call(
        moments_kernel,
        in_specs=[smem] + [pl.BlockSpec()] * 3,
        out_shape=(
            jax.ShapeDtypeStruct((wide, leaves - PAIR), BF),
            jax.ShapeDtypeStruct((pairs, height, PAIR), BF),
            jax.ShapeDtypeStruct((pairs + 1, height, PAIR), BF),
            jax.ShapeDtypeStruct((message, PAIR), BF),
            jax.ShapeDtypeStruct((message, PAIR), BF),
        ),
        compiler_params=WIDE_MEMORY,
        name="moments",
    )(place, orbitals, leaf_basis, transfer.reshape(-1, rank))

    from_left = step_along(to_right, 1, devices)
    from_right = step_along(to_left, -1, devices)
    cube_at = message - height
    beside = jnp.where(place[0] % 2 == 0, from_right[cube_at:], from_left[cube_at:])
    cubes = to_left[cube_at:] + beside
    bit = 2
    while 2 * bit < devices:
        cubes = cubes + swap(cubes, "space", bit)
        bit *= 2
    cubes = (cubes, swap(cubes, "space", bit))

    weight = pl.pallas_call(
        widen_kernel,
        out_shape=jax.ShapeDtypeStruct((2 * height, slots // 2 * height), BF),
        compiler_params=WIDE_MEMORY,
        name="widen",
    )(coupling)

    block = lambda which: pl.BlockSpec((wide, PAIR), which)
    inner = pairs - 2
    near = near_call(
        functools.partial(near_inner_kernel, 1, pairs),
        inner,
        lambda i: i + 1,
        leaves,
        orbits,
        near_table,
        (dense, dense),
        (block(lambda i: (0, i)), block(lambda i: (0, i + 1))),
        place,
        near_source.T,
        None,
    )
    near, near_sum = near_call(
        functools.partial(near_outer_kernel, pairs),
        2,
        lambda i: i * (pairs - 1),
        leaves,
        orbits,
        near_table,
        (dense, dense, to_left, to_right, from_left, from_right),
        (
            block(lambda i: (0, 0)),
            block(lambda i: (0, inner)),
            block(lambda i: (0, 0)),
            block(lambda i: (0, 0)),
            block(lambda i: (0, 0)),
            block(lambda i: (0, 0)),
        ),
        place,
        near_source.T,
        near,
    )
    near_chip = near_sum + swap(near_sum, "orb", 1)

    box = lambda n: pl.BlockSpec((height, 128), lambda i: (n, 0))
    base = wide // height
    full = lambda shape: pl.BlockSpec(shape, lambda i: (0,) * len(shape))
    down = pl.pallas_call(
        functools.partial(tree_kernel, count, leaves, rank),
        grid=(1,),
        in_specs=[
            smem,
            box(base + 3),
            box(base + 4),
            box(base + 3),
            box(base + 4),
            box(base + 3),
            box(base + 4),
            full((height, 128)),
            full((height, 128)),
            full(weight.shape),
            full(transfer.shape),
            full(pair_transfer.shape),
            full(coarse_coupling.shape),
            full(far_mid.T.shape),
            full(far_top.shape),
        ],
        out_specs=full((height, leaves)),
        out_shape=jax.ShapeDtypeStruct((height, leaves), F32),
        scratch_shapes=[
            pltpu.VMEM((128, 128), F32),
            pltpu.VMEM((2, 128, 128), F32),
            pltpu.VMEM((slots * height, 256), BF),
        ],
        compiler_params=WIDE_MEMORY,
        name="tree",
    )(
        place,
        to_left,
        to_left,
        from_left,
        from_left,
        from_right,
        from_right,
        *cubes,
        weight,
        transfer,
        pair_transfer,
        coarse_coupling,
        far_mid.T,
        far_top,
    )
    near_other = swap(near_chip, "orb", 2)

    edge = lambda: full(from_left.shape)
    coeffs, coeff_sum = pl.pallas_call(
        functools.partial(leaf_kernel, pairs),
        grid=(pairs,),
        in_specs=[
            smem,
            pl.BlockSpec((slots, PAIR), lambda i: (0, i)),
            full(whole.shape),
            full(odd.shape),
            edge(),
            edge(),
            full(weight.shape),
            pl.BlockSpec((height, PAIR), lambda i: (0, i)),
        ],
        out_specs=(
            pl.BlockSpec((height, PAIR), lambda i: (0, i)),
            pl.BlockSpec((rank, PAIR), lambda i: (0, i)),
        ),
        out_shape=(
            jax.ShapeDtypeStruct((height, leaves), BF),
            jax.ShapeDtypeStruct((rank, leaves), BF),
        ),
        scratch_shapes=[
            pltpu.VMEM((pairs + 2, height, PAIR), BF),
            pltpu.VMEM((pairs + 3, height, PAIR), BF),
            pltpu.VMEM((slots + 4, PAIR), F32),
            pltpu.VMEM((2, slots // 2 + 2, PAIR), F32),
            pltpu.VMEM((slots // 2 * height, 2 * PAIR), BF),
        ],
        compiler_params=WIDE_MEMORY,
        name="leaf",
    )(
        place,
        far_leaf.T,
        whole,
        odd,
        from_left,
        from_right,
        weight,
        down,
    )
    coeff_chip = coeff_sum + swap(coeff_sum, "orb", 1)
    coeff_other = swap(coeff_chip, "orb", 2)

    batch = 2
    per_pair = pl.BlockSpec((batch, points, PAIR), lambda i: (i, 0, 0))
    per_rank = pl.BlockSpec((rank, batch * PAIR), lambda i: (0, i))
    per_leaf = pl.BlockSpec((orbits, batch * PAIR, points), lambda i: (0, i, 0))
    return pl.pallas_call(
        final_kernel,
        grid=(pairs // batch,),
        in_specs=[
            per_leaf,
            pl.BlockSpec((batch, points, orbits * PAIR), lambda i: (i, 0, 0)),
            per_pair,
            per_pair,
            pl.BlockSpec((height, batch * PAIR), lambda i: (0, i)),
            per_rank,
            per_rank,
            full(leaf_basis.shape),
        ],
        out_specs=per_leaf,
        out_shape=jax.ShapeDtypeStruct(orbitals.shape, F32),
        compiler_params=WIDE_MEMORY,
        name="final",
    )(orbitals, near, near_chip, near_other, coeffs, coeff_chip, coeff_other, leaf_basis)


def solution(mesh):
    placed = (
        P("orb", "space", None),
        P("space", None),
        P("space", None),
        P("space", None),
        P("space", None),
        P(),
        P(),
        P(),
        P(),
        P(),
        P(),
    )

    return jax.shard_map(
        shards, mesh=mesh, in_specs=placed, out_specs=P("orb", "space", None), check_vma=False
    )
```

```python
import functools

import jax
import jax.numpy as jnp
from jax import lax
from jax.experimental import pallas as pl
from jax.experimental.pallas import tpu as pltpu
from jax.sharding import PartitionSpec as P


SIDE = 8
LAYER = SIDE * SIDE
PAIR = 2 * LAYER
BF = jnp.bfloat16
F32 = jnp.float32
relax_step = 0.1
MID_RIM = 3 * (SIDE // 2) ** 2
TOP_RIM = 3 * (SIDE // 4) ** 2
MID_AT = LAYER
TOP_AT = MID_AT + MID_RIM
CUBE_AT = TOP_AT + TOP_RIM
WIDE_MEMORY = pltpu.CompilerParams(vmem_limit_bytes=40 * 1024 * 1024)


def iota(shape, axis):
    return lax.broadcasted_iota(jnp.int32, shape, axis)


def dot(left, right):
    return jnp.dot(left, right, preferred_element_type=F32)


def dot_tn(left, right):
    return lax.dot_general(left, right, (((0,), (0,)), ((), ())), preferred_element_type=F32)


def dot_nt(left, right):
    return lax.dot_general(left, right, (((1,), (1,)), ((), ())), preferred_element_type=F32)


def pick_matrix(rows, source_of_lane):
    lanes = source_of_lane.shape[1]
    hit = iota((rows, lanes), 0) == jnp.broadcast_to(source_of_lane, (rows, lanes))
    return jnp.where(hit, 1.0, 0.0).astype(BF)


def index_columns(row, rows):
    lanes = row.shape[1]
    thin = jnp.broadcast_to(row, (16, lanes)).astype(BF)
    tall = jnp.concatenate([thin] * (rows // 16), axis=0)
    steps = iota((rows, lanes), 0).astype(F32).astype(BF)
    return jnp.where(steps == tall, jnp.ones((), BF), jnp.zeros((), BF))


def turned(values):
    return jnp.transpose(values)


def up_level(children, side, transfer, rank):
    half_bits = (side // 2).bit_length() - 1
    lane = iota((1, 128), 1)
    depth = lax.shift_right_logical(lane, 2 * half_bits)
    across = lax.shift_right_logical(lane, half_bits) & (side // 2 - 1)
    along = lane & (side // 2 - 1)
    base = 2 * depth * side * side + 2 * across * side + 2 * along
    orbits = children.shape[0] // rank
    pieces = []
    for octant in range(8):
        offset = (octant // 4) * side * side + (octant // 2 % 2) * side + octant % 2
        pieces.append(dot(children, pick_matrix(children.shape[1], base + offset)).astype(BF))
    totals = []
    for o in range(orbits):
        stacked = jnp.concatenate([piece[o * rank : (o + 1) * rank] for piece in pieces], axis=0)
        totals.append(dot_tn(transfer, stacked))
    return jnp.concatenate(totals, axis=0).astype(BF)


def down_level(parents, child_lanes, side, transfer, rank):
    bits = side.bit_length() - 1
    lane = iota((1, child_lanes), 1)
    depth = lax.shift_right_logical(lane, 2 * bits)
    across = lax.shift_right_logical(lane, bits) & (side - 1)
    along = lane & (side - 1)
    half = side // 2
    parent = (
        lax.shift_right_logical(depth, 1) * half * half
        + lax.shift_right_logical(across, 1) * half
        + lax.shift_right_logical(along, 1)
    )
    octant_of = 4 * (depth & 1) + 2 * (across & 1) + (along & 1)
    spread = dot(parents, pick_matrix(parents.shape[1], parent)).astype(BF)
    thin = jnp.broadcast_to(octant_of.astype(F32), (16, child_lanes)).astype(BF)
    tall = jnp.concatenate([thin] * (rank // 16), axis=0)
    totals = []
    for o in range(parents.shape[0] // rank):
        own = spread[o * rank : (o + 1) * rank]
        kept = [jnp.where(tall == jnp.full((), octant, BF), own, jnp.zeros((), BF)) for octant in range(8)]
        totals.append(dot(transfer, jnp.concatenate(kept, axis=0)))
    return jnp.concatenate(totals, axis=0)


def moments_kernel(
    orbitals_ref,
    basis_ref,
    transfer_ref,
    dense_ref,
    first_ref,
    last_ref,
    whole_ref,
    odd_ref,
    mid_ref,
    top_ref,
    cube_ref,
    left_ref,
    right_ref,
):
    orbits, leaves, points = orbitals_ref.shape
    rank = basis_ref.shape[0]
    basis = basis_ref[...]
    gap = jnp.zeros((LAYER, points), F32)
    moments = []
    moments_odd = []
    first = []
    last = []
    for o in range(orbits):
        value = orbitals_ref[o]
        density = value * value
        rows = slice(o * points, (o + 1) * points)
        dense_ref[rows, :] = turned(density[LAYER : leaves - LAYER]).astype(BF)
        first.append(density[:LAYER])
        last.append(density[leaves - LAYER :])
        first_ref[rows, :] = turned(jnp.concatenate([gap, first[o]], axis=0)).astype(BF)
        last_ref[rows, :] = turned(jnp.concatenate([last[o], gap], axis=0)).astype(BF)
        moments.append(dot_nt(basis, density.astype(BF)))
        shifted = jnp.concatenate([gap, density, gap], axis=0).astype(BF)
        moments_odd.append(dot_nt(basis, shifted))
    left_ref[:points, :] = turned(jnp.concatenate(first[::-1], axis=0)).astype(BF)
    right_ref[:points, :] = turned(jnp.concatenate(last, axis=0)).astype(BF)
    moments = jnp.concatenate(moments, axis=0).astype(BF)
    moments_odd = jnp.concatenate(moments_odd, axis=0).astype(BF)
    blocks = leaves // PAIR
    for b in range(blocks):
        whole_ref[b] = moments[:, b * PAIR : (b + 1) * PAIR]
    for b in range(blocks + 1):
        odd_ref[b] = moments_odd[:, b * PAIR : (b + 1) * PAIR]
    transfer = transfer_ref[...]
    mid = up_level(moments, SIDE, transfer, rank)
    top = up_level(mid, SIDE // 2, transfer, rank)
    cube = up_level(top, SIDE // 4, transfer, rank)
    mid_ref[...] = mid
    top_ref[...] = top
    cube_ref[...] = cube
    height = orbits * rank
    lane = iota((height, 128), 1)
    mid = mid.astype(F32)
    top = top.astype(F32)
    cube = rolled(cube.astype(F32), CUBE_AT)
    tops = leaves // LAYER
    left_ref[points : points + height, :] = moments[:, :PAIR]
    right_ref[points : points + height, :] = moments[:, leaves - PAIR :]
    for ref, third, mid_lane, top_lane in (
        (left_ref, moments[:, PAIR : 2 * PAIR], 0, 0),
        (right_ref, moments_odd[:, leaves - PAIR : leaves], 128 - MID_RIM, tops - TOP_RIM),
    ):
        mixed = jnp.where(
            lane < MID_AT,
            third.astype(F32),
            jnp.where(
                lane < TOP_AT,
                rolled(mid, (MID_AT - mid_lane) % 128),
                jnp.where(lane < CUBE_AT, rolled(top, (TOP_AT - top_lane) % 128), cube),
            ),
        )
        ref[points + height :, :] = mixed.astype(BF)


def join_kernel(own, place_ref, cube_ref, left_ref, right_ref, out_ref):
    place = place_ref[0]
    lane = iota((1, 128), 1)

    def placed(values, device, start):
        which = lane - device * own
        return dot(values, pick_matrix(128, jnp.where((which >= 0) & (which < own), which + start, -1)))

    even = place % 2 == 0
    other = jnp.where(even, right_ref[...].astype(F32), left_ref[...].astype(F32)).astype(BF)
    beside = jnp.where(even, place + 1, place - 1)
    out_ref[...] = (placed(cube_ref[...], place, 0) + placed(other, beside, CUBE_AT)).astype(BF)


def widen_kernel(coupling_ref, out_ref):
    slots, rank, _ = coupling_ref.shape
    count = slots // 2
    blank = jnp.zeros((rank, rank), F32)
    for half in range(2):
        for j in range(count):
            block = coupling_ref[half * count + j].astype(F32)
            cols = slice(j * 2 * rank, (j + 1) * 2 * rank)
            row = half * 2 * rank
            out_ref[row : row + rank, cols] = jnp.concatenate([block, blank], axis=1).astype(BF)
            out_ref[row + rank : row + 2 * rank, cols] = jnp.concatenate([blank, block], axis=1).astype(BF)


def near_body(start, source_ref, table_hbm, out_ref, sum_ref, side_ref, table_ref, turn_ref, picked_ref, sems):
    step = pl.program_id(0)
    slots, points, _ = table_hbm.shape

    def table_copy(k):
        return pltpu.make_async_copy(
            table_hbm.at[k], table_ref.at[:, pl.ds(k * points, points)], sems.at[k]
        )

    @pl.when(step == 0)
    def _():
        for k in range(slots):
            table_copy(k).start()

    turn_ref[:slots, :] = (source_ref[...] - start).astype(F32)
    orbits = side_ref.shape[0] // points
    group = 2
    for begin in range(0, slots, group):
        chunk = range(begin, min(begin + group, slots))
        columns = [index_columns(turn_ref[k : k + 1, :], 2 * PAIR) for k in chunk]
        columns = jnp.concatenate(columns, axis=1)
        for o in range(orbits):
            picked = dot(side_ref[o * points : (o + 1) * points], columns).astype(BF)
            for n, k in enumerate(chunk):
                picked_ref[k * points : (k + 1) * points, o * PAIR : (o + 1) * PAIR] = picked[
                    :, n * PAIR : (n + 1) * PAIR
                ]

    @pl.when(step == 0)
    def _():
        for k in range(slots):
            table_copy(k).wait()

    for rows in (slice(0, points // 2), slice(points // 2, points)):
        field = dot(table_ref[rows, :], picked_ref[...])
        out_ref[step, rows, :] = field
        total = field[:, :PAIR]
        for o in range(1, orbits):
            total = total + field[:, o * PAIR : (o + 1) * PAIR]
        sum_ref[0, rows, :] = total.astype(BF)


def near_kernel(
    place_ref,
    source_ref,
    early_ref,
    late_ref,
    first_ref,
    last_ref,
    got_left_ref,
    got_right_ref,
    table_hbm,
    out_ref,
    sum_ref,
    side_ref,
    *scratch,
):
    step = pl.program_id(0)
    pairs = pl.num_programs(0)
    points = got_left_ref.shape[0]
    side_ref[:, :PAIR] = early_ref[...]
    side_ref[:, PAIR:] = late_ref[...]
    low = iota((points, PAIR), 1) < LAYER

    @pl.when(step == 0)
    def _():
        got = got_left_ref[...].astype(F32)
        for o, part in ((0, got), (1, rolled(got, LAYER))):
            rows = slice(o * points, (o + 1) * points)
            side_ref[rows, :PAIR] = jnp.where(low, part, first_ref[rows, :].astype(F32)).astype(BF)

    @pl.when(step == pairs - 1)
    def _():
        got = got_right_ref[...].astype(F32)
        for o, part in ((0, got), (1, rolled(got, LAYER))):
            rows = slice(o * points, (o + 1) * points)
            side_ref[rows, PAIR:] = jnp.where(low, last_ref[rows, :].astype(F32), part).astype(BF)

    start = (place_ref[0] * pairs + step) * PAIR - LAYER
    near_body(start, source_ref, table_hbm, out_ref, sum_ref, side_ref, *scratch)


def rolled(values, shift):
    return pltpu.roll(values, shift, 1)


def coarse_part(cubes, coupling_ref, pair_ref, count, rank):
    orbits = cubes.shape[0] // rank
    sizes = [count]
    while sizes[-1] > 1:
        sizes.append(sizes[-1] // 2)
    starts = [sum(sizes[:j]) for j in range(len(sizes))]
    last = len(sizes) - 1
    lane = iota((1, 128), 1)
    level = jnp.full((1, 128), -1, jnp.int32)
    node = jnp.zeros((1, 128), jnp.int32)
    size = jnp.zeros((1, 128), jnp.int32)
    start = jnp.zeros((1, 128), jnp.int32)
    child = jnp.full((1, 128), -1, jnp.int32)
    parent = jnp.full((1, 128), -1, jnp.int32)
    scale = jnp.zeros((1, 128), F32)
    for j, (begin, n) in enumerate(zip(starts, sizes)):
        here = (lane >= begin) & (lane < begin + n)
        level = jnp.where(here, j, level)
        node = jnp.where(here, lane - begin, node)
        size = jnp.where(here, n, size)
        start = jnp.where(here, begin, start)
        scale = jnp.where(here, 0.5 ** (3 + j), scale)
        if j:
            child = jnp.where(here, starts[j - 1] + 2 * (lane - begin), child)
        if j < last:
            parent = jnp.where(here, starts[j + 1] + lax.shift_right_logical(lane - begin, 1), parent)
    odd = node & 1
    picks = [pick_matrix(128, jnp.where(child >= 0, child + p, -1)) for p in range(2)]
    current = jnp.where(level == 0, cubes.astype(F32), 0.0).astype(BF)

    def split(values, o):
        return values[o * rank : (o + 1) * rank]

    for j in range(1, last + 1):
        sides = [dot(current, picks[p]).astype(BF) for p in range(2)]
        raised = jnp.concatenate(
            [
                dot_tn(pair_ref[0], split(sides[0], o)) + dot_tn(pair_ref[1], split(sides[1], o))
                for o in range(orbits)
            ],
            axis=0,
        )
        current = jnp.where(level == j, raised, current.astype(F32)).astype(BF)
    far = [None] * orbits
    for which, offset, parity in ((1, -2, None), (2, 2, None), (3, 3, 0), (0, -3, 1)):
        there = node + offset
        good = (there >= 0) & (there < size)
        if parity is not None:
            good = good & (odd == parity)
        side = dot(current, pick_matrix(128, jnp.where(good, start + there, -1))).astype(BF)
        for o in range(orbits):
            part = dot(coupling_ref[which], split(side, o))
            far[o] = part if far[o] is None else far[o] + part
    far = scale * jnp.concatenate(far, axis=0)
    coeffs = far.astype(BF)
    widen = pick_matrix(128, parent)
    for j in range(last - 1, -1, -1):
        spread = dot(coeffs, widen)
        parts = [jnp.where(odd == p, spread, 0.0).astype(BF) for p in range(2)]
        pushed = jnp.concatenate(
            [
                dot(pair_ref[0], split(parts[0], o)) + dot(pair_ref[1], split(parts[1], o))
                for o in range(orbits)
            ],
            axis=0,
        )
        coeffs = jnp.where(level == j, far + pushed, coeffs.astype(F32)).astype(BF)
    return coeffs


def tree_kernel(
    count,
    leaves,
    rank,
    place_ref,
    own_mid_ref,
    own_top_ref,
    left_ref,
    right_ref,
    cube_ref,
    cube_one_ref,
    cube_two_ref,
    cube_three_ref,
    weight_ref,
    transfer_ref,
    pair_ref,
    coarse_ref,
    far_mid_ref,
    far_top_ref,
    out_ref,
    wide_ref,
    turn_ref,
    picked_ref,
):
    place = place_ref[0]
    height = own_mid_ref.shape[0]
    slots = far_mid_ref.shape[0]
    half_slots = slots // 2
    mids = far_mid_ref.shape[1]
    tops = far_top_ref.shape[0]
    mid_rim = MID_RIM
    top_rim = TOP_RIM
    lane = iota((height, 128), 1)

    transfer = jnp.concatenate([transfer_ref[n].astype(F32) for n in range(8)], axis=1).astype(BF)
    cubes = (cube_ref[...] + cube_one_ref[...]) + (cube_two_ref[...] + cube_three_ref[...])
    cube_coeffs = coarse_part(cubes, coarse_ref, pair_ref, count, rank)
    own = leaves // (LAYER * SIDE)
    lane_row = iota((1, 128), 1)
    cube_own = dot(
        cube_coeffs, pick_matrix(128, jnp.where(lane_row < own, lane_row + place * own, -1))
    ).astype(BF)

    left = left_ref[...].astype(F32)
    right = right_ref[...].astype(F32)
    middle = rolled(own_mid_ref[...].astype(F32), mid_rim)
    mid_ext = jnp.concatenate(
        [
            jnp.where(lane < mid_rim, rolled(left, 128 - MID_AT), middle),
            jnp.where(lane < mid_rim, middle, rolled(right, (mid_rim - MID_AT) % 128)),
        ],
        axis=1,
    ).astype(BF)
    middle = rolled(own_top_ref[...].astype(F32), top_rim)
    top_ext = jnp.where(
        lane < top_rim,
        rolled(left, 128 - TOP_AT),
        jnp.where(lane < top_rim + tops, middle, rolled(right, (top_rim + tops - TOP_AT) % 128)),
    ).astype(BF)

    wide_ref[...] = jnp.full(wide_ref.shape, -1.0, F32)
    wide_ref[:tops, :slots] = (far_top_ref[...] - (place * tops - top_rim)).astype(F32)
    turn_ref[0, :slots, :] = (far_mid_ref[...] - (place * mids - mid_rim)).astype(F32)
    packed = 128 // tops
    lanes = iota((1, 128), 1)
    tall = dot_tn(wide_ref[:tops, :].astype(BF), pick_matrix(tops, lanes & (tops - 1)))
    mine = iota((128, 128), 0) & (packed - 1)
    tall = jnp.where(mine == iota((128, 128), 1) // tops, tall, 0.0).astype(BF)
    rows = 128 // packed
    of_group = jnp.where(iota((rows, 128), 0) == iota((rows, 128), 1) // packed, 1.0, 0.0).astype(BF)
    turn_ref[1, :rows, :] = dot(of_group, tall)
    group = 2
    for begin in range(0, slots, packed * group):
        first = begin // packed
        here = range(min(group, pl.cdiv(slots - begin, packed)))
        top_columns = [index_columns(turn_ref[1, first + n : first + n + 1, :], 128) for n in here]
        top_picked = dot(top_ext, jnp.concatenate(top_columns, axis=1))
        for k in range(begin, min(slots, begin + packed * group)):
            block = top_picked[:, (k - begin) // packed * 128 :][:, :128]
            shift = (k % packed) * tops
            block = rolled(block, 128 - shift) if shift else block
            picked_ref[k * height : (k + 1) * height, 128:] = block.astype(BF)
    for begin in range(0, slots, group):
        mid_columns = [index_columns(turn_ref[0, begin + n : begin + n + 1, :], 256) for n in range(group)]
        mid_picked = dot(mid_ext, jnp.concatenate(mid_columns, axis=1)).astype(BF)
        for n in range(group):
            row = (begin + n) * height
            picked_ref[row : row + height, :128] = mid_picked[:, n * 128 : (n + 1) * 128]

    depth = half_slots * height
    far = dot(weight_ref[:height], picked_ref[:depth]) + dot(weight_ref[height:], picked_ref[depth:])
    top = (0.25 * far[:, 128:] + down_level(cube_own, 128, SIDE // 4, transfer, rank)).astype(BF)
    mid = (0.5 * far[:, :128] + down_level(top, 128, SIDE // 2, transfer, rank)).astype(BF)
    out_ref[...] = down_level(mid, leaves, SIDE, transfer, rank)


def leaf_kernel(
    pairs,
    place_ref,
    source_ref,
    whole_ref,
    odd_ref,
    left_ref,
    right_ref,
    weight_ref,
    down_ref,
    coeffs_ref,
    sum_ref,
    even_ref,
    shift_ref,
    turn_ref,
    rows_ref,
    picked_ref,
):
    step = pl.program_id(0)
    height = whole_ref.shape[1]
    slots = source_ref.shape[0]
    half_slots = slots // 2

    @pl.when(step == 0)
    def _():
        first = left_ref.shape[0] - 2 * height
        left = left_ref[first : first + height]
        right = right_ref[first : first + height]
        left_third = left_ref[first + height :].astype(F32)
        right_third = rolled(right_ref[first + height :].astype(F32), LAYER)
        left_turned = rolled(left.astype(F32), LAYER)
        right_turned = rolled(right.astype(F32), LAYER)
        low = iota((height, PAIR), 1) < LAYER
        even_ref[0] = left
        for b in range(pairs):
            even_ref[b + 1] = whole_ref[b]
        even_ref[pairs + 1] = right
        shift_ref[0] = jnp.where(low, left_third, left_turned).astype(BF)
        shift_ref[1] = jnp.where(low, left_turned, odd_ref[0].astype(F32)).astype(BF)
        for b in range(1, pairs):
            shift_ref[b + 1] = odd_ref[b]
        shift_ref[pairs + 1] = jnp.where(low, odd_ref[pairs].astype(F32), right_turned).astype(BF)
        shift_ref[pairs + 2] = jnp.where(low, right_turned, right_third).astype(BF)

    source = source_ref[...]
    batch = source.shape[1] // PAIR
    layer_bits = LAYER.bit_length() - 1
    target_layer = (place_ref[0] * pairs + step * batch) * 2 + lax.shift_right_logical(iota(source.shape, 1), layer_bits)
    away = lax.shift_right_logical(source, layer_bits) - target_layer
    away = jnp.where(away < 0, away + 3, away)
    turn_ref[:slots, :] = (away * LAYER + (source & (LAYER - 1))).astype(F32)
    low = iota((half_slots, PAIR), 1) < LAYER
    for p in range(batch):
        early = turn_ref[:half_slots, p * PAIR : (p + 1) * PAIR]
        late = turn_ref[half_slots:slots, p * PAIR : (p + 1) * PAIR]
        rows_ref[p, 0, :half_slots, :] = jnp.where(low, early, rolled(late, LAYER))
        rows_ref[p, 1, :half_slots, :] = jnp.where(low, rolled(late, LAYER), early)
    group = 2
    low = (iota((height, group * PAIR), 1) & (PAIR - 1)).astype(F32).astype(BF) < jnp.full((), LAYER, BF)
    for p in range(batch):
        pair = step * batch + p
        sides = (
            jnp.concatenate([shift_ref[pair], even_ref[pair + 2]], axis=1),
            jnp.concatenate([even_ref[pair], shift_ref[pair + 3]], axis=1),
        )
        for begin in range(0, half_slots, group):
            picked = []
            for z in range(2):
                columns = [index_columns(rows_ref[p, z, begin + n : begin + n + 1, :], 256) for n in range(group)]
                picked.append(dot(sides[z], jnp.concatenate(columns, axis=1)).astype(BF))
            mixed = (jnp.where(low, picked[0], picked[1]), jnp.where(low, picked[1], picked[0]))
            for half in range(2):
                for n in range(group):
                    row = (begin + n) * height
                    picked_ref[half, row : row + height, p * PAIR : (p + 1) * PAIR] = mixed[half][
                        :, n * PAIR : (n + 1) * PAIR
                    ]

    straight = dot(weight_ref[:height], picked_ref[0])
    crossed = dot(weight_ref[height:], picked_ref[1])
    crossed = [rolled(crossed[:, p * PAIR : (p + 1) * PAIR], LAYER) for p in range(batch)]
    coeffs = (straight + jnp.concatenate(crossed, axis=1) + down_ref[...]).astype(BF)
    coeffs_ref[...] = coeffs
    rank = sum_ref.shape[0]
    total = coeffs[:rank].astype(F32)
    for o in range(1, height // rank):
        total = total + coeffs[o * rank : (o + 1) * rank].astype(F32)
    sum_ref[...] = total.astype(BF)


def final_kernel(
    orbitals_ref, near_ref, sum_ref, other_sum_ref, coeffs_ref, total_ref, other_total_ref, basis_ref, out_ref
):
    orbits = orbitals_ref.shape[0]
    rank = basis_ref.shape[0]
    batch = orbitals_ref.shape[1] // PAIR
    for n in range(batch):
        lanes = slice(n * PAIR, (n + 1) * PAIR)
        pair = pl.program_id(0) * batch + n
        hartree = sum_ref[n].astype(F32) + other_sum_ref[pair].astype(F32)
        total = total_ref[:, lanes].astype(F32) + other_total_ref[:, lanes].astype(F32)
        for o in range(orbits):
            rest = (total - coeffs_ref[o * rank : (o + 1) * rank, lanes].astype(F32)).astype(BF)
            gap = hartree - near_ref[pair, :, o * PAIR : (o + 1) * PAIR] + dot_tn(basis_ref[...], rest)
            value = orbitals_ref[o, lanes]
            out_ref[o, lanes] = value - relax_step * turned(gap) * value


def swap(values, axis, bit):
    count = lax.axis_size(axis)
    return lax.ppermute(values, axis, [(i, i ^ bit) for i in range(count)])


def step_along(values, distance, devices):
    pairs = [(i, i + distance) for i in range(devices) if 0 <= i + distance < devices]
    return lax.ppermute(values, "space", pairs)


def shards(
    orbitals,
    near_source,
    far_leaf,
    far_mid,
    far_top,
    leaf_basis,
    near_table,
    transfer,
    coupling,
    pair_transfer,
    coarse_coupling,
):
    orbits, leaves, points = orbitals.shape
    rank = leaf_basis.shape[0]
    devices = lax.axis_size("space")
    groups = lax.axis_size("orb")
    height = orbits * rank
    wide = orbits * points
    pairs = leaves // PAIR
    slots = far_leaf.shape[1]
    count = devices * (leaves // (LAYER * SIDE))
    assert height == 128 and leaves == 1024 and 2 * count - 1 <= 128
    assert devices & (devices - 1) == 0 and groups == 4
    place = lax.axis_index("space").astype(jnp.int32).reshape(1)
    own = leaves // (LAYER * SIDE)
    assert CUBE_AT + own <= 128
    message = points + 2 * height
    smem = pl.BlockSpec(memory_space=pltpu.SMEM)
    square = jax.ShapeDtypeStruct((height, 128), BF)

    dense, first, last, whole, odd, own_mid, own_top, own_cube, to_left, to_right = pl.pallas_call(
        moments_kernel,
        out_shape=(
            jax.ShapeDtypeStruct((wide, leaves - PAIR), BF),
            jax.ShapeDtypeStruct((wide, PAIR), BF),
            jax.ShapeDtypeStruct((wide, PAIR), BF),
            jax.ShapeDtypeStruct((pairs, height, PAIR), BF),
            jax.ShapeDtypeStruct((pairs + 1, height, PAIR), BF),
            square,
            square,
            square,
            jax.ShapeDtypeStruct((message, PAIR), BF),
            jax.ShapeDtypeStruct((message, PAIR), BF),
        ),
        compiler_params=WIDE_MEMORY,
        name="moments",
    )(orbitals, leaf_basis, transfer.reshape(-1, rank))

    from_left = step_along(to_right, 1, devices)
    from_right = step_along(to_left, -1, devices)
    mixed = pl.BlockSpec((height, 128), lambda i: (message // height - 1, 0))
    full = lambda shape: pl.BlockSpec(shape, lambda i: (0,) * len(shape))
    cubes = pl.pallas_call(
        functools.partial(join_kernel, own),
        grid=(1,),
        in_specs=[smem, full((height, 128)), mixed, mixed],
        out_specs=full((height, 128)),
        out_shape=square,
        compiler_params=WIDE_MEMORY,
        name="join",
    )(place, own_cube, from_left, from_right)
    bit = 2
    while 4 * bit < devices:
        cubes = cubes + swap(cubes, "space", bit)
        bit *= 2
    assert 4 * bit == devices
    cubes = [cubes] + [swap(cubes, "space", n * bit) for n in (1, 2, 3)]

    weight = pl.pallas_call(
        widen_kernel,
        out_shape=jax.ShapeDtypeStruct((2 * height, slots // 2 * height), BF),
        compiler_params=WIDE_MEMORY,
        name="widen",
    )(coupling)

    block = lambda which: pl.BlockSpec((wide, PAIR), which)
    near_slots = near_table.shape[0]
    in_vmem = pl.BlockSpec(memory_space=pltpu.VMEM)
    near, near_sum = pl.pallas_call(
        near_kernel,
        grid=(pairs,),
        in_specs=[
            smem,
            pl.BlockSpec((near_slots, PAIR), lambda i: (0, i)),
            block(lambda i: (0, jnp.maximum(i - 1, 0))),
            block(lambda i: (0, jnp.minimum(i, pairs - 2))),
            *[block(lambda i: (0, 0))] * 2,
            *[pl.BlockSpec((points, PAIR), lambda i: (0, 0))] * 2,
            pl.BlockSpec(memory_space=pl.ANY),
        ],
        out_specs=(in_vmem, pl.BlockSpec((1, points, PAIR), lambda i: (i, 0, 0))),
        out_shape=(
            jax.ShapeDtypeStruct((pairs, points, orbits * PAIR), F32),
            jax.ShapeDtypeStruct((pairs, points, PAIR), BF),
        ),
        scratch_shapes=[
            pltpu.VMEM((wide, 2 * PAIR), BF),
            pltpu.VMEM((points, near_slots * points), BF),
            pltpu.VMEM((32, PAIR), F32),
            pltpu.VMEM((near_slots * points, orbits * PAIR), BF),
            pltpu.SemaphoreType.DMA((near_slots,)),
        ],
        compiler_params=WIDE_MEMORY,
        name="near",
    )(place, near_source.T, dense, dense, first, last, from_left, from_right, near_table)
    near_chip = near_sum + swap(near_sum, "orb", 1)

    down = pl.pallas_call(
        functools.partial(tree_kernel, count, leaves, rank),
        grid=(1,),
        in_specs=[
            smem,
            full((height, 128)),
            full((height, 128)),
            mixed,
            mixed,
            *[full((height, 128))] * 4,
            full(weight.shape),
            full(transfer.shape),
            full(pair_transfer.shape),
            full(coarse_coupling.shape),
            full(far_mid.T.shape),
            full(far_top.shape),
        ],
        out_specs=full((height, leaves)),
        out_shape=jax.ShapeDtypeStruct((height, leaves), F32),
        scratch_shapes=[
            pltpu.VMEM((128, 128), F32),
            pltpu.VMEM((2, 128, 128), F32),
            pltpu.VMEM((slots * height, 256), BF),
        ],
        compiler_params=WIDE_MEMORY,
        name="tree",
    )(
        place,
        own_mid,
        own_top,
        from_left,
        from_right,
        *cubes,
        weight,
        transfer,
        pair_transfer,
        coarse_coupling,
        far_mid.T,
        far_top,
    )
    near_other = swap(near_chip, "orb", 2)

    edge = lambda: full(from_left.shape)
    coeffs, coeff_sum = pl.pallas_call(
        functools.partial(leaf_kernel, pairs),
        grid=(pairs // 2,),
        in_specs=[
            smem,
            pl.BlockSpec((slots, 2 * PAIR), lambda i: (0, i)),
            full(whole.shape),
            full(odd.shape),
            edge(),
            edge(),
            full(weight.shape),
            pl.BlockSpec((height, 2 * PAIR), lambda i: (0, i)),
        ],
        out_specs=(
            pl.BlockSpec((height, 2 * PAIR), lambda i: (0, i)),
            pl.BlockSpec((rank, 2 * PAIR), lambda i: (0, i)),
        ),
        out_shape=(
            jax.ShapeDtypeStruct((height, leaves), BF),
            jax.ShapeDtypeStruct((rank, leaves), BF),
        ),
        scratch_shapes=[
            pltpu.VMEM((pairs + 2, height, PAIR), BF),
            pltpu.VMEM((pairs + 3, height, PAIR), BF),
            pltpu.VMEM((slots + 4, 2 * PAIR), F32),
            pltpu.VMEM((2, 2, slots // 2 + 2, PAIR), F32),
            pltpu.VMEM((2, slots // 2 * height, 2 * PAIR), BF),
        ],
        compiler_params=WIDE_MEMORY,
        name="leaf",
    )(
        place,
        far_leaf.T,
        whole,
        odd,
        from_left,
        from_right,
        weight,
        down,
    )
    coeff_chip = coeff_sum + swap(coeff_sum, "orb", 1)
    coeff_other = swap(coeff_chip, "orb", 2)

    batch = 2
    per_pair = pl.BlockSpec((batch, points, PAIR), lambda i: (i, 0, 0))
    per_rank = pl.BlockSpec((rank, batch * PAIR), lambda i: (0, i))
    per_leaf = pl.BlockSpec((orbits, batch * PAIR, points), lambda i: (0, i, 0))
    return pl.pallas_call(
        final_kernel,
        grid=(pairs // batch,),
        in_specs=[
            per_leaf,
            in_vmem,
            per_pair,
            in_vmem,
            pl.BlockSpec((height, batch * PAIR), lambda i: (0, i)),
            per_rank,
            per_rank,
            full(leaf_basis.shape),
        ],
        out_specs=per_leaf,
        out_shape=jax.ShapeDtypeStruct(orbitals.shape, F32),
        compiler_params=WIDE_MEMORY,
        name="final",
    )(orbitals, near, near_chip, near_other, coeffs, coeff_chip, coeff_other, leaf_basis)


def solution(mesh):
    placed = (
        P("orb", "space", None),
        P("space", None),
        P("space", None),
        P("space", None),
        P("space", None),
        P(),
        P(),
        P(),
        P(),
        P(),
        P(),
    )

    return jax.shard_map(
        shards, mesh=mesh, in_specs=placed, out_specs=P("orb", "space", None), check_vma=False
    )
```

```python
import functools

import jax
import jax.numpy as jnp
from jax import lax
from jax.experimental import pallas as pl
from jax.experimental.pallas import tpu as pltpu
from jax.sharding import PartitionSpec as P


SIDE = 8
LAYER = SIDE * SIDE
PAIR = 2 * LAYER
BF = jnp.bfloat16
F32 = jnp.float32
relax_step = 0.1
MID_RIM = 3 * (SIDE // 2) ** 2
TOP_RIM = 3 * (SIDE // 4) ** 2
MID_AT = LAYER
TOP_AT = MID_AT + MID_RIM
CUBE_AT = TOP_AT + TOP_RIM
WIDE_MEMORY = pltpu.CompilerParams(vmem_limit_bytes=40 * 1024 * 1024)


def iota(shape, axis):
    return lax.broadcasted_iota(jnp.int32, shape, axis)


def dot(left, right):
    return jnp.dot(left, right, preferred_element_type=F32)


def dot_tn(left, right):
    return lax.dot_general(left, right, (((0,), (0,)), ((), ())), preferred_element_type=F32)


def dot_nt(left, right):
    return lax.dot_general(left, right, (((1,), (1,)), ((), ())), preferred_element_type=F32)


def pick_matrix(rows, source_of_lane):
    lanes = source_of_lane.shape[1]
    hit = iota((rows, lanes), 0) == jnp.broadcast_to(source_of_lane, (rows, lanes))
    return jnp.where(hit, 1.0, 0.0).astype(BF)


def index_columns(row, rows):
    lanes = row.shape[1]
    thin = jnp.broadcast_to(row, (16, lanes)).astype(BF)
    tall = jnp.concatenate([thin] * (rows // 16), axis=0)
    steps = iota((rows, lanes), 0).astype(F32).astype(BF)
    return jnp.where(steps == tall, jnp.ones((), BF), jnp.zeros((), BF))


def turned(values):
    return jnp.transpose(values)


def up_level(children, side, transfer, rank):
    half_bits = (side // 2).bit_length() - 1
    lane = iota((1, 128), 1)
    depth = lax.shift_right_logical(lane, 2 * half_bits)
    across = lax.shift_right_logical(lane, half_bits) & (side // 2 - 1)
    along = lane & (side // 2 - 1)
    base = 2 * depth * side * side + 2 * across * side + 2 * along
    orbits = children.shape[0] // rank
    pieces = []
    for octant in range(8):
        offset = (octant // 4) * side * side + (octant // 2 % 2) * side + octant % 2
        pieces.append(dot(children, pick_matrix(children.shape[1], base + offset)).astype(BF))
    totals = []
    for o in range(orbits):
        stacked = jnp.concatenate([piece[o * rank : (o + 1) * rank] for piece in pieces], axis=0)
        totals.append(dot_tn(transfer, stacked))
    return jnp.concatenate(totals, axis=0).astype(BF)


def down_level(parents, child_lanes, side, transfer, rank):
    bits = side.bit_length() - 1
    lane = iota((1, child_lanes), 1)
    depth = lax.shift_right_logical(lane, 2 * bits)
    across = lax.shift_right_logical(lane, bits) & (side - 1)
    along = lane & (side - 1)
    half = side // 2
    parent = (
        lax.shift_right_logical(depth, 1) * half * half
        + lax.shift_right_logical(across, 1) * half
        + lax.shift_right_logical(along, 1)
    )
    octant_of = 4 * (depth & 1) + 2 * (across & 1) + (along & 1)
    spread = dot(parents, pick_matrix(parents.shape[1], parent)).astype(BF)
    thin = jnp.broadcast_to(octant_of.astype(F32), (16, child_lanes)).astype(BF)
    tall = jnp.concatenate([thin] * (rank // 16), axis=0)
    totals = []
    for o in range(parents.shape[0] // rank):
        own = spread[o * rank : (o + 1) * rank]
        kept = [jnp.where(tall == jnp.full((), octant, BF), own, jnp.zeros((), BF)) for octant in range(8)]
        totals.append(dot(transfer, jnp.concatenate(kept, axis=0)))
    return jnp.concatenate(totals, axis=0)


def moments_kernel(
    orbitals_hbm,
    basis_hbm,
    transfer_hbm,
    dense_ref,
    first_ref,
    last_ref,
    whole_ref,
    odd_ref,
    mid_ref,
    top_ref,
    cube_ref,
    left_ref,
    right_ref,
    orbitals_ref,
    basis_ref,
    transfer_ref,
    sems,
):
    orbits, leaves, points = orbitals_ref.shape
    rank = basis_ref.shape[0]
    fetch_basis = pltpu.make_async_copy(basis_hbm, basis_ref, sems.at[orbits])
    fetch_transfer = pltpu.make_async_copy(transfer_hbm, transfer_ref, sems.at[orbits + 1])
    fetches = [
        pltpu.make_async_copy(orbitals_hbm.at[o], orbitals_ref.at[o], sems.at[o]) for o in range(orbits)
    ]
    fetch_basis.start()
    for fetch in fetches:
        fetch.start()
    fetch_transfer.start()
    fetch_basis.wait()
    basis = basis_ref[...]
    gap = jnp.zeros((LAYER, points), F32)
    moments = []
    moments_odd = []
    first = []
    last = []
    for o in range(orbits):
        fetches[o].wait()
        value = orbitals_ref[o]
        density = value * value
        rows = slice(o * points, (o + 1) * points)
        dense_ref[rows, :] = turned(density[LAYER : leaves - LAYER]).astype(BF)
        first.append(density[:LAYER])
        last.append(density[leaves - LAYER :])
        first_ref[rows, :] = turned(jnp.concatenate([gap, first[o]], axis=0)).astype(BF)
        last_ref[rows, :] = turned(jnp.concatenate([last[o], gap], axis=0)).astype(BF)
        moments.append(dot_nt(basis, density.astype(BF)))
        shifted = jnp.concatenate([gap, density, gap], axis=0).astype(BF)
        moments_odd.append(dot_nt(basis, shifted))
    left_ref[:points, :] = turned(jnp.concatenate(first[::-1], axis=0)).astype(BF)
    right_ref[:points, :] = turned(jnp.concatenate(last, axis=0)).astype(BF)
    moments = jnp.concatenate(moments, axis=0).astype(BF)
    moments_odd = jnp.concatenate(moments_odd, axis=0).astype(BF)
    blocks = leaves // PAIR
    for b in range(blocks):
        whole_ref[b] = moments[:, b * PAIR : (b + 1) * PAIR]
    for b in range(blocks + 1):
        odd_ref[b] = moments_odd[:, b * PAIR : (b + 1) * PAIR]
    fetch_transfer.wait()
    transfer = transfer_ref[...]
    mid = up_level(moments, SIDE, transfer, rank)
    top = up_level(mid, SIDE // 2, transfer, rank)
    cube = up_level(top, SIDE // 4, transfer, rank)
    mid_ref[...] = mid
    top_ref[...] = top
    cube_ref[...] = cube
    height = orbits * rank
    lane = iota((height, 128), 1)
    mid = mid.astype(F32)
    top = top.astype(F32)
    cube = rolled(cube.astype(F32), CUBE_AT)
    tops = leaves // LAYER
    left_ref[points : points + height, :] = moments[:, :PAIR]
    right_ref[points : points + height, :] = moments[:, leaves - PAIR :]
    for ref, third, mid_lane, top_lane in (
        (left_ref, moments[:, PAIR : 2 * PAIR], 0, 0),
        (right_ref, moments_odd[:, leaves - PAIR : leaves], 128 - MID_RIM, tops - TOP_RIM),
    ):
        mixed = jnp.where(
            lane < MID_AT,
            third.astype(F32),
            jnp.where(
                lane < TOP_AT,
                rolled(mid, (MID_AT - mid_lane) % 128),
                jnp.where(lane < CUBE_AT, rolled(top, (TOP_AT - top_lane) % 128), cube),
            ),
        )
        ref[points + height :, :] = mixed.astype(BF)


def join_kernel(own, place_ref, cube_ref, left_ref, right_ref, out_ref):
    place = place_ref[0]
    lane = iota((1, 128), 1)

    def placed(values, device, start):
        which = lane - device * own
        return dot(values, pick_matrix(128, jnp.where((which >= 0) & (which < own), which + start, -1)))

    even = place % 2 == 0
    other = jnp.where(even, right_ref[...].astype(F32), left_ref[...].astype(F32)).astype(BF)
    beside = jnp.where(even, place + 1, place - 1)
    out_ref[...] = (placed(cube_ref[...], place, 0) + placed(other, beside, CUBE_AT)).astype(BF)


def widen_kernel(coupling_ref, out_ref):
    slots, rank, _ = coupling_ref.shape
    count = slots // 2
    blank = jnp.zeros((rank, rank), F32)
    for half in range(2):
        for j in range(count):
            block = coupling_ref[half * count + j].astype(F32)
            cols = slice(j * 2 * rank, (j + 1) * 2 * rank)
            row = half * 2 * rank
            out_ref[row : row + rank, cols] = jnp.concatenate([block, blank], axis=1).astype(BF)
            out_ref[row + rank : row + 2 * rank, cols] = jnp.concatenate([blank, block], axis=1).astype(BF)


def near_body(start, source_ref, table_hbm, out_ref, sum_ref, side_ref, table_ref, turn_ref, picked_ref, sems):
    step = pl.program_id(0)
    slots, points, _ = table_hbm.shape

    def table_copy(k):
        return pltpu.make_async_copy(
            table_hbm.at[k], table_ref.at[:, pl.ds(k * points, points)], sems.at[k]
        )

    @pl.when(step == 0)
    def _():
        for k in range(slots):
            table_copy(k).start()

    turn_ref[:slots, :] = (source_ref[...] - start).astype(F32)
    orbits = side_ref.shape[0] // points
    group = 2
    for begin in range(0, slots, group):
        chunk = range(begin, min(begin + group, slots))
        columns = [index_columns(turn_ref[k : k + 1, :], 2 * PAIR) for k in chunk]
        columns = jnp.concatenate(columns, axis=1)
        for o in range(orbits):
            picked = dot(side_ref[o * points : (o + 1) * points], columns).astype(BF)
            for n, k in enumerate(chunk):
                picked_ref[k * points : (k + 1) * points, o * PAIR : (o + 1) * PAIR] = picked[
                    :, n * PAIR : (n + 1) * PAIR
                ]

    @pl.when(step == 0)
    def _():
        for k in range(slots):
            table_copy(k).wait()

    for rows in (slice(0, points // 2), slice(points // 2, points)):
        field = dot(table_ref[rows, :], picked_ref[...])
        out_ref[step, rows, :] = field
        total = field[:, :PAIR]
        for o in range(1, orbits):
            total = total + field[:, o * PAIR : (o + 1) * PAIR]
        sum_ref[0, rows, :] = total.astype(BF)


def near_kernel(
    place_ref,
    source_ref,
    early_ref,
    late_ref,
    first_ref,
    last_ref,
    got_left_ref,
    got_right_ref,
    table_hbm,
    out_ref,
    sum_ref,
    side_ref,
    *scratch,
):
    step = pl.program_id(0)
    pairs = pl.num_programs(0)
    points = got_left_ref.shape[0]
    side_ref[:, :PAIR] = early_ref[...]
    side_ref[:, PAIR:] = late_ref[...]
    low = iota((points, PAIR), 1) < LAYER

    @pl.when(step == 0)
    def _():
        got = got_left_ref[...].astype(F32)
        for o, part in ((0, got), (1, rolled(got, LAYER))):
            rows = slice(o * points, (o + 1) * points)
            side_ref[rows, :PAIR] = jnp.where(low, part, first_ref[rows, :].astype(F32)).astype(BF)

    @pl.when(step == pairs - 1)
    def _():
        got = got_right_ref[...].astype(F32)
        for o, part in ((0, got), (1, rolled(got, LAYER))):
            rows = slice(o * points, (o + 1) * points)
            side_ref[rows, PAIR:] = jnp.where(low, last_ref[rows, :].astype(F32), part).astype(BF)

    start = (place_ref[0] * pairs + step) * PAIR - LAYER
    near_body(start, source_ref, table_hbm, out_ref, sum_ref, side_ref, *scratch)


def rolled(values, shift):
    return pltpu.roll(values, shift, 1)


def coarse_part(cubes, coupling_ref, pair_ref, count, rank):
    orbits = cubes.shape[0] // rank
    sizes = [count]
    while sizes[-1] > 1:
        sizes.append(sizes[-1] // 2)
    starts = [sum(sizes[:j]) for j in range(len(sizes))]
    last = len(sizes) - 1
    lane = iota((1, 128), 1)
    level = jnp.full((1, 128), -1, jnp.int32)
    node = jnp.zeros((1, 128), jnp.int32)
    size = jnp.zeros((1, 128), jnp.int32)
    start = jnp.zeros((1, 128), jnp.int32)
    child = jnp.full((1, 128), -1, jnp.int32)
    parent = jnp.full((1, 128), -1, jnp.int32)
    scale = jnp.zeros((1, 128), F32)
    for j, (begin, n) in enumerate(zip(starts, sizes)):
        here = (lane >= begin) & (lane < begin + n)
        level = jnp.where(here, j, level)
        node = jnp.where(here, lane - begin, node)
        size = jnp.where(here, n, size)
        start = jnp.where(here, begin, start)
        scale = jnp.where(here, 0.5 ** (3 + j), scale)
        if j:
            child = jnp.where(here, starts[j - 1] + 2 * (lane - begin), child)
        if j < last:
            parent = jnp.where(here, starts[j + 1] + lax.shift_right_logical(lane - begin, 1), parent)
    odd = node & 1
    picks = [pick_matrix(128, jnp.where(child >= 0, child + p, -1)) for p in range(2)]
    current = jnp.where(level == 0, cubes.astype(F32), 0.0).astype(BF)

    def split(values, o):
        return values[o * rank : (o + 1) * rank]

    for j in range(1, last + 1):
        sides = [dot(current, picks[p]).astype(BF) for p in range(2)]
        raised = jnp.concatenate(
            [
                dot_tn(pair_ref[0], split(sides[0], o)) + dot_tn(pair_ref[1], split(sides[1], o))
                for o in range(orbits)
            ],
            axis=0,
        )
        current = jnp.where(level == j, raised, current.astype(F32)).astype(BF)
    far = [None] * orbits
    for which, offset, parity in ((1, -2, None), (2, 2, None), (3, 3, 0), (0, -3, 1)):
        there = node + offset
        good = (there >= 0) & (there < size)
        if parity is not None:
            good = good & (odd == parity)
        side = dot(current, pick_matrix(128, jnp.where(good, start + there, -1))).astype(BF)
        for o in range(orbits):
            part = dot(coupling_ref[which], split(side, o))
            far[o] = part if far[o] is None else far[o] + part
    far = scale * jnp.concatenate(far, axis=0)
    coeffs = far.astype(BF)
    widen = pick_matrix(128, parent)
    for j in range(last - 1, -1, -1):
        spread = dot(coeffs, widen)
        parts = [jnp.where(odd == p, spread, 0.0).astype(BF) for p in range(2)]
        pushed = jnp.concatenate(
            [
                dot(pair_ref[0], split(parts[0], o)) + dot(pair_ref[1], split(parts[1], o))
                for o in range(orbits)
            ],
            axis=0,
        )
        coeffs = jnp.where(level == j, far + pushed, coeffs.astype(F32)).astype(BF)
    return coeffs


def tree_kernel(
    count,
    leaves,
    rank,
    place_ref,
    own_mid_ref,
    own_top_ref,
    left_ref,
    right_ref,
    cube_ref,
    cube_one_ref,
    cube_two_ref,
    cube_three_ref,
    weight_ref,
    transfer_ref,
    pair_ref,
    coarse_ref,
    far_mid_ref,
    far_top_ref,
    out_ref,
    wide_ref,
    turn_ref,
    picked_ref,
):
    place = place_ref[0]
    height = own_mid_ref.shape[0]
    slots = far_mid_ref.shape[0]
    half_slots = slots // 2
    mids = far_mid_ref.shape[1]
    tops = far_top_ref.shape[0]
    mid_rim = MID_RIM
    top_rim = TOP_RIM
    lane = iota((height, 128), 1)

    transfer = jnp.concatenate([transfer_ref[n].astype(F32) for n in range(8)], axis=1).astype(BF)
    cubes = (cube_ref[...] + cube_one_ref[...]) + (cube_two_ref[...] + cube_three_ref[...])
    cube_coeffs = coarse_part(cubes, coarse_ref, pair_ref, count, rank)
    own = leaves // (LAYER * SIDE)
    lane_row = iota((1, 128), 1)
    cube_own = dot(
        cube_coeffs, pick_matrix(128, jnp.where(lane_row < own, lane_row + place * own, -1))
    ).astype(BF)

    left = left_ref[...].astype(F32)
    right = right_ref[...].astype(F32)
    middle = rolled(own_mid_ref[...].astype(F32), mid_rim)
    mid_ext = jnp.concatenate(
        [
            jnp.where(lane < mid_rim, rolled(left, 128 - MID_AT), middle),
            jnp.where(lane < mid_rim, middle, rolled(right, (mid_rim - MID_AT) % 128)),
        ],
        axis=1,
    ).astype(BF)
    middle = rolled(own_top_ref[...].astype(F32), top_rim)
    top_ext = jnp.where(
        lane < top_rim,
        rolled(left, 128 - TOP_AT),
        jnp.where(lane < top_rim + tops, middle, rolled(right, (top_rim + tops - TOP_AT) % 128)),
    ).astype(BF)

    wide_ref[...] = jnp.full(wide_ref.shape, -1.0, F32)
    wide_ref[:tops, :slots] = (far_top_ref[...] - (place * tops - top_rim)).astype(F32)
    turn_ref[0, :slots, :] = (far_mid_ref[...] - (place * mids - mid_rim)).astype(F32)
    packed = 128 // tops
    lanes = iota((1, 128), 1)
    tall = dot_tn(wide_ref[:tops, :].astype(BF), pick_matrix(tops, lanes & (tops - 1)))
    mine = iota((128, 128), 0) & (packed - 1)
    tall = jnp.where(mine == iota((128, 128), 1) // tops, tall, 0.0).astype(BF)
    rows = 128 // packed
    of_group = jnp.where(iota((rows, 128), 0) == iota((rows, 128), 1) // packed, 1.0, 0.0).astype(BF)
    turn_ref[1, :rows, :] = dot(of_group, tall)
    group = 2
    for begin in range(0, slots, packed * group):
        first = begin // packed
        here = range(min(group, pl.cdiv(slots - begin, packed)))
        top_columns = [index_columns(turn_ref[1, first + n : first + n + 1, :], 128) for n in here]
        top_picked = dot(top_ext, jnp.concatenate(top_columns, axis=1))
        for k in range(begin, min(slots, begin + packed * group)):
            block = top_picked[:, (k - begin) // packed * 128 :][:, :128]
            shift = (k % packed) * tops
            block = rolled(block, 128 - shift) if shift else block
            picked_ref[k * height : (k + 1) * height, 128:] = block.astype(BF)
    for begin in range(0, slots, group):
        mid_columns = [index_columns(turn_ref[0, begin + n : begin + n + 1, :], 256) for n in range(group)]
        mid_picked = dot(mid_ext, jnp.concatenate(mid_columns, axis=1)).astype(BF)
        for n in range(group):
            row = (begin + n) * height
            picked_ref[row : row + height, :128] = mid_picked[:, n * 128 : (n + 1) * 128]

    depth = half_slots * height
    far = dot(weight_ref[:height], picked_ref[:depth]) + dot(weight_ref[height:], picked_ref[depth:])
    top = (0.25 * far[:, 128:] + down_level(cube_own, 128, SIDE // 4, transfer, rank)).astype(BF)
    mid = (0.5 * far[:, :128] + down_level(top, 128, SIDE // 2, transfer, rank)).astype(BF)
    out_ref[...] = down_level(mid, leaves, SIDE, transfer, rank)


def leaf_kernel(
    pairs,
    place_ref,
    source_ref,
    whole_ref,
    odd_ref,
    left_ref,
    right_ref,
    weight_ref,
    down_ref,
    coeffs_ref,
    sum_ref,
    even_ref,
    shift_ref,
    turn_ref,
    rows_ref,
    picked_ref,
):
    step = pl.program_id(0)
    height = whole_ref.shape[1]
    slots = source_ref.shape[0]
    half_slots = slots // 2

    @pl.when(step == 0)
    def _():
        first = left_ref.shape[0] - 2 * height
        left = left_ref[first : first + height]
        right = right_ref[first : first + height]
        left_third = left_ref[first + height :].astype(F32)
        right_third = rolled(right_ref[first + height :].astype(F32), LAYER)
        left_turned = rolled(left.astype(F32), LAYER)
        right_turned = rolled(right.astype(F32), LAYER)
        low = iota((height, PAIR), 1) < LAYER
        even_ref[0] = left
        for b in range(pairs):
            even_ref[b + 1] = whole_ref[b]
        even_ref[pairs + 1] = right
        shift_ref[0] = jnp.where(low, left_third, left_turned).astype(BF)
        shift_ref[1] = jnp.where(low, left_turned, odd_ref[0].astype(F32)).astype(BF)
        for b in range(1, pairs):
            shift_ref[b + 1] = odd_ref[b]
        shift_ref[pairs + 1] = jnp.where(low, odd_ref[pairs].astype(F32), right_turned).astype(BF)
        shift_ref[pairs + 2] = jnp.where(low, right_turned, right_third).astype(BF)

    source = source_ref[...]
    batch = source.shape[1] // PAIR
    layer_bits = LAYER.bit_length() - 1
    target_layer = (place_ref[0] * pairs + step * batch) * 2 + lax.shift_right_logical(iota(source.shape, 1), layer_bits)
    away = lax.shift_right_logical(source, layer_bits) - target_layer
    away = jnp.where(away < 0, away + 3, away)
    turn_ref[:slots, :] = (away * LAYER + (source & (LAYER - 1))).astype(F32)
    low = iota((half_slots, PAIR), 1) < LAYER
    for p in range(batch):
        early = turn_ref[:half_slots, p * PAIR : (p + 1) * PAIR]
        late = turn_ref[half_slots:slots, p * PAIR : (p + 1) * PAIR]
        rows_ref[p, 0, :half_slots, :] = jnp.where(low, early, rolled(late, LAYER))
        rows_ref[p, 1, :half_slots, :] = jnp.where(low, rolled(late, LAYER), early)
    group = 2
    low = (iota((height, group * PAIR), 1) & (PAIR - 1)).astype(F32).astype(BF) < jnp.full((), LAYER, BF)
    for p in range(batch):
        pair = step * batch + p
        sides = (
            jnp.concatenate([shift_ref[pair], even_ref[pair + 2]], axis=1),
            jnp.concatenate([even_ref[pair], shift_ref[pair + 3]], axis=1),
        )
        for begin in range(0, half_slots, group):
            picked = []
            for z in range(2):
                columns = [index_columns(rows_ref[p, z, begin + n : begin + n + 1, :], 256) for n in range(group)]
                picked.append(dot(sides[z], jnp.concatenate(columns, axis=1)).astype(BF))
            mixed = (jnp.where(low, picked[0], picked[1]), jnp.where(low, picked[1], picked[0]))
            for half in range(2):
                for n in range(group):
                    row = (begin + n) * height
                    picked_ref[half, row : row + height, p * PAIR : (p + 1) * PAIR] = mixed[half][
                        :, n * PAIR : (n + 1) * PAIR
                    ]

    straight = dot(weight_ref[:height], picked_ref[0])
    crossed = dot(weight_ref[height:], picked_ref[1])
    crossed = [rolled(crossed[:, p * PAIR : (p + 1) * PAIR], LAYER) for p in range(batch)]
    coeffs = (straight + jnp.concatenate(crossed, axis=1) + down_ref[...]).astype(BF)
    coeffs_ref[...] = coeffs
    rank = sum_ref.shape[0]
    total = coeffs[:rank].astype(F32)
    for o in range(1, height // rank):
        total = total + coeffs[o * rank : (o + 1) * rank].astype(F32)
    sum_ref[...] = total.astype(BF)


def final_kernel(
    orbitals_ref, near_ref, sum_ref, other_sum_ref, coeffs_ref, total_ref, other_total_ref, basis_ref, out_ref
):
    orbits = orbitals_ref.shape[0]
    rank = basis_ref.shape[0]
    batch = orbitals_ref.shape[1] // PAIR
    for n in range(batch):
        lanes = slice(n * PAIR, (n + 1) * PAIR)
        pair = pl.program_id(0) * batch + n
        hartree = sum_ref[n].astype(F32) + other_sum_ref[pair].astype(F32)
        total = total_ref[:, lanes].astype(F32) + other_total_ref[:, lanes].astype(F32)
        for o in range(orbits):
            rest = (total - coeffs_ref[o * rank : (o + 1) * rank, lanes].astype(F32)).astype(BF)
            gap = hartree - near_ref[pair, :, o * PAIR : (o + 1) * PAIR] + dot_tn(basis_ref[...], rest)
            value = orbitals_ref[o, lanes]
            out_ref[o, lanes] = value - relax_step * turned(gap) * value


def swap(values, axis, bit):
    count = lax.axis_size(axis)
    return lax.ppermute(values, axis, [(i, i ^ bit) for i in range(count)])


def step_along(values, distance, devices):
    pairs = [(i, i + distance) for i in range(devices) if 0 <= i + distance < devices]
    return lax.ppermute(values, "space", pairs)


def shards(
    orbitals,
    near_source,
    far_leaf,
    far_mid,
    far_top,
    leaf_basis,
    near_table,
    transfer,
    coupling,
    pair_transfer,
    coarse_coupling,
):
    orbits, leaves, points = orbitals.shape
    rank = leaf_basis.shape[0]
    devices = lax.axis_size("space")
    groups = lax.axis_size("orb")
    height = orbits * rank
    wide = orbits * points
    pairs = leaves // PAIR
    slots = far_leaf.shape[1]
    count = devices * (leaves // (LAYER * SIDE))
    assert height == 128 and leaves == 1024 and 2 * count - 1 <= 128
    assert devices & (devices - 1) == 0 and groups == 4
    place = lax.axis_index("space").astype(jnp.int32).reshape(1)
    own = leaves // (LAYER * SIDE)
    assert CUBE_AT + own <= 128
    message = points + 2 * height
    smem = pl.BlockSpec(memory_space=pltpu.SMEM)
    in_vmem = pl.BlockSpec(memory_space=pltpu.VMEM)
    square = jax.ShapeDtypeStruct((height, 128), BF)

    dense, first, last, whole, odd, own_mid, own_top, own_cube, to_left, to_right = pl.pallas_call(
        moments_kernel,
        in_specs=[pl.BlockSpec(memory_space=pl.ANY)] * 3,
        out_shape=(
            jax.ShapeDtypeStruct((wide, leaves - PAIR), BF),
            jax.ShapeDtypeStruct((wide, PAIR), BF),
            jax.ShapeDtypeStruct((wide, PAIR), BF),
            jax.ShapeDtypeStruct((pairs, height, PAIR), BF),
            jax.ShapeDtypeStruct((pairs + 1, height, PAIR), BF),
            square,
            square,
            square,
            jax.ShapeDtypeStruct((message, PAIR), BF),
            jax.ShapeDtypeStruct((message, PAIR), BF),
        ),
        scratch_shapes=[
            pltpu.VMEM((orbits, leaves, points), F32),
            pltpu.VMEM((rank, points), BF),
            pltpu.VMEM((8 * rank, rank), BF),
            pltpu.SemaphoreType.DMA((orbits + 2,)),
        ],
        compiler_params=pltpu.CompilerParams(vmem_limit_bytes=60 * 1024 * 1024),
        name="moments",
    )(orbitals, leaf_basis, transfer.reshape(-1, rank))

    from_left = step_along(to_right, 1, devices)
    from_right = step_along(to_left, -1, devices)
    mixed = pl.BlockSpec((height, 128), lambda i: (message // height - 1, 0))
    full = lambda shape: pl.BlockSpec(shape, lambda i: (0,) * len(shape))
    cubes = pl.pallas_call(
        functools.partial(join_kernel, own),
        grid=(1,),
        in_specs=[smem, full((height, 128)), mixed, mixed],
        out_specs=full((height, 128)),
        out_shape=square,
        compiler_params=WIDE_MEMORY,
        name="join",
    )(place, own_cube, from_left, from_right)
    bit = 2
    while 4 * bit < devices:
        cubes = cubes + swap(cubes, "space", bit)
        bit *= 2
    assert 4 * bit == devices
    cubes = [cubes] + [swap(cubes, "space", n * bit) for n in (1, 2, 3)]

    weight = pl.pallas_call(
        widen_kernel,
        out_shape=jax.ShapeDtypeStruct((2 * height, slots // 2 * height), BF),
        compiler_params=WIDE_MEMORY,
        name="widen",
    )(coupling)

    block = lambda which: pl.BlockSpec((wide, PAIR), which)
    near_slots = near_table.shape[0]
    near, near_sum = pl.pallas_call(
        near_kernel,
        grid=(pairs,),
        in_specs=[
            smem,
            pl.BlockSpec((near_slots, PAIR), lambda i: (0, i)),
            block(lambda i: (0, jnp.maximum(i - 1, 0))),
            block(lambda i: (0, jnp.minimum(i, pairs - 2))),
            *[block(lambda i: (0, 0))] * 2,
            *[pl.BlockSpec((points, PAIR), lambda i: (0, 0))] * 2,
            pl.BlockSpec(memory_space=pl.ANY),
        ],
        out_specs=(in_vmem, pl.BlockSpec((1, points, PAIR), lambda i: (i, 0, 0))),
        out_shape=(
            jax.ShapeDtypeStruct((pairs, points, orbits * PAIR), F32),
            jax.ShapeDtypeStruct((pairs, points, PAIR), BF),
        ),
        scratch_shapes=[
            pltpu.VMEM((wide, 2 * PAIR), BF),
            pltpu.VMEM((points, near_slots * points), BF),
            pltpu.VMEM((32, PAIR), F32),
            pltpu.VMEM((near_slots * points, orbits * PAIR), BF),
            pltpu.SemaphoreType.DMA((near_slots,)),
        ],
        compiler_params=WIDE_MEMORY,
        name="near",
    )(place, near_source.T, dense, dense, first, last, from_left, from_right, near_table)
    near_chip = near_sum + swap(near_sum, "orb", 1)

    down = pl.pallas_call(
        functools.partial(tree_kernel, count, leaves, rank),
        grid=(1,),
        in_specs=[
            smem,
            full((height, 128)),
            full((height, 128)),
            mixed,
            mixed,
            *[full((height, 128))] * 4,
            full(weight.shape),
            full(transfer.shape),
            full(pair_transfer.shape),
            full(coarse_coupling.shape),
            full(far_mid.T.shape),
            full(far_top.shape),
        ],
        out_specs=full((height, leaves)),
        out_shape=jax.ShapeDtypeStruct((height, leaves), F32),
        scratch_shapes=[
            pltpu.VMEM((128, 128), F32),
            pltpu.VMEM((2, 128, 128), F32),
            pltpu.VMEM((slots * height, 256), BF),
        ],
        compiler_params=WIDE_MEMORY,
        name="tree",
    )(
        place,
        own_mid,
        own_top,
        from_left,
        from_right,
        *cubes,
        weight,
        transfer,
        pair_transfer,
        coarse_coupling,
        far_mid.T,
        far_top,
    )
    near_other = swap(near_chip, "orb", 2)

    edge = lambda: full(from_left.shape)
    coeffs, coeff_sum = pl.pallas_call(
        functools.partial(leaf_kernel, pairs),
        grid=(pairs // 2,),
        in_specs=[
            smem,
            pl.BlockSpec((slots, 2 * PAIR), lambda i: (0, i)),
            full(whole.shape),
            full(odd.shape),
            edge(),
            edge(),
            full(weight.shape),
            pl.BlockSpec((height, 2 * PAIR), lambda i: (0, i)),
        ],
        out_specs=(
            pl.BlockSpec((height, 2 * PAIR), lambda i: (0, i)),
            pl.BlockSpec((rank, 2 * PAIR), lambda i: (0, i)),
        ),
        out_shape=(
            jax.ShapeDtypeStruct((height, leaves), BF),
            jax.ShapeDtypeStruct((rank, leaves), BF),
        ),
        scratch_shapes=[
            pltpu.VMEM((pairs + 2, height, PAIR), BF),
            pltpu.VMEM((pairs + 3, height, PAIR), BF),
            pltpu.VMEM((slots + 4, 2 * PAIR), F32),
            pltpu.VMEM((2, 2, slots // 2 + 2, PAIR), F32),
            pltpu.VMEM((2, slots // 2 * height, 2 * PAIR), BF),
        ],
        compiler_params=WIDE_MEMORY,
        name="leaf",
    )(
        place,
        far_leaf.T,
        whole,
        odd,
        from_left,
        from_right,
        weight,
        down,
    )
    coeff_chip = coeff_sum + swap(coeff_sum, "orb", 1)
    coeff_other = swap(coeff_chip, "orb", 2)

    batch = 2
    per_pair = pl.BlockSpec((batch, points, PAIR), lambda i: (i, 0, 0))
    per_rank = pl.BlockSpec((rank, batch * PAIR), lambda i: (0, i))
    per_leaf = pl.BlockSpec((orbits, batch * PAIR, points), lambda i: (0, i, 0))
    return pl.pallas_call(
        final_kernel,
        grid=(pairs // batch,),
        in_specs=[
            per_leaf,
            in_vmem,
            per_pair,
            in_vmem,
            pl.BlockSpec((height, batch * PAIR), lambda i: (0, i)),
            per_rank,
            per_rank,
            full(leaf_basis.shape),
        ],
        out_specs=per_leaf,
        out_shape=jax.ShapeDtypeStruct(orbitals.shape, F32),
        compiler_params=WIDE_MEMORY,
        name="final",
    )(orbitals, near, near_chip, near_other, coeffs, coeff_chip, coeff_other, leaf_basis)


def solution(mesh):
    placed = (
        P("orb", "space", None),
        P("space", None),
        P("space", None),
        P("space", None),
        P("space", None),
        P(),
        P(),
        P(),
        P(),
        P(),
        P(),
    )

    return jax.shard_map(
        shards, mesh=mesh, in_specs=placed, out_specs=P("orb", "space", None), check_vma=False
    )
```

```python
import functools

import jax
import jax.numpy as jnp
from jax import lax
from jax.experimental import pallas as pl
from jax.experimental.pallas import tpu as pltpu
from jax.sharding import PartitionSpec as P


SIDE = 8
LAYER = SIDE * SIDE
PAIR = 2 * LAYER
BF = jnp.bfloat16
F32 = jnp.float32
relax_step = 0.1
SELF = 13
MID_RIM = 3 * (SIDE // 2) ** 2
TOP_RIM = 3 * (SIDE // 4) ** 2
MID_AT = LAYER
TOP_AT = MID_AT + MID_RIM
CUBE_AT = TOP_AT + TOP_RIM
WIDE_MEMORY = pltpu.CompilerParams(vmem_limit_bytes=40 * 1024 * 1024)


def iota(shape, axis):
    return lax.broadcasted_iota(jnp.int32, shape, axis)


def dot(left, right):
    return jnp.dot(left, right, preferred_element_type=F32)


def dot_tn(left, right):
    return lax.dot_general(left, right, (((0,), (0,)), ((), ())), preferred_element_type=F32)


def dot_nt(left, right):
    return lax.dot_general(left, right, (((1,), (1,)), ((), ())), preferred_element_type=F32)


def pick_matrix(rows, source_of_lane):
    lanes = source_of_lane.shape[1]
    hit = iota((rows, lanes), 0) == jnp.broadcast_to(source_of_lane, (rows, lanes))
    return jnp.where(hit, 1.0, 0.0).astype(BF)


def index_columns(row, rows):
    lanes = row.shape[1]
    thin = jnp.broadcast_to(row, (16, lanes)).astype(BF)
    tall = jnp.concatenate([thin] * (rows // 16), axis=0)
    steps = iota((rows, lanes), 0).astype(F32).astype(BF)
    return jnp.where(steps == tall, jnp.ones((), BF), jnp.zeros((), BF))


def turned(values):
    return jnp.transpose(values)


def up_level(children, side, transfer, rank):
    half_bits = (side // 2).bit_length() - 1
    lane = iota((1, 128), 1)
    depth = lax.shift_right_logical(lane, 2 * half_bits)
    across = lax.shift_right_logical(lane, half_bits) & (side // 2 - 1)
    along = lane & (side // 2 - 1)
    base = 2 * depth * side * side + 2 * across * side + 2 * along
    orbits = children.shape[0] // rank
    pieces = []
    for octant in range(8):
        offset = (octant // 4) * side * side + (octant // 2 % 2) * side + octant % 2
        pieces.append(dot(children, pick_matrix(children.shape[1], base + offset)).astype(BF))
    totals = []
    for o in range(orbits):
        stacked = jnp.concatenate([piece[o * rank : (o + 1) * rank] for piece in pieces], axis=0)
        totals.append(dot_tn(transfer, stacked))
    return jnp.concatenate(totals, axis=0).astype(BF)


def down_level(parents, child_lanes, side, transfer, rank):
    bits = side.bit_length() - 1
    lane = iota((1, child_lanes), 1)
    depth = lax.shift_right_logical(lane, 2 * bits)
    across = lax.shift_right_logical(lane, bits) & (side - 1)
    along = lane & (side - 1)
    half = side // 2
    parent = (
        lax.shift_right_logical(depth, 1) * half * half
        + lax.shift_right_logical(across, 1) * half
        + lax.shift_right_logical(along, 1)
    )
    octant_of = 4 * (depth & 1) + 2 * (across & 1) + (along & 1)
    spread = dot(parents, pick_matrix(parents.shape[1], parent)).astype(BF)
    thin = jnp.broadcast_to(octant_of.astype(F32), (16, child_lanes)).astype(BF)
    tall = jnp.concatenate([thin] * (rank // 16), axis=0)
    totals = []
    for o in range(parents.shape[0] // rank):
        own = spread[o * rank : (o + 1) * rank]
        kept = [jnp.where(tall == jnp.full((), octant, BF), own, jnp.zeros((), BF)) for octant in range(8)]
        totals.append(dot(transfer, jnp.concatenate(kept, axis=0)))
    return jnp.concatenate(totals, axis=0)


def moments_kernel(
    orbitals_hbm,
    basis_hbm,
    transfer_hbm,
    dense_ref,
    first_ref,
    last_ref,
    whole_ref,
    odd_ref,
    mid_ref,
    top_ref,
    cube_ref,
    left_ref,
    right_ref,
    orbitals_ref,
    basis_ref,
    transfer_ref,
    sems,
):
    orbits, leaves, points = orbitals_ref.shape
    rank = basis_ref.shape[0]
    fetch_basis = pltpu.make_async_copy(basis_hbm, basis_ref, sems.at[orbits])
    fetch_transfer = pltpu.make_async_copy(transfer_hbm, transfer_ref, sems.at[orbits + 1])
    fetches = [
        pltpu.make_async_copy(orbitals_hbm.at[o], orbitals_ref.at[o], sems.at[o]) for o in range(orbits)
    ]
    fetch_basis.start()
    for fetch in fetches:
        fetch.start()
    fetch_transfer.start()
    fetch_basis.wait()
    basis = basis_ref[...]
    gap = jnp.zeros((LAYER, points), F32)
    moments = []
    moments_odd = []
    first = []
    last = []
    for o in range(orbits):
        fetches[o].wait()
        value = orbitals_ref[o]
        density = value * value
        rows = slice(o * points, (o + 1) * points)
        dense_ref[rows, :] = turned(density[LAYER : leaves - LAYER]).astype(BF)
        first.append(density[:LAYER])
        last.append(density[leaves - LAYER :])
        first_ref[rows, :] = turned(jnp.concatenate([gap, first[o]], axis=0)).astype(BF)
        last_ref[rows, :] = turned(jnp.concatenate([last[o], gap], axis=0)).astype(BF)
        moments.append(dot_nt(basis, density.astype(BF)))
        shifted = jnp.concatenate([gap, density, gap], axis=0).astype(BF)
        moments_odd.append(dot_nt(basis, shifted))
    left_ref[:points, :] = turned(jnp.concatenate(first[::-1], axis=0)).astype(BF)
    right_ref[:points, :] = turned(jnp.concatenate(last, axis=0)).astype(BF)
    moments = jnp.concatenate(moments, axis=0).astype(BF)
    moments_odd = jnp.concatenate(moments_odd, axis=0).astype(BF)
    blocks = leaves // PAIR
    for b in range(blocks):
        whole_ref[b] = moments[:, b * PAIR : (b + 1) * PAIR]
    for b in range(blocks + 1):
        odd_ref[b] = moments_odd[:, b * PAIR : (b + 1) * PAIR]
    fetch_transfer.wait()
    transfer = transfer_ref[...]
    mid = up_level(moments, SIDE, transfer, rank)
    top = up_level(mid, SIDE // 2, transfer, rank)
    cube = up_level(top, SIDE // 4, transfer, rank)
    mid_ref[...] = mid
    top_ref[...] = top
    cube_ref[...] = cube
    height = orbits * rank
    lane = iota((height, 128), 1)
    mid = mid.astype(F32)
    top = top.astype(F32)
    cube = rolled(cube.astype(F32), CUBE_AT)
    tops = leaves // LAYER
    left_ref[points : points + height, :] = moments[:, :PAIR]
    right_ref[points : points + height, :] = moments[:, leaves - PAIR :]
    for ref, third, mid_lane, top_lane in (
        (left_ref, moments[:, PAIR : 2 * PAIR], 0, 0),
        (right_ref, moments_odd[:, leaves - PAIR : leaves], 128 - MID_RIM, tops - TOP_RIM),
    ):
        mixed = jnp.where(
            lane < MID_AT,
            third.astype(F32),
            jnp.where(
                lane < TOP_AT,
                rolled(mid, (MID_AT - mid_lane) % 128),
                jnp.where(lane < CUBE_AT, rolled(top, (TOP_AT - top_lane) % 128), cube),
            ),
        )
        ref[points + height :, :] = mixed.astype(BF)


def join_kernel(own, place_ref, cube_ref, left_ref, right_ref, out_ref):
    place = place_ref[0]
    lane = iota((1, 128), 1)

    def placed(values, device, start):
        which = lane - device * own
        return dot(values, pick_matrix(128, jnp.where((which >= 0) & (which < own), which + start, -1)))

    even = place % 2 == 0
    other = jnp.where(even, right_ref[...].astype(F32), left_ref[...].astype(F32)).astype(BF)
    beside = jnp.where(even, place + 1, place - 1)
    out_ref[...] = (placed(cube_ref[...], place, 0) + placed(other, beside, CUBE_AT)).astype(BF)


def widen_kernel(coupling_ref, out_ref):
    slots, rank, _ = coupling_ref.shape
    count = slots // 2
    blank = jnp.zeros((rank, rank), F32)
    for half in range(2):
        for j in range(count):
            block = coupling_ref[half * count + j].astype(F32)
            cols = slice(j * 2 * rank, (j + 1) * 2 * rank)
            row = half * 2 * rank
            out_ref[row : row + rank, cols] = jnp.concatenate([block, blank], axis=1).astype(BF)
            out_ref[row + rank : row + 2 * rank, cols] = jnp.concatenate([blank, block], axis=1).astype(BF)


def near_body(start, source_ref, table_hbm, out_ref, sum_ref, side_ref, table_ref, turn_ref, picked_ref, sems):
    step = pl.program_id(0)
    slots, points, _ = table_hbm.shape

    def table_copy(k):
        return pltpu.make_async_copy(
            table_hbm.at[k], table_ref.at[:, pl.ds(k * points, points)], sems.at[k]
        )

    @pl.when(step == 0)
    def _():
        for k in range(slots):
            table_copy(k).start()

    turn_ref[:slots, :] = (source_ref[...] - start).astype(F32)
    orbits = side_ref.shape[0] // points
    group = 2
    low = iota((points, PAIR), 1) < LAYER
    for o in range(orbits):
        rows = slice(o * points, (o + 1) * points)
        before = side_ref[rows, :PAIR].astype(F32)
        after = side_ref[rows, PAIR:].astype(F32)
        picked_ref[SELF * points : (SELF + 1) * points, o * PAIR : (o + 1) * PAIR] = rolled(
            jnp.where(low, after, before), LAYER
        ).astype(BF)
    entries = [k for k in range(slots) if k != SELF]
    for begin in range(0, len(entries), group):
        chunk = entries[begin : begin + group]
        columns = [index_columns(turn_ref[k : k + 1, :], 2 * PAIR) for k in chunk]
        columns = jnp.concatenate(columns, axis=1)
        for o in range(orbits):
            picked = dot(side_ref[o * points : (o + 1) * points], columns).astype(BF)
            for n, k in enumerate(chunk):
                picked_ref[k * points : (k + 1) * points, o * PAIR : (o + 1) * PAIR] = picked[
                    :, n * PAIR : (n + 1) * PAIR
                ]

    @pl.when(step == 0)
    def _():
        for k in range(slots):
            table_copy(k).wait()

    for rows in (slice(0, points // 2), slice(points // 2, points)):
        field = dot(table_ref[rows, :], picked_ref[...])
        out_ref[step, rows, :] = field
        total = field[:, :PAIR]
        for o in range(1, orbits):
            total = total + field[:, o * PAIR : (o + 1) * PAIR]
        sum_ref[0, rows, :] = total.astype(BF)


def near_kernel(
    place_ref,
    source_ref,
    early_ref,
    late_ref,
    first_ref,
    last_ref,
    got_left_ref,
    got_right_ref,
    table_hbm,
    out_ref,
    sum_ref,
    side_ref,
    *scratch,
):
    step = pl.program_id(0)
    pairs = pl.num_programs(0)
    points = got_left_ref.shape[0]
    side_ref[:, :PAIR] = early_ref[...]
    side_ref[:, PAIR:] = late_ref[...]
    low = iota((points, PAIR), 1) < LAYER

    @pl.when(step == 0)
    def _():
        got = got_left_ref[...].astype(F32)
        for o, part in ((0, got), (1, rolled(got, LAYER))):
            rows = slice(o * points, (o + 1) * points)
            side_ref[rows, :PAIR] = jnp.where(low, part, first_ref[rows, :].astype(F32)).astype(BF)

    @pl.when(step == pairs - 1)
    def _():
        got = got_right_ref[...].astype(F32)
        for o, part in ((0, got), (1, rolled(got, LAYER))):
            rows = slice(o * points, (o + 1) * points)
            side_ref[rows, PAIR:] = jnp.where(low, last_ref[rows, :].astype(F32), part).astype(BF)

    start = (place_ref[0] * pairs + step) * PAIR - LAYER
    near_body(start, source_ref, table_hbm, out_ref, sum_ref, side_ref, *scratch)


def rolled(values, shift):
    return pltpu.roll(values, shift, 1)


def coarse_part(cubes, coupling_ref, pair_ref, count, rank):
    orbits = cubes.shape[0] // rank
    sizes = [count]
    while sizes[-1] > 1:
        sizes.append(sizes[-1] // 2)
    starts = [sum(sizes[:j]) for j in range(len(sizes))]
    last = len(sizes) - 1
    lane = iota((1, 128), 1)
    level = jnp.full((1, 128), -1, jnp.int32)
    node = jnp.zeros((1, 128), jnp.int32)
    size = jnp.zeros((1, 128), jnp.int32)
    start = jnp.zeros((1, 128), jnp.int32)
    child = jnp.full((1, 128), -1, jnp.int32)
    parent = jnp.full((1, 128), -1, jnp.int32)
    scale = jnp.zeros((1, 128), F32)
    for j, (begin, n) in enumerate(zip(starts, sizes)):
        here = (lane >= begin) & (lane < begin + n)
        level = jnp.where(here, j, level)
        node = jnp.where(here, lane - begin, node)
        size = jnp.where(here, n, size)
        start = jnp.where(here, begin, start)
        scale = jnp.where(here, 0.5 ** (3 + j), scale)
        if j:
            child = jnp.where(here, starts[j - 1] + 2 * (lane - begin), child)
        if j < last:
            parent = jnp.where(here, starts[j + 1] + lax.shift_right_logical(lane - begin, 1), parent)
    odd = node & 1
    picks = [pick_matrix(128, jnp.where(child >= 0, child + p, -1)) for p in range(2)]
    current = jnp.where(level == 0, cubes.astype(F32), 0.0).astype(BF)

    def split(values, o):
        return values[o * rank : (o + 1) * rank]

    for j in range(1, last + 1):
        sides = [dot(current, picks[p]).astype(BF) for p in range(2)]
        raised = jnp.concatenate(
            [
                dot_tn(pair_ref[0], split(sides[0], o)) + dot_tn(pair_ref[1], split(sides[1], o))
                for o in range(orbits)
            ],
            axis=0,
        )
        current = jnp.where(level == j, raised, current.astype(F32)).astype(BF)
    far = [None] * orbits
    for which, offset, parity in ((1, -2, None), (2, 2, None), (3, 3, 0), (0, -3, 1)):
        there = node + offset
        good = (there >= 0) & (there < size)
        if parity is not None:
            good = good & (odd == parity)
        side = dot(current, pick_matrix(128, jnp.where(good, start + there, -1))).astype(BF)
        for o in range(orbits):
            part = dot(coupling_ref[which], split(side, o))
            far[o] = part if far[o] is None else far[o] + part
    far = scale * jnp.concatenate(far, axis=0)
    coeffs = far.astype(BF)
    widen = pick_matrix(128, parent)
    for j in range(last - 1, -1, -1):
        spread = dot(coeffs, widen)
        parts = [jnp.where(odd == p, spread, 0.0).astype(BF) for p in range(2)]
        pushed = jnp.concatenate(
            [
                dot(pair_ref[0], split(parts[0], o)) + dot(pair_ref[1], split(parts[1], o))
                for o in range(orbits)
            ],
            axis=0,
        )
        coeffs = jnp.where(level == j, far + pushed, coeffs.astype(F32)).astype(BF)
    return coeffs


def tree_kernel(
    count,
    leaves,
    rank,
    place_ref,
    own_mid_ref,
    own_top_ref,
    left_ref,
    right_ref,
    cube_ref,
    cube_one_ref,
    cube_two_ref,
    cube_three_ref,
    weight_ref,
    transfer_ref,
    pair_ref,
    coarse_ref,
    far_mid_ref,
    far_top_ref,
    out_ref,
    wide_ref,
    turn_ref,
    picked_ref,
):
    place = place_ref[0]
    height = own_mid_ref.shape[0]
    slots = far_mid_ref.shape[0]
    half_slots = slots // 2
    mids = far_mid_ref.shape[1]
    tops = far_top_ref.shape[0]
    mid_rim = MID_RIM
    top_rim = TOP_RIM
    lane = iota((height, 128), 1)

    transfer = jnp.concatenate([transfer_ref[n].astype(F32) for n in range(8)], axis=1).astype(BF)
    cubes = (cube_ref[...] + cube_one_ref[...]) + (cube_two_ref[...] + cube_three_ref[...])
    cube_coeffs = coarse_part(cubes, coarse_ref, pair_ref, count, rank)
    own = leaves // (LAYER * SIDE)
    lane_row = iota((1, 128), 1)
    cube_own = dot(
        cube_coeffs, pick_matrix(128, jnp.where(lane_row < own, lane_row + place * own, -1))
    ).astype(BF)

    left = left_ref[...].astype(F32)
    right = right_ref[...].astype(F32)
    middle = rolled(own_mid_ref[...].astype(F32), mid_rim)
    mid_ext = jnp.concatenate(
        [
            jnp.where(lane < mid_rim, rolled(left, 128 - MID_AT), middle),
            jnp.where(lane < mid_rim, middle, rolled(right, (mid_rim - MID_AT) % 128)),
        ],
        axis=1,
    ).astype(BF)
    middle = rolled(own_top_ref[...].astype(F32), top_rim)
    top_ext = jnp.where(
        lane < top_rim,
        rolled(left, 128 - TOP_AT),
        jnp.where(lane < top_rim + tops, middle, rolled(right, (top_rim + tops - TOP_AT) % 128)),
    ).astype(BF)

    wide_ref[...] = jnp.full(wide_ref.shape, -1.0, F32)
    wide_ref[:tops, :slots] = (far_top_ref[...] - (place * tops - top_rim)).astype(F32)
    turn_ref[0, :slots, :] = (far_mid_ref[...] - (place * mids - mid_rim)).astype(F32)
    packed = 128 // tops
    lanes = iota((1, 128), 1)
    tall = dot_tn(wide_ref[:tops, :].astype(BF), pick_matrix(tops, lanes & (tops - 1)))
    mine = iota((128, 128), 0) & (packed - 1)
    tall = jnp.where(mine == iota((128, 128), 1) // tops, tall, 0.0).astype(BF)
    rows = 128 // packed
    of_group = jnp.where(iota((rows, 128), 0) == iota((rows, 128), 1) // packed, 1.0, 0.0).astype(BF)
    turn_ref[1, :rows, :] = dot(of_group, tall)
    group = 2
    for begin in range(0, slots, packed * group):
        first = begin // packed
        here = range(min(group, pl.cdiv(slots - begin, packed)))
        top_columns = [index_columns(turn_ref[1, first + n : first + n + 1, :], 128) for n in here]
        top_picked = dot(top_ext, jnp.concatenate(top_columns, axis=1))
        for k in range(begin, min(slots, begin + packed * group)):
            block = top_picked[:, (k - begin) // packed * 128 :][:, :128]
            shift = (k % packed) * tops
            block = rolled(block, 128 - shift) if shift else block
            picked_ref[k * height : (k + 1) * height, 128:] = block.astype(BF)
    for begin in range(0, slots, group):
        mid_columns = [index_columns(turn_ref[0, begin + n : begin + n + 1, :], 256) for n in range(group)]
        mid_picked = dot(mid_ext, jnp.concatenate(mid_columns, axis=1)).astype(BF)
        for n in range(group):
            row = (begin + n) * height
            picked_ref[row : row + height, :128] = mid_picked[:, n * 128 : (n + 1) * 128]

    depth = half_slots * height
    scale = jnp.where(iota((1, 256), 1) < 128, 0.5, 0.25)
    far = scale * dot(weight_ref[:height], picked_ref[:depth]) + scale * dot(
        weight_ref[height:], picked_ref[depth:]
    )
    top = (far[:, 128:] + down_level(cube_own, 128, SIDE // 4, transfer, rank)).astype(BF)
    mid = (far[:, :128] + down_level(top, 128, SIDE // 2, transfer, rank)).astype(BF)
    out_ref[...] = down_level(mid, leaves, SIDE, transfer, rank)


def leaf_kernel(
    pairs,
    place_ref,
    source_ref,
    whole_ref,
    odd_ref,
    left_ref,
    right_ref,
    weight_ref,
    down_ref,
    coeffs_ref,
    sum_ref,
    even_ref,
    shift_ref,
    turn_ref,
    rows_ref,
    picked_ref,
):
    step = pl.program_id(0)
    height = whole_ref.shape[1]
    slots = source_ref.shape[0]
    half_slots = slots // 2

    @pl.when(step == 0)
    def _():
        first = left_ref.shape[0] - 2 * height
        left = left_ref[first : first + height]
        right = right_ref[first : first + height]
        left_third = left_ref[first + height :].astype(F32)
        right_third = rolled(right_ref[first + height :].astype(F32), LAYER)
        left_turned = rolled(left.astype(F32), LAYER)
        right_turned = rolled(right.astype(F32), LAYER)
        low = iota((height, PAIR), 1) < LAYER
        even_ref[0] = left
        for b in range(pairs):
            even_ref[b + 1] = whole_ref[b]
        even_ref[pairs + 1] = right
        shift_ref[0] = jnp.where(low, left_third, left_turned).astype(BF)
        shift_ref[1] = jnp.where(low, left_turned, odd_ref[0].astype(F32)).astype(BF)
        for b in range(1, pairs):
            shift_ref[b + 1] = odd_ref[b]
        shift_ref[pairs + 1] = jnp.where(low, odd_ref[pairs].astype(F32), right_turned).astype(BF)
        shift_ref[pairs + 2] = jnp.where(low, right_turned, right_third).astype(BF)

    source = source_ref[...]
    batch = source.shape[1] // PAIR
    layer_bits = LAYER.bit_length() - 1
    target_layer = (place_ref[0] * pairs + step * batch) * 2 + lax.shift_right_logical(iota(source.shape, 1), layer_bits)
    away = lax.shift_right_logical(source, layer_bits) - target_layer
    away = jnp.where(away < 0, away + 3, away)
    turn_ref[:slots, :] = (away * LAYER + (source & (LAYER - 1))).astype(F32)
    low = iota((half_slots, PAIR), 1) < LAYER
    for p in range(batch):
        early = turn_ref[:half_slots, p * PAIR : (p + 1) * PAIR]
        late = turn_ref[half_slots:slots, p * PAIR : (p + 1) * PAIR]
        rows_ref[p, 0, :half_slots, :] = jnp.where(low, early, rolled(late, LAYER))
        rows_ref[p, 1, :half_slots, :] = jnp.where(low, rolled(late, LAYER), early)
    group = 2
    low = (iota((height, group * PAIR), 1) & (PAIR - 1)).astype(F32).astype(BF) < jnp.full((), LAYER, BF)
    for p in range(batch):
        pair = step * batch + p
        sides = (
            jnp.concatenate([shift_ref[pair], even_ref[pair + 2]], axis=1),
            jnp.concatenate([even_ref[pair], shift_ref[pair + 3]], axis=1),
        )
        for begin in range(0, half_slots, group):
            picked = []
            for z in range(2):
                columns = [index_columns(rows_ref[p, z, begin + n : begin + n + 1, :], 256) for n in range(group)]
                picked.append(dot(sides[z], jnp.concatenate(columns, axis=1)).astype(BF))
            mixed = (jnp.where(low, picked[0], picked[1]), jnp.where(low, picked[1], picked[0]))
            for half in range(2):
                for n in range(group):
                    row = (begin + n) * height
                    picked_ref[half, row : row + height, p * PAIR : (p + 1) * PAIR] = mixed[half][
                        :, n * PAIR : (n + 1) * PAIR
                    ]

    straight = dot(weight_ref[:height], picked_ref[0])
    crossed = dot(weight_ref[height:], picked_ref[1])
    crossed = [rolled(crossed[:, p * PAIR : (p + 1) * PAIR], LAYER) for p in range(batch)]
    coeffs = (straight + jnp.concatenate(crossed, axis=1) + down_ref[...]).astype(BF)
    coeffs_ref[...] = coeffs
    rank = sum_ref.shape[0]
    total = coeffs[:rank].astype(F32)
    for o in range(1, height // rank):
        total = total + coeffs[o * rank : (o + 1) * rank].astype(F32)
    sum_ref[...] = total.astype(BF)


def gap_kernel(near_ref, sum_ref, other_sum_ref, coeffs_ref, basis_ref, out_ref):
    orbits, leaves, _ = out_ref.shape
    rank = basis_ref.shape[0]
    batch = leaves // PAIR
    for n in range(batch):
        lanes = slice(n * PAIR, (n + 1) * PAIR)
        pair = pl.program_id(0) * batch + n
        hartree = sum_ref[n].astype(F32) + other_sum_ref[pair].astype(F32)
        for o in range(orbits):
            own = dot_tn(basis_ref[...], coeffs_ref[o * rank : (o + 1) * rank, lanes])
            out_ref[o, lanes] = turned(hartree - near_ref[pair, :, o * PAIR : (o + 1) * PAIR] - own)


def final_kernel(orbitals_ref, gap_ref, total_ref, other_total_ref, basis_ref, out_ref):
    total = (total_ref[...].astype(F32) + other_total_ref[...].astype(F32)).astype(BF)
    shared = dot_tn(total, basis_ref[...])
    for o in range(orbitals_ref.shape[0]):
        value = orbitals_ref[o]
        out_ref[o] = value - relax_step * (gap_ref[o] + shared) * value


def swap(values, axis, bit):
    count = lax.axis_size(axis)
    return lax.ppermute(values, axis, [(i, i ^ bit) for i in range(count)])


def step_along(values, distance, devices):
    pairs = [(i, i + distance) for i in range(devices) if 0 <= i + distance < devices]
    return lax.ppermute(values, "space", pairs)


def shards(
    orbitals,
    near_source,
    far_leaf,
    far_mid,
    far_top,
    leaf_basis,
    near_table,
    transfer,
    coupling,
    pair_transfer,
    coarse_coupling,
):
    orbits, leaves, points = orbitals.shape
    rank = leaf_basis.shape[0]
    devices = lax.axis_size("space")
    groups = lax.axis_size("orb")
    height = orbits * rank
    wide = orbits * points
    pairs = leaves // PAIR
    slots = far_leaf.shape[1]
    count = devices * (leaves // (LAYER * SIDE))
    assert height == 128 and leaves == 1024 and 2 * count - 1 <= 128
    assert devices & (devices - 1) == 0 and groups == 4
    place = lax.axis_index("space").astype(jnp.int32).reshape(1)
    own = leaves // (LAYER * SIDE)
    assert CUBE_AT + own <= 128
    message = points + 2 * height
    smem = pl.BlockSpec(memory_space=pltpu.SMEM)
    in_vmem = pl.BlockSpec(memory_space=pltpu.VMEM)
    square = jax.ShapeDtypeStruct((height, 128), BF)

    dense, first, last, whole, odd, own_mid, own_top, own_cube, to_left, to_right = pl.pallas_call(
        moments_kernel,
        in_specs=[pl.BlockSpec(memory_space=pl.ANY)] * 3,
        out_shape=(
            jax.ShapeDtypeStruct((wide, leaves - PAIR), BF),
            jax.ShapeDtypeStruct((wide, PAIR), BF),
            jax.ShapeDtypeStruct((wide, PAIR), BF),
            jax.ShapeDtypeStruct((pairs, height, PAIR), BF),
            jax.ShapeDtypeStruct((pairs + 1, height, PAIR), BF),
            square,
            square,
            square,
            jax.ShapeDtypeStruct((message, PAIR), BF),
            jax.ShapeDtypeStruct((message, PAIR), BF),
        ),
        scratch_shapes=[
            pltpu.VMEM((orbits, leaves, points), F32),
            pltpu.VMEM((rank, points), BF),
            pltpu.VMEM((8 * rank, rank), BF),
            pltpu.SemaphoreType.DMA((orbits + 2,)),
        ],
        compiler_params=pltpu.CompilerParams(vmem_limit_bytes=60 * 1024 * 1024),
        name="moments",
    )(orbitals, leaf_basis, transfer.reshape(-1, rank))

    from_left = step_along(to_right, 1, devices)
    from_right = step_along(to_left, -1, devices)
    mixed = pl.BlockSpec((height, 128), lambda i: (message // height - 1, 0))
    full = lambda shape: pl.BlockSpec(shape, lambda i: (0,) * len(shape))
    cubes = pl.pallas_call(
        functools.partial(join_kernel, own),
        grid=(1,),
        in_specs=[smem, full((height, 128)), mixed, mixed],
        out_specs=full((height, 128)),
        out_shape=square,
        compiler_params=WIDE_MEMORY,
        name="join",
    )(place, own_cube, from_left, from_right)
    bit = 2
    while 4 * bit < devices:
        cubes = cubes + swap(cubes, "space", bit)
        bit *= 2
    assert 4 * bit == devices
    cubes = [cubes] + [swap(cubes, "space", n * bit) for n in (1, 2, 3)]

    weight = pl.pallas_call(
        widen_kernel,
        out_shape=jax.ShapeDtypeStruct((2 * height, slots // 2 * height), BF),
        compiler_params=WIDE_MEMORY,
        name="widen",
    )(coupling)

    block = lambda which: pl.BlockSpec((wide, PAIR), which)
    near_slots = near_table.shape[0]
    near, near_sum = pl.pallas_call(
        near_kernel,
        grid=(pairs,),
        in_specs=[
            smem,
            pl.BlockSpec((near_slots, PAIR), lambda i: (0, i)),
            block(lambda i: (0, jnp.maximum(i - 1, 0))),
            block(lambda i: (0, jnp.minimum(i, pairs - 2))),
            *[block(lambda i: (0, 0))] * 2,
            *[pl.BlockSpec((points, PAIR), lambda i: (0, 0))] * 2,
            pl.BlockSpec(memory_space=pl.ANY),
        ],
        out_specs=(in_vmem, pl.BlockSpec((1, points, PAIR), lambda i: (i, 0, 0))),
        out_shape=(
            jax.ShapeDtypeStruct((pairs, points, orbits * PAIR), F32),
            jax.ShapeDtypeStruct((pairs, points, PAIR), BF),
        ),
        scratch_shapes=[
            pltpu.VMEM((wide, 2 * PAIR), BF),
            pltpu.VMEM((points, near_slots * points), BF),
            pltpu.VMEM((32, PAIR), F32),
            pltpu.VMEM((near_slots * points, orbits * PAIR), BF),
            pltpu.SemaphoreType.DMA((near_slots,)),
        ],
        compiler_params=WIDE_MEMORY,
        name="near",
    )(place, near_source.T, dense, dense, first, last, from_left, from_right, near_table)
    near_chip = near_sum + swap(near_sum, "orb", 1)

    down = pl.pallas_call(
        functools.partial(tree_kernel, count, leaves, rank),
        grid=(1,),
        in_specs=[
            smem,
            full((height, 128)),
            full((height, 128)),
            mixed,
            mixed,
            *[full((height, 128))] * 4,
            full(weight.shape),
            full(transfer.shape),
            full(pair_transfer.shape),
            full(coarse_coupling.shape),
            full(far_mid.T.shape),
            full(far_top.shape),
        ],
        out_specs=full((height, leaves)),
        out_shape=jax.ShapeDtypeStruct((height, leaves), F32),
        scratch_shapes=[
            pltpu.VMEM((128, 128), F32),
            pltpu.VMEM((2, 128, 128), F32),
            pltpu.VMEM((slots * height, 256), BF),
        ],
        compiler_params=WIDE_MEMORY,
        name="tree",
    )(
        place,
        own_mid,
        own_top,
        from_left,
        from_right,
        *cubes,
        weight,
        transfer,
        pair_transfer,
        coarse_coupling,
        far_mid.T,
        far_top,
    )
    near_other = swap(near_chip, "orb", 2)

    edge = lambda: full(from_left.shape)
    coeffs, coeff_sum = pl.pallas_call(
        functools.partial(leaf_kernel, pairs),
        grid=(pairs // 2,),
        in_specs=[
            smem,
            pl.BlockSpec((slots, 2 * PAIR), lambda i: (0, i)),
            full(whole.shape),
            full(odd.shape),
            edge(),
            edge(),
            full(weight.shape),
            pl.BlockSpec((height, 2 * PAIR), lambda i: (0, i)),
        ],
        out_specs=(
            pl.BlockSpec((height, 2 * PAIR), lambda i: (0, i)),
            pl.BlockSpec((rank, 2 * PAIR), lambda i: (0, i)),
        ),
        out_shape=(
            jax.ShapeDtypeStruct((height, leaves), BF),
            jax.ShapeDtypeStruct((rank, leaves), BF),
        ),
        scratch_shapes=[
            pltpu.VMEM((pairs + 2, height, PAIR), BF),
            pltpu.VMEM((pairs + 3, height, PAIR), BF),
            pltpu.VMEM((slots + 4, 2 * PAIR), F32),
            pltpu.VMEM((2, 2, slots // 2 + 2, PAIR), F32),
            pltpu.VMEM((2, slots // 2 * height, 2 * PAIR), BF),
        ],
        compiler_params=WIDE_MEMORY,
        name="leaf",
    )(
        place,
        far_leaf.T,
        whole,
        odd,
        from_left,
        from_right,
        weight,
        down,
    )
    coeff_chip = coeff_sum + swap(coeff_sum, "orb", 1)
    coeff_other = swap(coeff_chip, "orb", 2)

    batch = 2
    per_pair = pl.BlockSpec((batch, points, PAIR), lambda i: (i, 0, 0))
    per_rank = pl.BlockSpec((rank, batch * PAIR), lambda i: (0, i))
    per_leaf = pl.BlockSpec((orbits, batch * PAIR, points), lambda i: (0, i, 0))
    gap = pl.pallas_call(
        gap_kernel,
        grid=(pairs // batch,),
        in_specs=[
            in_vmem,
            per_pair,
            in_vmem,
            pl.BlockSpec((height, batch * PAIR), lambda i: (0, i)),
            full(leaf_basis.shape),
        ],
        out_specs=per_leaf,
        out_shape=jax.ShapeDtypeStruct(orbitals.shape, F32),
        compiler_params=WIDE_MEMORY,
        name="gap",
    )(near, near_chip, near_other, coeffs, leaf_basis)
    return pl.pallas_call(
        final_kernel,
        grid=(pairs // batch,),
        in_specs=[per_leaf, per_leaf, per_rank, per_rank, full(leaf_basis.shape)],
        out_specs=per_leaf,
        out_shape=jax.ShapeDtypeStruct(orbitals.shape, F32),
        compiler_params=WIDE_MEMORY,
        name="final",
    )(orbitals, gap, coeff_chip, coeff_other, leaf_basis)


def solution(mesh):
    placed = (
        P("orb", "space", None),
        P("space", None),
        P("space", None),
        P("space", None),
        P("space", None),
        P(),
        P(),
        P(),
        P(),
        P(),
        P(),
    )

    return jax.shard_map(
        shards, mesh=mesh, in_specs=placed, out_specs=P("orb", "space", None), check_vma=False
    )
```

```python
import functools

import jax
import jax.numpy as jnp
from jax import lax
from jax.experimental import pallas as pl
from jax.experimental.pallas import tpu as pltpu
from jax.sharding import PartitionSpec as P


SIDE = 8
LAYER = SIDE * SIDE
PAIR = 2 * LAYER
BF = jnp.bfloat16
F32 = jnp.float32
relax_step = 0.1
SELF = 13
MID_RIM = 3 * (SIDE // 2) ** 2
TOP_RIM = 3 * (SIDE // 4) ** 2
MID_AT = LAYER
TOP_AT = MID_AT + MID_RIM
CUBE_AT = TOP_AT + TOP_RIM
WIDE_MEMORY = pltpu.CompilerParams(vmem_limit_bytes=40 * 1024 * 1024)


def iota(shape, axis):
    return lax.broadcasted_iota(jnp.int32, shape, axis)


def dot(left, right):
    return jnp.dot(left, right, preferred_element_type=F32)


def dot_tn(left, right):
    return lax.dot_general(left, right, (((0,), (0,)), ((), ())), preferred_element_type=F32)


def dot_nt(left, right):
    return lax.dot_general(left, right, (((1,), (1,)), ((), ())), preferred_element_type=F32)


def pick_matrix(rows, source_of_lane):
    lanes = source_of_lane.shape[1]
    hit = iota((rows, lanes), 0) == jnp.broadcast_to(source_of_lane, (rows, lanes))
    return jnp.where(hit, 1.0, 0.0).astype(BF)


def index_columns(row, rows):
    lanes = row.shape[1]
    thin = jnp.broadcast_to(row, (16, lanes)).astype(BF)
    tall = jnp.concatenate([thin] * (rows // 16), axis=0)
    steps = iota((rows, lanes), 0).astype(F32).astype(BF)
    return jnp.where(steps == tall, jnp.ones((), BF), jnp.zeros((), BF))


def turned(values):
    return jnp.transpose(values)


def up_level(children, side, transfer, rank):
    half_bits = (side // 2).bit_length() - 1
    lane = iota((1, 128), 1)
    depth = lax.shift_right_logical(lane, 2 * half_bits)
    across = lax.shift_right_logical(lane, half_bits) & (side // 2 - 1)
    along = lane & (side // 2 - 1)
    base = 2 * depth * side * side + 2 * across * side + 2 * along
    orbits = children.shape[0] // rank
    pieces = []
    for octant in range(8):
        offset = (octant // 4) * side * side + (octant // 2 % 2) * side + octant % 2
        pieces.append(dot(children, pick_matrix(children.shape[1], base + offset)).astype(BF))
    totals = []
    for o in range(orbits):
        stacked = jnp.concatenate([piece[o * rank : (o + 1) * rank] for piece in pieces], axis=0)
        totals.append(dot_tn(transfer, stacked))
    return jnp.concatenate(totals, axis=0).astype(BF)


def down_level(parents, child_lanes, side, transfer, rank):
    bits = side.bit_length() - 1
    lane = iota((1, child_lanes), 1)
    depth = lax.shift_right_logical(lane, 2 * bits)
    across = lax.shift_right_logical(lane, bits) & (side - 1)
    along = lane & (side - 1)
    half = side // 2
    parent = (
        lax.shift_right_logical(depth, 1) * half * half
        + lax.shift_right_logical(across, 1) * half
        + lax.shift_right_logical(along, 1)
    )
    octant_of = 4 * (depth & 1) + 2 * (across & 1) + (along & 1)
    spread = dot(parents, pick_matrix(parents.shape[1], parent)).astype(BF)
    thin = jnp.broadcast_to(octant_of.astype(F32), (16, child_lanes)).astype(BF)
    tall = jnp.concatenate([thin] * (rank // 16), axis=0)
    totals = []
    for o in range(parents.shape[0] // rank):
        own = spread[o * rank : (o + 1) * rank]
        kept = [jnp.where(tall == jnp.full((), octant, BF), own, jnp.zeros((), BF)) for octant in range(8)]
        totals.append(dot(transfer, jnp.concatenate(kept, axis=0)))
    return jnp.concatenate(totals, axis=0)


def moments_kernel(
    orbitals_hbm,
    basis_hbm,
    transfer_hbm,
    dense_ref,
    first_ref,
    last_ref,
    whole_ref,
    odd_ref,
    mid_ref,
    top_ref,
    cube_ref,
    left_ref,
    right_ref,
    orbitals_ref,
    basis_ref,
    transfer_ref,
    sems,
):
    orbits, leaves, points = orbitals_ref.shape
    rank = basis_ref.shape[0]
    fetch_basis = pltpu.make_async_copy(basis_hbm, basis_ref, sems.at[orbits])
    fetch_transfer = pltpu.make_async_copy(transfer_hbm, transfer_ref, sems.at[orbits + 1])
    fetches = [
        pltpu.make_async_copy(orbitals_hbm.at[o], orbitals_ref.at[o], sems.at[o]) for o in range(orbits)
    ]
    fetch_basis.start()
    for fetch in fetches:
        fetch.start()
    fetch_transfer.start()
    fetch_basis.wait()
    basis = basis_ref[...]
    gap = jnp.zeros((LAYER, points), F32)
    moments = []
    moments_odd = []
    first = []
    last = []
    for o in range(orbits):
        fetches[o].wait()
        value = orbitals_ref[o]
        density = value * value
        rows = slice(o * points, (o + 1) * points)
        dense_ref[rows, :] = turned(density[LAYER : leaves - LAYER]).astype(BF)
        first.append(density[:LAYER])
        last.append(density[leaves - LAYER :])
        first_ref[rows, :] = turned(jnp.concatenate([gap, first[o]], axis=0)).astype(BF)
        last_ref[rows, :] = turned(jnp.concatenate([last[o], gap], axis=0)).astype(BF)
        moments.append(dot_nt(basis, density.astype(BF)))
        shifted = jnp.concatenate([gap, density, gap], axis=0).astype(BF)
        moments_odd.append(dot_nt(basis, shifted))
    left_ref[:points, :] = turned(jnp.concatenate(first[::-1], axis=0)).astype(BF)
    right_ref[:points, :] = turned(jnp.concatenate(last, axis=0)).astype(BF)
    moments = jnp.concatenate(moments, axis=0).astype(BF)
    moments_odd = jnp.concatenate(moments_odd, axis=0).astype(BF)
    blocks = leaves // PAIR
    for b in range(blocks):
        whole_ref[b] = moments[:, b * PAIR : (b + 1) * PAIR]
    for b in range(blocks + 1):
        odd_ref[b] = moments_odd[:, b * PAIR : (b + 1) * PAIR]
    fetch_transfer.wait()
    transfer = transfer_ref[...]
    mid = up_level(moments, SIDE, transfer, rank)
    top = up_level(mid, SIDE // 2, transfer, rank)
    cube = up_level(top, SIDE // 4, transfer, rank)
    mid_ref[...] = mid
    top_ref[...] = top
    cube_ref[...] = cube
    height = orbits * rank
    lane = iota((height, 128), 1)
    mid = mid.astype(F32)
    top = top.astype(F32)
    cube = rolled(cube.astype(F32), CUBE_AT)
    tops = leaves // LAYER
    left_ref[points : points + height, :] = moments[:, :PAIR]
    right_ref[points : points + height, :] = moments[:, leaves - PAIR :]
    for ref, third, mid_lane, top_lane in (
        (left_ref, moments[:, PAIR : 2 * PAIR], 0, 0),
        (right_ref, moments_odd[:, leaves - PAIR : leaves], 128 - MID_RIM, tops - TOP_RIM),
    ):
        mixed = jnp.where(
            lane < MID_AT,
            third.astype(F32),
            jnp.where(
                lane < TOP_AT,
                rolled(mid, (MID_AT - mid_lane) % 128),
                jnp.where(lane < CUBE_AT, rolled(top, (TOP_AT - top_lane) % 128), cube),
            ),
        )
        ref[points + height :, :] = mixed.astype(BF)


def join_kernel(own, place_ref, cube_ref, left_ref, right_ref, out_ref):
    place = place_ref[0]
    lane = iota((1, 128), 1)

    def placed(values, device, start):
        which = lane - device * own
        return dot(values, pick_matrix(128, jnp.where((which >= 0) & (which < own), which + start, -1)))

    even = place % 2 == 0
    other = jnp.where(even, right_ref[...].astype(F32), left_ref[...].astype(F32)).astype(BF)
    beside = jnp.where(even, place + 1, place - 1)
    out_ref[...] = (placed(cube_ref[...], place, 0) + placed(other, beside, CUBE_AT)).astype(BF)


def widen_kernel(coupling_ref, out_ref):
    slots, rank, _ = coupling_ref.shape
    count = slots // 2
    blank = jnp.zeros((rank, rank), F32)
    for half in range(2):
        for j in range(count):
            block = coupling_ref[half * count + j].astype(F32)
            cols = slice(j * 2 * rank, (j + 1) * 2 * rank)
            row = half * 2 * rank
            out_ref[row : row + rank, cols] = jnp.concatenate([block, blank], axis=1).astype(BF)
            out_ref[row + rank : row + 2 * rank, cols] = jnp.concatenate([blank, block], axis=1).astype(BF)


def near_body(start, source_ref, table_hbm, out_ref, sum_ref, side_ref, table_ref, turn_ref, picked_ref, sems):
    step = pl.program_id(0)
    slots, points, _ = table_hbm.shape

    def table_copy(k):
        return pltpu.make_async_copy(
            table_hbm.at[k], table_ref.at[:, pl.ds(k * points, points)], sems.at[k]
        )

    @pl.when(step == 0)
    def _():
        for k in range(slots):
            table_copy(k).start()

    turn_ref[:slots, :] = (source_ref[...] - start).astype(F32)
    orbits = side_ref.shape[0] // points
    group = 2
    low = iota((points, PAIR), 1) < LAYER
    for o in range(orbits):
        rows = slice(o * points, (o + 1) * points)
        before = side_ref[rows, :PAIR].astype(F32)
        after = side_ref[rows, PAIR:].astype(F32)
        picked_ref[SELF * points : (SELF + 1) * points, o * PAIR : (o + 1) * PAIR] = rolled(
            jnp.where(low, after, before), LAYER
        ).astype(BF)
    entries = [k for k in range(slots) if k != SELF]
    for begin in range(0, len(entries), group):
        chunk = entries[begin : begin + group]
        columns = [index_columns(turn_ref[k : k + 1, :], 2 * PAIR) for k in chunk]
        columns = jnp.concatenate(columns, axis=1)
        for o in range(orbits):
            picked = dot(side_ref[o * points : (o + 1) * points], columns).astype(BF)
            for n, k in enumerate(chunk):
                picked_ref[k * points : (k + 1) * points, o * PAIR : (o + 1) * PAIR] = picked[
                    :, n * PAIR : (n + 1) * PAIR
                ]

    @pl.when(step == 0)
    def _():
        for k in range(slots):
            table_copy(k).wait()

    for rows in (slice(0, points // 2), slice(points // 2, points)):
        field = dot(table_ref[rows, :], picked_ref[...])
        out_ref[step, rows, :] = field
        total = field[:, :PAIR]
        for o in range(1, orbits):
            total = total + field[:, o * PAIR : (o + 1) * PAIR]
        sum_ref[0, rows, :] = total.astype(BF)


def near_kernel(
    place_ref,
    source_ref,
    early_ref,
    late_ref,
    first_ref,
    last_ref,
    got_left_ref,
    got_right_ref,
    table_hbm,
    out_ref,
    sum_ref,
    side_ref,
    *scratch,
):
    step = pl.program_id(0)
    pairs = pl.num_programs(0)
    points = got_left_ref.shape[0]
    side_ref[:, :PAIR] = early_ref[...]
    side_ref[:, PAIR:] = late_ref[...]
    low = iota((points, PAIR), 1) < LAYER

    @pl.when(step == 0)
    def _():
        got = got_left_ref[...].astype(F32)
        for o, part in ((0, got), (1, rolled(got, LAYER))):
            rows = slice(o * points, (o + 1) * points)
            side_ref[rows, :PAIR] = jnp.where(low, part, first_ref[rows, :].astype(F32)).astype(BF)

    @pl.when(step == pairs - 1)
    def _():
        got = got_right_ref[...].astype(F32)
        for o, part in ((0, got), (1, rolled(got, LAYER))):
            rows = slice(o * points, (o + 1) * points)
            side_ref[rows, PAIR:] = jnp.where(low, last_ref[rows, :].astype(F32), part).astype(BF)

    start = (place_ref[0] * pairs + step) * PAIR - LAYER
    near_body(start, source_ref, table_hbm, out_ref, sum_ref, side_ref, *scratch)


def rolled(values, shift):
    return pltpu.roll(values, shift, 1)


def coarse_part(cubes, coupling_ref, pair_ref, count, rank):
    orbits = cubes.shape[0] // rank
    sizes = [count]
    while sizes[-1] > 1:
        sizes.append(sizes[-1] // 2)
    starts = [sum(sizes[:j]) for j in range(len(sizes))]
    last = len(sizes) - 1
    lane = iota((1, 128), 1)
    level = jnp.full((1, 128), -1, jnp.int32)
    node = jnp.zeros((1, 128), jnp.int32)
    size = jnp.zeros((1, 128), jnp.int32)
    start = jnp.zeros((1, 128), jnp.int32)
    child = jnp.full((1, 128), -1, jnp.int32)
    parent = jnp.full((1, 128), -1, jnp.int32)
    scale = jnp.zeros((1, 128), F32)
    for j, (begin, n) in enumerate(zip(starts, sizes)):
        here = (lane >= begin) & (lane < begin + n)
        level = jnp.where(here, j, level)
        node = jnp.where(here, lane - begin, node)
        size = jnp.where(here, n, size)
        start = jnp.where(here, begin, start)
        scale = jnp.where(here, 0.5 ** (3 + j), scale)
        if j:
            child = jnp.where(here, starts[j - 1] + 2 * (lane - begin), child)
        if j < last:
            parent = jnp.where(here, starts[j + 1] + lax.shift_right_logical(lane - begin, 1), parent)
    odd = node & 1
    picks = [pick_matrix(128, jnp.where(child >= 0, child + p, -1)) for p in range(2)]
    current = jnp.where(level == 0, cubes.astype(F32), 0.0).astype(BF)

    def split(values, o):
        return values[o * rank : (o + 1) * rank]

    for j in range(1, last + 1):
        sides = [dot(current, picks[p]).astype(BF) for p in range(2)]
        raised = jnp.concatenate(
            [
                dot_tn(pair_ref[0], split(sides[0], o)) + dot_tn(pair_ref[1], split(sides[1], o))
                for o in range(orbits)
            ],
            axis=0,
        )
        current = jnp.where(level == j, raised, current.astype(F32)).astype(BF)
    far = [None] * orbits
    for which, offset, parity in ((1, -2, None), (2, 2, None), (3, 3, 0), (0, -3, 1)):
        there = node + offset
        good = (there >= 0) & (there < size)
        if parity is not None:
            good = good & (odd == parity)
        side = dot(current, pick_matrix(128, jnp.where(good, start + there, -1))).astype(BF)
        for o in range(orbits):
            part = dot(coupling_ref[which], split(side, o))
            far[o] = part if far[o] is None else far[o] + part
    far = scale * jnp.concatenate(far, axis=0)
    coeffs = far.astype(BF)
    widen = pick_matrix(128, parent)
    for j in range(last - 1, -1, -1):
        spread = dot(coeffs, widen)
        parts = [jnp.where(odd == p, spread, 0.0).astype(BF) for p in range(2)]
        pushed = jnp.concatenate(
            [
                dot(pair_ref[0], split(parts[0], o)) + dot(pair_ref[1], split(parts[1], o))
                for o in range(orbits)
            ],
            axis=0,
        )
        coeffs = jnp.where(level == j, far + pushed, coeffs.astype(F32)).astype(BF)
    return coeffs


def tree_kernel(
    count,
    leaves,
    rank,
    place_ref,
    own_mid_ref,
    own_top_ref,
    left_ref,
    right_ref,
    cube_ref,
    cube_one_ref,
    cube_two_ref,
    cube_three_ref,
    weight_ref,
    transfer_ref,
    pair_ref,
    coarse_ref,
    far_mid_ref,
    far_top_ref,
    out_ref,
    wide_ref,
    turn_ref,
    picked_ref,
):
    place = place_ref[0]
    height = own_mid_ref.shape[0]
    slots = far_mid_ref.shape[0]
    half_slots = slots // 2
    mids = far_mid_ref.shape[1]
    tops = far_top_ref.shape[0]
    mid_rim = MID_RIM
    top_rim = TOP_RIM
    lane = iota((height, 128), 1)

    transfer = jnp.concatenate([transfer_ref[n].astype(F32) for n in range(8)], axis=1).astype(BF)
    cubes = (cube_ref[...] + cube_one_ref[...]) + (cube_two_ref[...] + cube_three_ref[...])
    cube_coeffs = coarse_part(cubes, coarse_ref, pair_ref, count, rank)
    own = leaves // (LAYER * SIDE)
    lane_row = iota((1, 128), 1)
    cube_own = dot(
        cube_coeffs, pick_matrix(128, jnp.where(lane_row < own, lane_row + place * own, -1))
    ).astype(BF)

    left = left_ref[...].astype(F32)
    right = right_ref[...].astype(F32)
    middle = rolled(own_mid_ref[...].astype(F32), mid_rim)
    mid_ext = jnp.concatenate(
        [
            jnp.where(lane < mid_rim, rolled(left, 128 - MID_AT), middle),
            jnp.where(lane < mid_rim, middle, rolled(right, (mid_rim - MID_AT) % 128)),
        ],
        axis=1,
    ).astype(BF)
    middle = rolled(own_top_ref[...].astype(F32), top_rim)
    top_ext = jnp.where(
        lane < top_rim,
        rolled(left, 128 - TOP_AT),
        jnp.where(lane < top_rim + tops, middle, rolled(right, (top_rim + tops - TOP_AT) % 128)),
    ).astype(BF)

    wide_ref[...] = jnp.full(wide_ref.shape, -1.0, F32)
    wide_ref[:tops, :slots] = (far_top_ref[...] - (place * tops - top_rim)).astype(F32)
    turn_ref[0, :slots, :] = (far_mid_ref[...] - (place * mids - mid_rim)).astype(F32)
    packed = 128 // tops
    lanes = iota((1, 128), 1)
    tall = dot_tn(wide_ref[:tops, :].astype(BF), pick_matrix(tops, lanes & (tops - 1)))
    mine = iota((128, 128), 0) & (packed - 1)
    tall = jnp.where(mine == iota((128, 128), 1) // tops, tall, 0.0).astype(BF)
    rows = 128 // packed
    of_group = jnp.where(iota((rows, 128), 0) == iota((rows, 128), 1) // packed, 1.0, 0.0).astype(BF)
    turn_ref[1, :rows, :] = dot(of_group, tall)
    group = 2
    for begin in range(0, slots, packed * group):
        first = begin // packed
        here = range(min(group, pl.cdiv(slots - begin, packed)))
        top_columns = [index_columns(turn_ref[1, first + n : first + n + 1, :], 128) for n in here]
        top_picked = dot(top_ext, jnp.concatenate(top_columns, axis=1))
        for k in range(begin, min(slots, begin + packed * group)):
            block = top_picked[:, (k - begin) // packed * 128 :][:, :128]
            shift = (k % packed) * tops
            block = rolled(block, 128 - shift) if shift else block
            picked_ref[k * height : (k + 1) * height, 128:] = block.astype(BF)
    for begin in range(0, slots, group):
        mid_columns = [index_columns(turn_ref[0, begin + n : begin + n + 1, :], 256) for n in range(group)]
        mid_picked = dot(mid_ext, jnp.concatenate(mid_columns, axis=1)).astype(BF)
        for n in range(group):
            row = (begin + n) * height
            picked_ref[row : row + height, :128] = mid_picked[:, n * 128 : (n + 1) * 128]

    depth = half_slots * height
    scale = jnp.where(iota((1, 256), 1) < 128, 0.5, 0.25)
    far = scale * dot(weight_ref[:height], picked_ref[:depth]) + scale * dot(
        weight_ref[height:], picked_ref[depth:]
    )
    top = (far[:, 128:] + down_level(cube_own, 128, SIDE // 4, transfer, rank)).astype(BF)
    mid = (far[:, :128] + down_level(top, 128, SIDE // 2, transfer, rank)).astype(BF)
    out_ref[...] = down_level(mid, leaves, SIDE, transfer, rank)


def leaf_kernel(
    pairs,
    place_ref,
    source_ref,
    whole_ref,
    odd_ref,
    left_ref,
    right_ref,
    weight_ref,
    down_ref,
    coeffs_ref,
    sum_ref,
    even_ref,
    shift_ref,
    turn_ref,
    rows_ref,
    picked_ref,
):
    step = pl.program_id(0)
    height = whole_ref.shape[1]
    slots = source_ref.shape[0]
    half_slots = slots // 2

    @pl.when(step == 0)
    def _():
        first = left_ref.shape[0] - 2 * height
        left = left_ref[first : first + height]
        right = right_ref[first : first + height]
        left_third = left_ref[first + height :].astype(F32)
        right_third = rolled(right_ref[first + height :].astype(F32), LAYER)
        left_turned = rolled(left.astype(F32), LAYER)
        right_turned = rolled(right.astype(F32), LAYER)
        low = iota((height, PAIR), 1) < LAYER
        even_ref[0] = left
        for b in range(pairs):
            even_ref[b + 1] = whole_ref[b]
        even_ref[pairs + 1] = right
        shift_ref[0] = jnp.where(low, left_third, left_turned).astype(BF)
        shift_ref[1] = jnp.where(low, left_turned, odd_ref[0].astype(F32)).astype(BF)
        for b in range(1, pairs):
            shift_ref[b + 1] = odd_ref[b]
        shift_ref[pairs + 1] = jnp.where(low, odd_ref[pairs].astype(F32), right_turned).astype(BF)
        shift_ref[pairs + 2] = jnp.where(low, right_turned, right_third).astype(BF)

    source = source_ref[...]
    batch = source.shape[1] // PAIR
    layer_bits = LAYER.bit_length() - 1
    target_layer = (place_ref[0] * pairs + step * batch) * 2 + lax.shift_right_logical(iota(source.shape, 1), layer_bits)
    away = lax.shift_right_logical(source, layer_bits) - target_layer
    away = jnp.where(away < 0, away + 3, away)
    turn_ref[:slots, :] = (away * LAYER + (source & (LAYER - 1))).astype(F32)
    low = iota((half_slots, PAIR), 1) < LAYER
    for p in range(batch):
        early = turn_ref[:half_slots, p * PAIR : (p + 1) * PAIR]
        late = turn_ref[half_slots:slots, p * PAIR : (p + 1) * PAIR]
        rows_ref[p, 0, :half_slots, :] = jnp.where(low, early, rolled(late, LAYER))
        rows_ref[p, 1, :half_slots, :] = jnp.where(low, rolled(late, LAYER), early)
    group = 2
    low = (iota((height, group * PAIR), 1) & (PAIR - 1)).astype(F32).astype(BF) < jnp.full((), LAYER, BF)
    for p in range(batch):
        pair = step * batch + p
        sides = (
            jnp.concatenate([shift_ref[pair], even_ref[pair + 2]], axis=1),
            jnp.concatenate([even_ref[pair], shift_ref[pair + 3]], axis=1),
        )
        for begin in range(0, half_slots, group):
            picked = []
            for z in range(2):
                columns = [index_columns(rows_ref[p, z, begin + n : begin + n + 1, :], 256) for n in range(group)]
                picked.append(dot(sides[z], jnp.concatenate(columns, axis=1)).astype(BF))
            mixed = (jnp.where(low, picked[0], picked[1]), jnp.where(low, picked[1], picked[0]))
            for half in range(2):
                for n in range(group):
                    row = (begin + n) * height
                    picked_ref[half, row : row + height, p * PAIR : (p + 1) * PAIR] = mixed[half][
                        :, n * PAIR : (n + 1) * PAIR
                    ]

    straight = dot(weight_ref[:height], picked_ref[0])
    crossed = dot(weight_ref[height:], picked_ref[1])
    crossed = [rolled(crossed[:, p * PAIR : (p + 1) * PAIR], LAYER) for p in range(batch)]
    coeffs = (straight + jnp.concatenate(crossed, axis=1) + down_ref[...]).astype(BF)
    coeffs_ref[...] = coeffs
    rank = sum_ref.shape[0]
    total = coeffs[:rank].astype(F32)
    for o in range(1, height // rank):
        total = total + coeffs[o * rank : (o + 1) * rank].astype(F32)
    sum_ref[...] = total.astype(BF)


def gap_kernel(near_ref, sum_ref, other_sum_ref, coeffs_ref, basis_ref, out_ref):
    orbits = out_ref.shape[0]
    rank = basis_ref.shape[0]
    batch = sum_ref.shape[0]
    for n in range(batch):
        lanes = slice(n * PAIR, (n + 1) * PAIR)
        pair = pl.program_id(0) * batch + n
        rows = pl.ds(pl.multiple_of(pair * PAIR, PAIR), PAIR)
        hartree = sum_ref[n].astype(F32) + other_sum_ref[pair].astype(F32)
        for o in range(orbits):
            own = dot_tn(basis_ref[...], coeffs_ref[o * rank : (o + 1) * rank, lanes])
            out_ref[o, rows] = turned(hartree - near_ref[pair, :, o * PAIR : (o + 1) * PAIR] - own)


def final_kernel(orbitals_ref, gap_ref, total_ref, other_total_ref, basis_ref, out_ref):
    total = (total_ref[...].astype(F32) + other_total_ref[...].astype(F32)).astype(BF)
    shared = dot_tn(total, basis_ref[...])
    count = out_ref.shape[1]
    rows = pl.ds(pl.multiple_of(pl.program_id(0) * count, count), count)
    for o in range(out_ref.shape[0]):
        value = orbitals_ref[o, rows]
        out_ref[o] = value - relax_step * (gap_ref[o, rows] + shared) * value


def swap(values, axis, bit):
    count = lax.axis_size(axis)
    return lax.ppermute(values, axis, [(i, i ^ bit) for i in range(count)])


def step_along(values, distance, devices):
    pairs = [(i, i + distance) for i in range(devices) if 0 <= i + distance < devices]
    return lax.ppermute(values, "space", pairs)


def shards(
    orbitals,
    near_source,
    far_leaf,
    far_mid,
    far_top,
    leaf_basis,
    near_table,
    transfer,
    coupling,
    pair_transfer,
    coarse_coupling,
):
    orbits, leaves, points = orbitals.shape
    rank = leaf_basis.shape[0]
    devices = lax.axis_size("space")
    groups = lax.axis_size("orb")
    height = orbits * rank
    wide = orbits * points
    pairs = leaves // PAIR
    slots = far_leaf.shape[1]
    count = devices * (leaves // (LAYER * SIDE))
    assert height == 128 and leaves == 1024 and 2 * count - 1 <= 128
    assert devices & (devices - 1) == 0 and groups == 4
    place = lax.axis_index("space").astype(jnp.int32).reshape(1)
    own = leaves // (LAYER * SIDE)
    assert CUBE_AT + own <= 128
    message = points + 2 * height
    smem = pl.BlockSpec(memory_space=pltpu.SMEM)
    in_vmem = pl.BlockSpec(memory_space=pltpu.VMEM)
    square = jax.ShapeDtypeStruct((height, 128), BF)

    dense, first, last, whole, odd, own_mid, own_top, own_cube, to_left, to_right = pl.pallas_call(
        moments_kernel,
        in_specs=[pl.BlockSpec(memory_space=pl.ANY)] * 3,
        out_shape=(
            jax.ShapeDtypeStruct((wide, leaves - PAIR), BF),
            jax.ShapeDtypeStruct((wide, PAIR), BF),
            jax.ShapeDtypeStruct((wide, PAIR), BF),
            jax.ShapeDtypeStruct((pairs, height, PAIR), BF),
            jax.ShapeDtypeStruct((pairs + 1, height, PAIR), BF),
            square,
            square,
            square,
            jax.ShapeDtypeStruct((message, PAIR), BF),
            jax.ShapeDtypeStruct((message, PAIR), BF),
        ),
        scratch_shapes=[
            pltpu.VMEM((orbits, leaves, points), F32),
            pltpu.VMEM((rank, points), BF),
            pltpu.VMEM((8 * rank, rank), BF),
            pltpu.SemaphoreType.DMA((orbits + 2,)),
        ],
        compiler_params=pltpu.CompilerParams(vmem_limit_bytes=60 * 1024 * 1024),
        name="moments",
    )(orbitals, leaf_basis, transfer.reshape(-1, rank))

    from_left = step_along(to_right, 1, devices)
    from_right = step_along(to_left, -1, devices)
    mixed = pl.BlockSpec((height, 128), lambda i: (message // height - 1, 0))
    full = lambda shape: pl.BlockSpec(shape, lambda i: (0,) * len(shape))
    cubes = pl.pallas_call(
        functools.partial(join_kernel, own),
        grid=(1,),
        in_specs=[smem, full((height, 128)), mixed, mixed],
        out_specs=full((height, 128)),
        out_shape=square,
        compiler_params=WIDE_MEMORY,
        name="join",
    )(place, own_cube, from_left, from_right)
    bit = 2
    while 4 * bit < devices:
        cubes = cubes + swap(cubes, "space", bit)
        bit *= 2
    assert 4 * bit == devices
    cubes = [cubes] + [swap(cubes, "space", n * bit) for n in (1, 2, 3)]

    weight = pl.pallas_call(
        widen_kernel,
        out_shape=jax.ShapeDtypeStruct((2 * height, slots // 2 * height), BF),
        compiler_params=WIDE_MEMORY,
        name="widen",
    )(coupling)

    block = lambda which: pl.BlockSpec((wide, PAIR), which)
    near_slots = near_table.shape[0]
    near, near_sum = pl.pallas_call(
        near_kernel,
        grid=(pairs,),
        in_specs=[
            smem,
            pl.BlockSpec((near_slots, PAIR), lambda i: (0, i)),
            block(lambda i: (0, jnp.maximum(i - 1, 0))),
            block(lambda i: (0, jnp.minimum(i, pairs - 2))),
            *[block(lambda i: (0, 0))] * 2,
            *[pl.BlockSpec((points, PAIR), lambda i: (0, 0))] * 2,
            pl.BlockSpec(memory_space=pl.ANY),
        ],
        out_specs=(in_vmem, pl.BlockSpec((1, points, PAIR), lambda i: (i, 0, 0))),
        out_shape=(
            jax.ShapeDtypeStruct((pairs, points, orbits * PAIR), F32),
            jax.ShapeDtypeStruct((pairs, points, PAIR), BF),
        ),
        scratch_shapes=[
            pltpu.VMEM((wide, 2 * PAIR), BF),
            pltpu.VMEM((points, near_slots * points), BF),
            pltpu.VMEM((32, PAIR), F32),
            pltpu.VMEM((near_slots * points, orbits * PAIR), BF),
            pltpu.SemaphoreType.DMA((near_slots,)),
        ],
        compiler_params=WIDE_MEMORY,
        name="near",
    )(place, near_source.T, dense, dense, first, last, from_left, from_right, near_table)
    near_chip = near_sum + swap(near_sum, "orb", 1)

    down = pl.pallas_call(
        functools.partial(tree_kernel, count, leaves, rank),
        grid=(1,),
        in_specs=[
            smem,
            in_vmem,
            in_vmem,
            mixed,
            mixed,
            *[in_vmem] * 10,
        ],
        out_specs=in_vmem,
        out_shape=jax.ShapeDtypeStruct((height, leaves), F32),
        scratch_shapes=[
            pltpu.VMEM((128, 128), F32),
            pltpu.VMEM((2, 128, 128), F32),
            pltpu.VMEM((slots * height, 256), BF),
        ],
        compiler_params=WIDE_MEMORY,
        name="tree",
    )(
        place,
        own_mid,
        own_top,
        from_left,
        from_right,
        *cubes,
        weight,
        transfer,
        pair_transfer,
        coarse_coupling,
        far_mid.T,
        far_top,
    )
    near_other = swap(near_chip, "orb", 2)

    coeffs, coeff_sum = pl.pallas_call(
        functools.partial(leaf_kernel, pairs),
        grid=(pairs // 2,),
        in_specs=[
            smem,
            pl.BlockSpec((slots, 2 * PAIR), lambda i: (0, i)),
            in_vmem,
            in_vmem,
            in_vmem,
            in_vmem,
            in_vmem,
            pl.BlockSpec((height, 2 * PAIR), lambda i: (0, i)),
        ],
        out_specs=(
            pl.BlockSpec((height, 2 * PAIR), lambda i: (0, i)),
            pl.BlockSpec((rank, 2 * PAIR), lambda i: (0, i)),
        ),
        out_shape=(
            jax.ShapeDtypeStruct((height, leaves), BF),
            jax.ShapeDtypeStruct((rank, leaves), BF),
        ),
        scratch_shapes=[
            pltpu.VMEM((pairs + 2, height, PAIR), BF),
            pltpu.VMEM((pairs + 3, height, PAIR), BF),
            pltpu.VMEM((slots + 4, 2 * PAIR), F32),
            pltpu.VMEM((2, 2, slots // 2 + 2, PAIR), F32),
            pltpu.VMEM((2, slots // 2 * height, 2 * PAIR), BF),
        ],
        compiler_params=WIDE_MEMORY,
        name="leaf",
    )(
        place,
        far_leaf.T,
        whole,
        odd,
        from_left,
        from_right,
        weight,
        down,
    )
    coeff_chip = coeff_sum + swap(coeff_sum, "orb", 1)
    coeff_other = swap(coeff_chip, "orb", 2)

    batch = 2
    per_pair = pl.BlockSpec((batch, points, PAIR), lambda i: (i, 0, 0))
    per_rank = pl.BlockSpec((rank, batch * PAIR), lambda i: (0, i))
    per_leaf = pl.BlockSpec((orbits, batch * PAIR, points), lambda i: (0, i, 0))
    gap = pl.pallas_call(
        gap_kernel,
        grid=(pairs // batch,),
        in_specs=[
            in_vmem,
            per_pair,
            in_vmem,
            pl.BlockSpec((height, batch * PAIR), lambda i: (0, i)),
            full(leaf_basis.shape),
        ],
        out_specs=in_vmem,
        out_shape=jax.ShapeDtypeStruct(orbitals.shape, F32),
        compiler_params=WIDE_MEMORY,
        name="gap",
    )(near, near_chip, near_other, coeffs, leaf_basis)
    return pl.pallas_call(
        final_kernel,
        grid=(pairs // batch,),
        in_specs=[in_vmem, in_vmem, per_rank, per_rank, full(leaf_basis.shape)],
        out_specs=per_leaf,
        out_shape=jax.ShapeDtypeStruct(orbitals.shape, F32),
        compiler_params=WIDE_MEMORY,
        name="final",
    )(orbitals, gap, coeff_chip, coeff_other, leaf_basis)


def solution(mesh):
    placed = (
        P("orb", "space", None),
        P("space", None),
        P("space", None),
        P("space", None),
        P("space", None),
        P(),
        P(),
        P(),
        P(),
        P(),
        P(),
    )

    return jax.shard_map(
        shards, mesh=mesh, in_specs=placed, out_specs=P("orb", "space", None), check_vma=False
    )
```
